512 devices in a mesh: obs: 32 (over x, y), det: 16 (over z, core).
Axes of the slice: x: 4, y: 8, z: 8, core: 2. Of those that a mesh axis runs over, the one named last changes fastest.
Arguments:
- sky: bfloat16 [1024, 3, 16, 128], P('obs'), may hold values from -6 to 6
- tile_list: int32 [32, 32], replicated, may hold values from 0 to 1023, as said below
- along: bfloat16 [32, 32, 128, 128], P('obs'), may hold values from -0.5 to 0.5
- detector_kernel: bfloat16 [1536, 48], P('det'), may hold values from -0.875 to 0.875
- sample_weight: bfloat16 [1536, 131072], P('det', 'obs'), may hold values from 0 to 2
- noise_inverse: bfloat16 [16, 1536, 1536], P('det', 'obs'), may hold values from -8 to 8, as said below
Outputs:
- normal_sky: float32 [1024, 3, 16, 128], P('obs')
The draws below stay inside these ranges and needn't reach their ends.
Inputs may be any that keep to these rules, and one draw needn't show every extreme that they name: `tile_list`: row p lists 32 different tiles; tile n is owned by index n // 32 of obs; a row holds at most 2 tiles of one owner, and every row holds exactly 2 tiles of some owner. `noise_inverse`: each band's matrix is symmetric.
All inputs are finite; a program needn't handle non-finite values.
Results may differ from the reference program's by a relative error of at most 0.0042.
Values may be sent and summed in bfloat16 or wider, within the bound.
A program may use at most 64 MiB of HBM per device.

```python
import math
import jax
import jax.numpy as jnp
from jax import lax

DETS = 1536
SLOW = 16
FAST = 256
ROWS = 16
COLS = 128
CAP = 2
TILE_DEV = 32
TILES_BLK = 32
SAMP_BLK = 4096
SEG = 128
NBLK = 32
SAMPLES = 131072
NTILES = 1024
BANDS = 16


coupling_strength = 4.0


def draw_tile_list(key, part):
    base_key = jax.random.fold_in(key, 11)
    key_hot, key_jitter, key_sizes, key_first, key_turn = jax.random.split(base_key, 5)
    owners = NBLK
    hot_order = jax.random.permutation(key_hot, owners)
    hot_rank = jnp.argsort(hot_order)
    spread = 4 * owners
    warm = max(owners // 8, 1)
    favour = jnp.where(hot_rank == 0, 3 * spread, jnp.where(hot_rank <= warm, spread, 0))
    jitter = jax.random.randint(key_jitter, (NBLK, owners), 0, spread)
    scores = (jitter + favour[None, :]) * owners + jnp.arange(owners)[None, :]
    ranking = jnp.argsort(-scores, axis=1)
    group_sizes = jax.random.randint(key_sizes, (NBLK, owners), 1, CAP + 1)
    forced = -(-TILES_BLK // CAP)
    position = jnp.arange(owners)[None, :]
    group_sizes = jnp.where(position == 0, CAP, group_sizes)
    group_sizes = jnp.where(position >= owners - forced, CAP, group_sizes)
    cumulative = jnp.cumsum(group_sizes, axis=1)
    slots = jnp.arange(TILES_BLK)
    group_of = jnp.sum((cumulative[:, None, :] <= slots[None, :, None]).astype(jnp.int32), axis=2)
    before = jnp.where(group_of > 0, jnp.take_along_axis(cumulative, jnp.maximum(group_of - 1, 0), axis=1), 0)
    rank_in = slots[None, :] - before
    owner_of = jnp.take_along_axis(ranking, group_of, axis=1)
    first_local = jax.random.randint(key_first, (NBLK, owners), 0, TILE_DEV)
    local_tile = (jnp.take_along_axis(first_local, owner_of, axis=1) + rank_in) % TILE_DEV
    scan_tiles = owner_of * TILE_DEV + local_tile
    rotation = jax.random.randint(key_turn, (NBLK, 1), 0, TILES_BLK)
    rotated = (slots[None, :] + rotation) % TILES_BLK
    return jnp.take_along_axis(scan_tiles, rotated, axis=1).astype(jnp.int32)


def draw_sample_weight(key, part):
    base_key = jax.random.fold_in(key, 37)
    level = jax.random.uniform(base_key, (DETS, SAMPLES), jnp.float32, 0.0, 1.0)
    share = 0.125
    high_log = math.log(0.7) + level / share * math.log(2.0 / 0.7)
    low_log = math.log(0.003) + (level - share) / (1.0 - share) * math.log(10.0)
    return jnp.exp(jnp.where(level < share, high_log, low_log)).astype(jnp.bfloat16)


def draw_noise_inverse(key, part):
    base_key = jax.random.fold_in(key, 23)
    key_entries, key_levels = jax.random.split(base_key)
    entries = jax.random.truncated_normal(key_entries, -4.0, 4.0, (BANDS, DETS, DETS), jnp.float32)
    levels = jnp.exp(jax.random.uniform(key_levels, (BANDS, DETS), jnp.float32, math.log(0.75), math.log(1.3)))
    identity = jnp.eye(DETS, dtype=jnp.float32)
    coupling = (entries + jnp.swapaxes(entries, 1, 2)) * (coupling_strength / math.sqrt(2.0 * DETS)) * (1.0 - identity)[None]
    pair_level = levels[:, :, None] * levels[:, None, :]
    return (pair_level * (identity[None] + coupling)).astype(jnp.bfloat16)


def block_scale(rng, extent, cuts, smallest, high):
    level, own = 1.0, jax.random.fold_in(rng, 6)
    for dim, parts in cuts:
        heights = jnp.exp(jax.random.uniform(jax.random.fold_in(own, dim), (parts,), jnp.float32, smallest / len(cuts), high / len(cuts)))
        level = level * jnp.repeat(heights, extent[dim] // parts).reshape([-1 if axis == dim else 1 for axis in range(len(extent))])
    return level


def centred(key, dims, scale, reach, pieces=(), held_as=jnp.bfloat16):
    drawn = jax.random.normal(key, dims, jnp.float32) * scale
    if len(pieces) > 0:
        drawn = block_scale(key, dims, pieces, -0.22, 0.18) * drawn
    return jnp.clip(drawn, min=-reach, max=reach).astype(held_as)


def setup_inputs(seed: int = 0) -> dict:
    key_of = jax.random.split(jax.random.key(seed), 7)
    sky = centred(key_of[0], (NTILES, 3, ROWS, COLS), 1.0, 6.0, ((0, 32),))
    tile_list = draw_tile_list(jax.random.fold_in(key_of[6], 71), 0)
    along = centred(key_of[2], (NBLK, TILES_BLK, COLS, SEG), SEG ** -0.5, 0.5, ((0, 32),))
    detector_kernel = centred(key_of[3], (DETS, 3 * ROWS), (3 * ROWS) ** -0.5, 0.875, ((0, 16),))
    sample_weight = draw_sample_weight(jax.random.fold_in(key_of[6], 71), 0)
    noise_inverse = draw_noise_inverse(jax.random.fold_in(key_of[6], 71), 0)
    return dict(sky=sky, tile_list=tile_list, along=along, detector_kernel=detector_kernel, sample_weight=sample_weight, noise_inverse=noise_inverse)


def dft_tables():
    slow_index = jnp.arange(SLOW, dtype=jnp.int32)
    fast_index = jnp.arange(FAST, dtype=jnp.int32)
    slow_angle = 2.0 * math.pi / SLOW * (slow_index[:, None] * slow_index[None, :] % SLOW).astype(jnp.float32)
    fast_angle = 2.0 * math.pi / FAST * (fast_index[:, None] * fast_index[None, :] % FAST).astype(jnp.float32)
    twist_angle = 2.0 * math.pi / (SLOW * FAST) * (slow_index[:, None] * fast_index[None, :] % (SLOW * FAST)).astype(jnp.float32)
    slow_scale = 1.0 / math.sqrt(SLOW)
    fast_scale = 1.0 / math.sqrt(FAST)
    return ((jnp.cos(slow_angle) * slow_scale).astype(jnp.bfloat16), (jnp.sin(slow_angle) * slow_scale).astype(jnp.bfloat16), (jnp.cos(fast_angle) * fast_scale).astype(jnp.bfloat16), (jnp.sin(fast_angle) * fast_scale).astype(jnp.bfloat16), jnp.cos(twist_angle), jnp.sin(twist_angle))

def widened(pattern, left_side, right_side):
    return jnp.einsum(pattern, left_side.astype(jnp.float32), right_side.astype(jnp.float32))

def forward_transform(signal, tables):
    slow_cos, slow_sin, fast_cos, fast_sin, twist_cos, twist_sin = tables
    first_real = widened('gv,nvu->ngu', slow_cos, signal)
    first_imag = -widened('gv,nvu->ngu', slow_sin, signal)
    half_real = (first_real * twist_cos + first_imag * twist_sin).astype(jnp.bfloat16)
    half_imag = (first_imag * twist_cos - first_real * twist_sin).astype(jnp.bfloat16)
    spec_real = widened('fu,ngu->ngf', fast_cos, half_real) + widened('fu,ngu->ngf', fast_sin, half_imag)
    spec_imag = widened('fu,ngu->ngf', fast_cos, half_imag) - widened('fu,ngu->ngf', fast_sin, half_real)
    return (spec_real.astype(jnp.bfloat16), spec_imag.astype(jnp.bfloat16))

def inverse_transform(mix_real, mix_imag, tables):
    slow_cos, slow_sin, fast_cos, fast_sin, twist_cos, twist_sin = tables
    back_real = widened('fu,ngf->ngu', fast_cos, mix_real) - widened('fu,ngf->ngu', fast_sin, mix_imag)
    back_imag = widened('fu,ngf->ngu', fast_cos, mix_imag) + widened('fu,ngf->ngu', fast_sin, mix_real)
    turn_real = (back_real * twist_cos - back_imag * twist_sin).astype(jnp.bfloat16)
    turn_imag = (back_imag * twist_cos + back_real * twist_sin).astype(jnp.bfloat16)
    return widened('gv,ngu->nvu', slow_cos, turn_real) - widened('gv,ngu->nvu', slow_sin, turn_imag)

def reference(sky, tile_list, along, detector_kernel, sample_weight, noise_inverse):
    tables = dft_tables()
    noise_wide = noise_inverse.astype(jnp.float32)
    kernel_wide = detector_kernel.astype(jnp.float32)
    band_cols = FAST // BANDS

    def one_block(block_index):
        block_list = tile_list[block_index]
        tiles_here = sky[block_list].reshape(TILES_BLK, 3 * ROWS, COLS)
        block_along = along[block_index]
        scan_rows = widened('kmc,kcu->mku', tiles_here, block_along).astype(jnp.bfloat16).reshape(3 * ROWS, SAMP_BLK)
        weights_here = lax.dynamic_slice_in_dim(sample_weight, (block_index * SAMP_BLK).astype(jnp.int32), SAMP_BLK, 1).astype(jnp.float32)
        timestream = (jnp.dot(detector_kernel, scan_rows, preferred_element_type=jnp.float32) * weights_here).astype(jnp.bfloat16)
        spec_real, spec_imag = forward_transform(timestream.reshape(DETS, SLOW, FAST), tables)
        stacked = jnp.stack([spec_real, spec_imag], 1).reshape(DETS, 2, SLOW, BANDS, band_cols).astype(jnp.float32)
        mixed = jnp.einsum('bde,ersbq->drsbq', noise_wide, stacked).astype(jnp.bfloat16).reshape(DETS, 2, SLOW, FAST)
        restored = inverse_transform(mixed[:, 0], mixed[:, 1], tables)
        filtered = (restored.reshape(DETS, SAMP_BLK) * weights_here).astype(jnp.bfloat16)
        projected = widened('dku,kcu->dkc', filtered.reshape(DETS, TILES_BLK, SEG), block_along).astype(jnp.bfloat16)
        return jnp.einsum('dkc,dm->kmc', projected.astype(jnp.float32), kernel_wide)
    all_terms = lax.map(one_block, jnp.arange(NBLK, dtype=jnp.int32))
    flat_tiles = tile_list.reshape(-1)
    summed = jnp.zeros((NTILES, 3 * ROWS, COLS), jnp.float32).at[flat_tiles].add(all_terms.reshape(-1, 3 * ROWS, COLS))
    return summed.reshape(NTILES, 3, ROWS, COLS)
```

```python
import functools
import math

import jax
import jax.numpy as jnp
import numpy as np
from jax import lax
from jax.experimental import pallas as pl
from jax.experimental.pallas import tpu as pltpu
from jax.sharding import PartitionSpec as P

CAP = 2
MP = 4
FAST = 256
LANES = 128
MESH = pl.DeviceIdType.MESH
F32 = jnp.float32
BF16 = jnp.bfloat16
VMEM = pl.BlockSpec(memory_space=pltpu.VMEM)


def tables(slow):
    lane = np.arange(FAST)
    half, rest = lane // LANES, lane % LANES
    j, i = rest // slow, rest % slow
    w = half * LANES + i * (LANES // slow) + j
    r = np.arange(FAST)
    angle = 2 * np.pi / FAST * (w[:, None] * r[None, :] % FAST)
    c, s = np.cos(angle) / math.sqrt(FAST), np.sin(angle) / math.sqrt(FAST)
    forward = np.concatenate([c, -s], 1)
    inverse = np.concatenate([c.T, -s.T], 0)
    twist = 2 * np.pi / (slow * FAST) * (np.arange(slow)[:, None] * r[None, :])
    tw = np.stack([np.cos(twist), np.sin(twist)], 1) / math.sqrt(slow)
    return (
        jnp.asarray(forward, BF16),
        jnp.asarray(inverse, BF16),
        jnp.asarray(tw.reshape(slow, 2, FAST), F32),
    )


def small_dft(re, im, sign):
    n = len(re)
    if n == 1:
        return re, im
    er, ei = small_dft(re[0::2], im[0::2], sign)
    odr, odi = small_dft(re[1::2], im[1::2], sign)
    outr, outi = [None] * n, [None] * n
    for k in range(n // 2):
        if k == 0:
            tr, ti = odr[0], odi[0]
        elif 4 * k == n:
            tr, ti = (-odi[k], odr[k]) if sign > 0 else (odi[k], -odr[k])
        else:
            c = math.cos(2 * math.pi * k / n)
            s = sign * math.sin(2 * math.pi * k / n)
            if 8 * k == n:
                tr, ti = (
                    c * (odr[k] - sign * odi[k]),
                    c * (odi[k] + sign * odr[k]),
                )
            else:
                tr, ti = c * odr[k] - s * odi[k], c * odi[k] + s * odr[k]
        outr[k], outi[k] = er[k] + tr, ei[k] + ti
        outr[k + n // 2], outi[k + n // 2] = er[k] - tr, ei[k] - ti
    return outr, outi


def digit_swap(tiles):
    n = len(tiles)
    tiles = list(tiles)
    lane = lax.broadcasted_iota(jnp.int32, tiles[0].shape, 1)
    step = 1
    while step < n:
        odd = (lane // step) % 2 == 1
        for i in range(n):
            if i & step:
                continue
            a, b = tiles[i], tiles[i | step]
            tiles[i] = jnp.where(odd, pltpu.roll(b, step, 1), a)
            tiles[i | step] = jnp.where(odd, b, pltpu.roll(a, LANES - step, 1))
        step *= 2
    return tiles


def greet(obs, det, with_obs, det_peers):
    barrier = pltpu.get_barrier_semaphore()
    count = 0
    if with_obs:
        me = lax.axis_index("obs")

        def signal(d, carry):
            pl.semaphore_signal(
                barrier, inc=1, device_id={"obs": lax.rem(me + d, obs)}, device_id_type=MESH
            )
            return carry

        lax.fori_loop(1, obs, signal, 0)
        count += obs - 1
    for peer in det_peers:
        pl.semaphore_signal(barrier, inc=1, device_id={"det": peer}, device_id_type=MESH)
    count += len(det_peers)
    pl.semaphore_wait(barrier, count)


def same_core(det):
    me = lax.axis_index("det")
    others = [lax.rem(me + 2 * d, det) for d in range(1, det // 2)]
    partner = me + 1 - 2 * lax.rem(me, 2)
    return others, partner


def obs_exchange(obs, src, dst, send_sem, recv_sem):
    me = lax.axis_index("obs")

    def copy(d):
        to = lax.rem(me + d, obs)
        return pltpu.make_async_remote_copy(
            src_ref=src.at[to],
            dst_ref=dst.at[me],
            send_sem=send_sem.at[d],
            recv_sem=recv_sem.at[d],
            device_id={"obs": to},
            device_id_type=MESH,
        )

    def start(d, carry):
        copy(d).start()
        return carry

    def wait(d, carry):
        copy(d).wait()
        return carry

    lax.fori_loop(1, obs, start, 0)
    dst[me] = src[me]
    lax.fori_loop(1, obs, wait, 0)


def det_gather(det, full, sems):
    send_sem, recv_sem, pass_send, pass_recv = sems
    me = lax.axis_index("det")
    others, partner = same_core(det)

    def copy(slot, to, a, b):
        return pltpu.make_async_remote_copy(
            src_ref=full.at[slot],
            dst_ref=full.at[slot],
            send_sem=a,
            recv_sem=b,
            device_id={"det": to},
            device_id_type=MESH,
        )

    n = det // 2
    order = sorted(range(1, n), key=lambda d: -min(d, n - d))
    outs = []
    for d in order:
        outs.append(copy(me, others[d - 1], send_sem.at[d], recv_sem.at[d]))
        outs[-1].start()
    outs.append(copy(me, partner, pass_send.at[0], pass_recv.at[0]))
    outs[-1].start()
    for d in reversed(order):
        source = lax.rem(me + det - 2 * d, det)
        copy(source, me, send_sem.at[d], recv_sem.at[d]).wait_recv()
        outs.append(copy(source, partner, pass_send.at[d], pass_recv.at[d]))
        outs[-1].start()
    for d in range(n):
        source = lax.rem(partner + det - 2 * d, det)
        copy(source, partner, pass_send.at[d], pass_recv.at[d]).wait_recv()
    for out in outs:
        out.wait_send()


def pair_products(rows, along, k, transposed):
    dims = (((1,), (1 if transposed else 0,)), ((), ()))
    first = lax.dot_general(rows, along[k], dims, preferred_element_type=F32)
    second = lax.dot_general(rows, along[k + 1], dims, preferred_element_type=F32)
    index = lax.broadcasted_iota(jnp.int32, first.shape, 0)
    return jnp.where(index < MP, first, second)


def split_dot(exact, x, dims):
    high = x.astype(BF16)
    low = (x - high.astype(F32)).astype(BF16)
    dot = functools.partial(lax.dot_general, dimension_numbers=dims, preferred_element_type=F32)
    return dot(exact, high) + dot(exact, low)


ROWS_COLS = (((1,), (0,)), ((), ()))
COLS_COLS = (((0,), (0,)), ((), ()))


def fetch_kernel(obs, det, out_ref, pick_ref, along_ref, scan_ref, recv, fetched, s0, s1, *sems):
    others, partner = same_core(det)
    greet(obs, det, True, others + [partner])
    obs_exchange(obs, out_ref, recv, s0, s1)
    flat = recv[...].reshape(obs * CAP * MP, LANES).astype(BF16)
    fetched[...] = jnp.dot(pick_ref[...], flat, preferred_element_type=F32).astype(BF16)
    me = lax.axis_index("det")
    tiles = along_ref.shape[0]
    for k in range(0, tiles, 4):
        rows = fetched[4 * k : 4 * k + 16]
        low = pair_products(rows[:8], along_ref, k, False)
        high = pair_products(rows[8:], along_ref, k + 2, False)
        scan_ref[me, 4 * k : 4 * k + 16] = jnp.concatenate([low, high], 0).astype(BF16)
    det_gather(det, scan_ref, sems)


def forward_kernel(slow, ke_ref, scan_ref, w_ref, fwd_ref, tw_ref, x_ref, ts, u, half):
    dets = w_ref.shape[0]
    tiles = w_ref.shape[1] // LANES
    for i in range(tiles // 4):
        rhs = scan_ref[:, 16 * i : 16 * i + 16, :].reshape(slow * 16, LANES)
        rows = jnp.dot(ke_ref[...], rhs, preferred_element_type=F32)
        for q in range(4):
            k = 4 * i + q
            ts[k] = rows[q * dets : (q + 1) * dets] * w_ref[:, k * LANES : (k + 1) * LANES].astype(F32)

    for h in range(2):

        def swap(g, carry):
            at = pl.ds(pl.multiple_of(g * 16, 16), 16)
            out = digit_swap([ts[h * slow + i, at, :] for i in range(slow)])
            for z in range(slow):
                u[z, at, h * LANES : (h + 1) * LANES] = out[z].astype(BF16)
            return carry

        lax.fori_loop(0, dets // 16, swap, 0)

    def fast(z, carry):
        a = jnp.dot(u[z], fwd_ref[...], preferred_element_type=F32)
        re, im = a[:, :FAST], a[:, FAST:]
        c, s = tw_ref[z, 0:1, :], tw_ref[z, 1:2, :]
        half[z, :, :FAST] = re * c + im * s
        half[z, :, FAST:] = im * c - re * s
        return carry

    lax.fori_loop(0, slow, fast, 0)

    for rc in range(2):
        lo, hi = rc * LANES, FAST + rc * LANES

        def last(g, carry):
            at = pl.ds(pl.multiple_of(g * 16, 16), 16)
            re = [half[z, at, lo : lo + LANES] for z in range(slow)]
            im = [half[z, at, hi : hi + LANES] for z in range(slow)]
            re, im = small_dft(re, im, -1)
            for b in range(slow):
                x_ref[b, at, lo : lo + LANES] = re[b].astype(BF16)
                x_ref[b, at, hi : hi + LANES] = im[b].astype(BF16)
            return carry

        lax.fori_loop(0, dets // 16, last, 0)


def inverse_kernel(slow, y_ref, w_ref, ke_ref, inv_ref, tw_ref, g_ref, turned, ts):
    dets = w_ref.shape[0]
    tiles = w_ref.shape[1] // LANES
    for rc in range(2):
        lo, hi = rc * LANES, FAST + rc * LANES

        def first(g, carry):
            at = pl.ds(pl.multiple_of(g * 16, 16), 16)
            re = [y_ref[b, at, lo : lo + LANES].astype(F32) for b in range(slow)]
            im = [y_ref[b, at, hi : hi + LANES].astype(F32) for b in range(slow)]
            re, im = small_dft(re, im, 1)
            for z in range(slow):
                c, s = tw_ref[z, 0:1, lo : lo + LANES], tw_ref[z, 1:2, lo : lo + LANES]
                turned[z, at, lo : lo + LANES] = (re[z] * c - im[z] * s).astype(BF16)
                turned[z, at, hi : hi + LANES] = (im[z] * c + re[z] * s).astype(BF16)
            return carry

        lax.fori_loop(0, dets // 16, first, 0)

    def fast(z, carry):
        o = jnp.dot(turned[z], inv_ref[...], preferred_element_type=F32)
        ts[z] = o[:, :LANES]
        ts[slow + z] = o[:, LANES:]
        return carry

    lax.fori_loop(0, slow, fast, 0)

    for h in range(2):

        def swap(g, carry):
            at = pl.ds(pl.multiple_of(g * 16, 16), 16)
            out = digit_swap([ts[h * slow + z, at, :] for z in range(slow)])
            for i in range(slow):
                ts[h * slow + i, at, :] = out[i]
            return carry

        lax.fori_loop(0, dets // 16, swap, 0)

    for i in range(tiles // 4):
        filtered = [
            (ts[k] * w_ref[:, k * LANES : (k + 1) * LANES].astype(F32)).astype(BF16)
            for k in range(4 * i, 4 * i + 4)
        ]
        rows = lax.dot_general(
            ke_ref[...], jnp.concatenate(filtered, 0), COLS_COLS, preferred_element_type=F32
        )
        g_ref[:, 16 * i : 16 * i + 16, :] = rows.reshape(slow, 16, LANES).astype(BF16)


def all_det(det):
    me = lax.axis_index("det")
    return [lax.rem(me + d, det) for d in range(1, det)]


def spread_kernel(det, x_ref, out_ref, send_sem, recv_sem):
    me = lax.axis_index("det")
    peers = all_det(det)
    greet(0, det, False, peers)
    copies = []
    for d in sorted(range(1, det), key=lambda d: -min(d, det - d)):
        copies.append(
            pltpu.make_async_remote_copy(
                src_ref=x_ref.at[peers[d - 1]],
                dst_ref=out_ref.at[me],
                send_sem=send_sem.at[d],
                recv_sem=recv_sem.at[d],
                device_id={"det": peers[d - 1]},
                device_id_type=MESH,
            )
        )
        copies[-1].start()
    out_ref[me] = x_ref[me]
    for copy in copies:
        copy.wait()


def mix_kernel(det, dets, n_ref, x_ref, out_ref, staged, send_sem, recv_sem):
    me = lax.axis_index("det")
    peers = all_det(det) + [me]
    greet(0, det, False, peers[:-1])
    copies = []
    for s in range(0, det, 4):
        rows = [
            n_ref[pl.ds(pl.multiple_of(to * dets, 16), dets), :] for to in peers[s : s + 4]
        ]
        got = jnp.dot(jnp.concatenate(rows, 0), x_ref[...], preferred_element_type=F32)
        got = got.astype(BF16)
        for i in range(4):
            d = s + i + 1
            block = got[i * dets : (i + 1) * dets]
            if d == det:
                out_ref[me] = block
                continue
            staged[d - 1] = block
            copies.append(
                pltpu.make_async_remote_copy(
                    src_ref=staged.at[d - 1],
                    dst_ref=out_ref.at[me],
                    send_sem=send_sem.at[d],
                    recv_sem=recv_sem.at[d],
                    device_id={"det": peers[d - 1]},
                    device_id_type=MESH,
                )
            )
            copies[-1].start()
    for copy in copies:
        copy.wait()


def give_kernel(
    obs, det, g_ref, along_ref, pick_ref, own_ref, sel_ref, sky_ref,
    parts, sums, terms, leave, recv, full, r0, r1, s0, s1, *sems,
):
    me = lax.axis_index("det")
    peers = all_det(det)
    greet(obs, det, True, peers)
    copies = []
    for d in sorted(range(1, det), key=lambda d: -min(d, det - d)):
        copies.append(
            pltpu.make_async_remote_copy(
                src_ref=g_ref.at[peers[d - 1]],
                dst_ref=parts.at[me],
                send_sem=r0.at[d],
                recv_sem=r1.at[d],
                device_id={"det": peers[d - 1]},
                device_id_type=MESH,
            )
        )
        copies[-1].start()
    parts[me] = g_ref[me]
    for copy in copies:
        copy.wait()
    total = parts[0].astype(F32)
    for j in range(1, det):
        total = total + parts[j].astype(F32)
    sums[...] = total
    tiles = along_ref.shape[0]
    for k in range(0, tiles, 2):
        rows = sums[4 * k : 4 * k + 8]
        high = rows.astype(BF16)
        low = (rows - high.astype(F32)).astype(BF16)
        terms[4 * k : 4 * k + 8] = pair_products(high, along_ref, k, True) + pair_products(
            low, along_ref, k, True
        )
    out = split_dot(pick_ref[...], terms[...], COLS_COLS)
    leave[...] = out.reshape(obs, CAP * MP, LANES)
    obs_exchange(obs, leave, recv, s0, s1)
    flat = recv[...].reshape(obs * CAP * MP, LANES)
    full[me] = split_dot(own_ref[...], flat, COLS_COLS).astype(BF16)
    det_gather(det, full, sems)
    held = sky_ref.shape[0]
    rows_all = sky_ref.shape[1]
    for i in range(held // 4):
        rhs = full[:, 16 * i : 16 * i + 16, :].reshape(det * 16, LANES)
        got = jnp.dot(sel_ref[...], rhs, preferred_element_type=F32)
        sky_ref[4 * i : 4 * i + 4] = got.reshape(4, rows_all, LANES)


def call(kernel, out, scratch, name, collective=None):
    if collective is None:
        params = pltpu.CompilerParams(vmem_limit_bytes=56 * 2**20)
    else:
        params = pltpu.CompilerParams(
            vmem_limit_bytes=56 * 2**20, collective_id=collective, has_side_effects=True
        )

    def run(*args):
        return pl.pallas_call(
            kernel,
            out_shape=out,
            in_specs=[VMEM] * len(args),
            out_specs=VMEM,
            scratch_shapes=scratch,
            compiler_params=params,
            name=name,
        )(*args)

    return run


def dma(n):
    return [pltpu.SemaphoreType.DMA((n,))] * 2


def local(sky, tile_list, along, detector_kernel, sample_weight, noise_inverse):
    obs, det = lax.axis_size("obs"), lax.axis_size("det")
    me_obs, me_det = lax.axis_index("obs"), lax.axis_index("det")
    held, tiles = sky.shape[0], tile_list.shape[1]
    dets, all_dets = detector_kernel.shape[0], noise_inverse.shape[2]
    rows_all = sky.shape[1] * sky.shape[2]
    mine = rows_all // det
    fwd, inv, tw = tables(det)

    noise = lax.all_gather(noise_inverse, "obs", axis=1, tiled=True)[0]

    owner = tile_list // held
    earlier = jnp.arange(tiles)[None, :] < jnp.arange(tiles)[:, None]
    rank = jnp.sum(
        ((owner[:, :, None] == owner[:, None, :]) & earlier[None]).astype(jnp.int32), axis=2
    )
    slot_hit = (
        (owner == me_obs)[:, None, :] & (rank[:, None, :] == jnp.arange(CAP)[None, :, None])
    )
    inside = tile_list - me_obs * held
    wanted = jnp.max(jnp.where(slot_hit, inside[:, None, :] + 1, 0), axis=2) - 1
    wanted = jnp.broadcast_to(wanted[:, :, None], (obs, CAP, MP))
    row = jnp.arange(MP)[None, None, :]
    wanted = jnp.where(wanted >= 0, wanted * MP + row, -1).reshape(obs * CAP * MP, 1)
    own = (wanted == jnp.arange(held * MP)[None, :]).astype(BF16)
    slot = lax.dynamic_index_in_dim(owner * CAP + rank, me_obs, 0, keepdims=False)
    slot = (slot[:, None] * MP + jnp.arange(MP)[None, :]).reshape(tiles * MP, 1)
    pick = (slot == jnp.arange(obs * CAP * MP)[None, :]).astype(BF16)

    my_rows = lax.dynamic_slice_in_dim(sky.reshape(held, rows_all, LANES), me_det * mine, mine, 1)
    my_rows = jnp.pad(my_rows, ((0, 0), (0, MP - mine), (0, 0))).reshape(held * MP, LANES)
    outgoing = jnp.dot(own, my_rows, preferred_element_type=F32).reshape(obs, CAP * MP, LANES)

    wide = jnp.pad(detector_kernel.reshape(dets, det, mine), ((0, 0), (0, 0), (0, MP - mine)))
    ke = jnp.eye(4, dtype=BF16)[:, None, None, :, None] * wide[None, :, :, None, :]
    ke = ke.reshape(4 * dets, det * 16)
    sel = np.zeros((4, det, mine, det, 4, MP), np.float32)
    for q in range(4):
        for j in range(det):
            for m in range(mine):
                sel[q, j, m, j, q, m] = 1
    sel = jnp.asarray(sel.reshape(4 * rows_all, det * 16), BF16)

    block = along[0]
    n = det // 2
    scan = call(
        functools.partial(fetch_kernel, obs, det),
        jax.ShapeDtypeStruct((det, tiles * MP, LANES), BF16),
        [
            pltpu.VMEM((obs, CAP * MP, LANES), F32),
            pltpu.VMEM((tiles * MP, LANES), BF16),
            *dma(obs),
            *dma(n),
            *dma(n),
        ],
        "fetch",
        0,
    )(outgoing, pick, block)
    spectra = call(
        functools.partial(forward_kernel, det),
        jax.ShapeDtypeStruct((det, dets, 2 * FAST), BF16),
        [
            pltpu.VMEM((tiles, dets, LANES), F32),
            pltpu.VMEM((det, dets, FAST), BF16),
            pltpu.VMEM((det, dets, 2 * FAST), F32),
        ],
        "forward",
    )(ke, scan, sample_weight, fwd, tw)
    banded = call(
        functools.partial(spread_kernel, det),
        jax.ShapeDtypeStruct((det, dets, 2 * FAST), BF16),
        dma(det),
        "spread",
        1,
    )(spectra)
    mixed = call(
        functools.partial(mix_kernel, det, dets),
        jax.ShapeDtypeStruct((det, dets, 2 * FAST), BF16),
        [pltpu.VMEM((det - 1, dets, 2 * FAST), BF16), *dma(det)],
        "mix",
        2,
    )(noise, banded.reshape(all_dets, 2 * FAST))
    given = call(
        functools.partial(inverse_kernel, det),
        jax.ShapeDtypeStruct((det, tiles * MP, LANES), BF16),
        [pltpu.VMEM((det, dets, 2 * FAST), BF16), pltpu.VMEM((tiles, dets, LANES), F32)],
        "inverse",
    )(mixed, sample_weight, ke, inv, tw)
    normal = call(
        functools.partial(give_kernel, obs, det),
        jax.ShapeDtypeStruct((held, rows_all, LANES), F32),
        [
            pltpu.VMEM((det, tiles * MP, LANES), BF16),
            pltpu.VMEM((tiles * MP, LANES), F32),
            pltpu.VMEM((tiles * MP, LANES), F32),
            pltpu.VMEM((obs, CAP * MP, LANES), F32),
            pltpu.VMEM((obs, CAP * MP, LANES), F32),
            pltpu.VMEM((det, held * MP, LANES), BF16),
            *dma(det),
            *dma(obs),
            *dma(n),
            *dma(n),
        ],
        "give",
        3,
    )(given, block, pick, own, sel)
    return normal.reshape(sky.shape)


def solution(mesh):
    in_specs = (
        P("obs", None, None, None),
        P(),
        P("obs", None, None, None),
        P("det", None),
        P("det", "obs"),
        P("det", "obs", None),
    )
    out_specs = P("obs", None, None, None)
    return jax.shard_map(local, mesh=mesh, in_specs=in_specs, out_specs=out_specs, check_vma=False)
```

```python
import functools
import math

import jax
import jax.numpy as jnp
import numpy as np
from jax import lax
from jax.experimental import pallas as pl
from jax.experimental.pallas import tpu as pltpu
from jax.sharding import PartitionSpec as P

CAP = 2
MP = 4
FAST = 256
LANES = 128
MESH = pl.DeviceIdType.MESH
F32 = jnp.float32
BF16 = jnp.bfloat16
VMEM = pl.BlockSpec(memory_space=pltpu.VMEM)


def band_of(slot, det):
    return slot if slot % 2 == 0 else det - slot


def tables(slow):
    lane = np.arange(FAST)
    half, rest = lane // LANES, lane % LANES
    j, i = rest // slow, rest % slow
    w = half * LANES + i * (LANES // slow) + j
    r = np.arange(LANES)
    angle = 2 * np.pi / FAST * (w[:, None] * r[None, :] % FAST)
    c, s = np.cos(angle) / math.sqrt(FAST), np.sin(angle) / math.sqrt(FAST)
    forward = np.concatenate([c, -s], 1)
    keep = (r > 0)[:, None]
    inverse = np.concatenate([c.T * keep, -s.T * keep], 0)
    twist = 2 * np.pi / (slow * FAST) * (np.arange(slow)[:, None] * r[None, :])
    tw = np.stack([np.cos(twist), np.sin(twist)], 1) / math.sqrt(slow)
    edge = np.zeros((slow, 8, slow, 8))
    for slot in range(slow):
        for v in range(2):
            turn = 2 * np.pi / slow * (band_of(slot, slow) + v / 2) * np.arange(slow)
            edge[slot, 2 * v, :, v] = np.cos(turn) / math.sqrt(slow)
            edge[slot, 2 * v + 1, :, v] = -np.sin(turn) / math.sqrt(slow)
    ends = np.zeros((8, FAST))
    ends[0] = 1 / math.sqrt(FAST)
    ends[1] = (1 - 2 * (w % 2)) / math.sqrt(FAST)
    return (
        jnp.asarray(forward, BF16),
        jnp.asarray(inverse, BF16),
        jnp.asarray(tw, F32),
        jnp.asarray(edge.reshape(8 * slow, 8 * slow), BF16),
        jnp.asarray(ends, BF16),
    )


def small_dft(re, im, sign):
    n = len(re)
    if n == 1:
        return re, im
    er, ei = small_dft(re[0::2], im[0::2], sign)
    odr, odi = small_dft(re[1::2], im[1::2], sign)
    outr, outi = [None] * n, [None] * n
    for k in range(n // 2):
        if k == 0:
            tr, ti = odr[0], odi[0]
        elif 4 * k == n:
            tr, ti = (-odi[k], odr[k]) if sign > 0 else (odi[k], -odr[k])
        else:
            c = math.cos(2 * math.pi * k / n)
            s = sign * math.sin(2 * math.pi * k / n)
            if 8 * k == n:
                tr, ti = (
                    c * (odr[k] - sign * odi[k]),
                    c * (odi[k] + sign * odr[k]),
                )
            else:
                tr, ti = c * odr[k] - s * odi[k], c * odi[k] + s * odr[k]
        outr[k], outi[k] = er[k] + tr, ei[k] + ti
        outr[k + n // 2], outi[k + n // 2] = er[k] - tr, ei[k] - ti
    return outr, outi


def digit_swap(tiles):
    n = len(tiles)
    tiles = list(tiles)
    lane = lax.broadcasted_iota(jnp.int32, tiles[0].shape, 1)
    step = 1
    while step < n:
        odd = (lane // step) % 2 == 1
        for i in range(n):
            if i & step:
                continue
            a, b = tiles[i], tiles[i | step]
            tiles[i] = jnp.where(odd, pltpu.roll(b, step, 1), a)
            tiles[i | step] = jnp.where(odd, b, pltpu.roll(a, LANES - step, 1))
        step *= 2
    return tiles


def greet(obs, det, with_obs, det_peers):
    barrier = pltpu.get_barrier_semaphore()
    count = 0
    if with_obs:
        me = lax.axis_index("obs")

        def signal(d, carry):
            pl.semaphore_signal(
                barrier, inc=1, device_id={"obs": lax.rem(me + d, obs)}, device_id_type=MESH
            )
            return carry

        lax.fori_loop(1, obs, signal, 0)
        count += obs - 1
    for peer in det_peers:
        pl.semaphore_signal(barrier, inc=1, device_id={"det": peer}, device_id_type=MESH)
    count += len(det_peers)
    pl.semaphore_wait(barrier, count)


def same_core(det):
    me = lax.axis_index("det")
    others = [lax.rem(me + 2 * d, det) for d in range(1, det // 2)]
    partner = me + 1 - 2 * lax.rem(me, 2)
    return others, partner


def obs_exchange(obs, src, dst, send_sem, recv_sem):
    me = lax.axis_index("obs")

    def copy(d):
        to = lax.rem(me + d, obs)
        return pltpu.make_async_remote_copy(
            src_ref=src.at[to],
            dst_ref=dst.at[me],
            send_sem=send_sem.at[d],
            recv_sem=recv_sem.at[d],
            device_id={"obs": to},
            device_id_type=MESH,
        )

    def start(d, carry):
        copy(d).start()
        return carry

    def wait(d, carry):
        copy(d).wait()
        return carry

    lax.fori_loop(1, obs, start, 0)
    dst[me] = src[me]
    lax.fori_loop(1, obs, wait, 0)


def det_gather(det, full, sems):
    send_sem, recv_sem, pass_send, pass_recv = sems
    me = lax.axis_index("det")
    others, partner = same_core(det)

    def copy(slot, to, a, b):
        return pltpu.make_async_remote_copy(
            src_ref=full.at[slot],
            dst_ref=full.at[slot],
            send_sem=a,
            recv_sem=b,
            device_id={"det": to},
            device_id_type=MESH,
        )

    n = det // 2
    order = sorted(range(1, n), key=lambda d: -min(d, n - d))
    outs = []
    for d in order:
        outs.append(copy(me, others[d - 1], send_sem.at[d], recv_sem.at[d]))
        outs[-1].start()
    outs.append(copy(me, partner, pass_send.at[0], pass_recv.at[0]))
    outs[-1].start()
    for d in reversed(order):
        source = lax.rem(me + det - 2 * d, det)
        copy(source, me, send_sem.at[d], recv_sem.at[d]).wait_recv()
        outs.append(copy(source, partner, pass_send.at[d], pass_recv.at[d]))
        outs[-1].start()
    for d in range(n):
        source = lax.rem(partner + det - 2 * d, det)
        copy(source, partner, pass_send.at[d], pass_recv.at[d]).wait_recv()
    for out in outs:
        out.wait_send()


def pair_products(rows, along, k, transposed):
    dims = (((1,), (1 if transposed else 0,)), ((), ()))
    first = lax.dot_general(rows, along[k], dims, preferred_element_type=F32)
    second = lax.dot_general(rows, along[k + 1], dims, preferred_element_type=F32)
    index = lax.broadcasted_iota(jnp.int32, first.shape, 0)
    return jnp.where(index < MP, first, second)


def split_dot(exact, x, dims):
    high = x.astype(BF16)
    low = (x - high.astype(F32)).astype(BF16)
    dot = functools.partial(lax.dot_general, dimension_numbers=dims, preferred_element_type=F32)
    return dot(exact, high) + dot(exact, low)


ROWS_COLS = (((1,), (0,)), ((), ()))
COLS_COLS = (((0,), (0,)), ((), ()))


def fetch_kernel(obs, det, out_ref, pick_ref, along_ref, scan_ref, recv, fetched, s0, s1, *sems):
    others, partner = same_core(det)
    greet(obs, det, True, others + [partner])
    obs_exchange(obs, out_ref, recv, s0, s1)
    flat = recv[...].reshape(obs * CAP * MP, LANES).astype(BF16)
    fetched[...] = jnp.dot(pick_ref[...], flat, preferred_element_type=F32).astype(BF16)
    me = lax.axis_index("det")
    tiles = along_ref.shape[0]
    for k in range(0, tiles, 4):
        rows = fetched[4 * k : 4 * k + 16]
        low = pair_products(rows[:8], along_ref, k, False)
        high = pair_products(rows[8:], along_ref, k + 2, False)
        scan_ref[me, 4 * k : 4 * k + 16] = jnp.concatenate([low, high], 0).astype(BF16)
    det_gather(det, scan_ref, sems)


def place(slot_band, b):
    slot = slot_band.index(b)
    return slot // 2, (slot % 2) * FAST


def forward_kernel(
    slow, ke_ref, scan_ref, w_ref, fwd_ref, tw_ref, edge_ref, ends_ref, x_ref, e_ref, ts, u, half, sums
):
    dets = w_ref.shape[0]
    tiles = w_ref.shape[1] // LANES
    bands = [band_of(slot, slow) for slot in range(slow)]
    for i in range(tiles // 4):
        rhs = scan_ref[:, 16 * i : 16 * i + 16, :].reshape(slow * 16, LANES)
        rows = jnp.dot(ke_ref[...], rhs, preferred_element_type=F32)
        for q in range(4):
            k = 4 * i + q
            ts[k] = rows[q * dets : (q + 1) * dets] * w_ref[:, k * LANES : (k + 1) * LANES].astype(F32)

    for h in range(2):

        def swap(g, carry):
            at = pl.ds(pl.multiple_of(g * 16, 16), 16)
            out = digit_swap([ts[h * slow + i, at, :] for i in range(slow)])
            for z in range(slow):
                u[z, at, h * LANES : (h + 1) * LANES] = out[z].astype(BF16)
            return carry

        lax.fori_loop(0, dets // 16, swap, 0)

    sums[...] = jnp.zeros_like(sums)

    def fast(z, carry):
        a = jnp.dot(u[z], fwd_ref[...], preferred_element_type=F32)
        re, im = a[:, :LANES], a[:, LANES:]
        c, s = tw_ref[z, 0:1, :], tw_ref[z, 1:2, :]
        half[z, :, :LANES] = re * c + im * s
        half[z, :, LANES:] = im * c - re * s
        sums[pl.ds(pl.multiple_of(z * 8, 8), 8), :dets] = lax.dot_general(
            ends_ref[...], u[z], (((1,), (1,)), ((), ())), preferred_element_type=F32
        )
        return carry

    lax.fori_loop(0, slow, fast, 0)
    e_ref[...] = split_dot(edge_ref[...], sums[...], ROWS_COLS)

    def last(g, carry):
        at = pl.ds(pl.multiple_of(g * 16, 16), 16)
        re = [half[z, at, :LANES] for z in range(slow)]
        im = [half[z, at, LANES:] for z in range(slow)]
        re, im = small_dft(re, im, -1)
        for b in range(slow):
            chip, lo = place(bands, b)
            x_ref[chip, at, lo : lo + LANES] = re[b].astype(BF16)
            x_ref[chip, at, lo + LANES : lo + FAST] = im[b].astype(BF16)
        return carry

    lax.fori_loop(0, dets // 16, last, 0)


def inverse_kernel(
    slow, y_ref, e_ref, w_ref, ke_ref, inv_ref, tw_ref, edge_ref, ends_ref, g_ref, turned, ts, sums
):
    dets = w_ref.shape[0]
    tiles = w_ref.shape[1] // LANES
    bands = [band_of(slot, slow) for slot in range(slow)]

    def first(g, carry):
        at = pl.ds(pl.multiple_of(g * 16, 16), 16)
        re, im = [], []
        for b in range(slow):
            chip, lo = place(bands, b)
            re.append(y_ref[chip, at, lo : lo + LANES].astype(F32))
            im.append(y_ref[chip, at, lo + LANES : lo + FAST].astype(F32))
        re, im = small_dft(re, im, 1)
        for z in range(slow):
            c, s = tw_ref[z, 0:1, :], tw_ref[z, 1:2, :]
            turned[z, at, :LANES] = (re[z] * c - im[z] * s).astype(BF16)
            turned[z, at, LANES:] = (im[z] * c + re[z] * s).astype(BF16)
        return carry

    lax.fori_loop(0, dets // 16, first, 0)
    part = dets // 2
    for q in range(2):
        rows = e_ref[:, q].reshape(8 * slow, LANES)
        sums[q] = split_dot(edge_ref[...], rows, COLS_COLS).astype(BF16).astype(F32)

    def fast(z, carry):
        o = jnp.dot(turned[z], inv_ref[...], preferred_element_type=F32)
        at = pl.ds(pl.multiple_of(z * 8, 8), 8)
        edge = [
            lax.dot_general(
                sums[q, at, :].astype(BF16), ends_ref[...], COLS_COLS, preferred_element_type=F32
            )[:part]
            for q in range(2)
        ]
        o = o + jnp.concatenate(edge, 0)
        ts[z] = o[:, :LANES]
        ts[slow + z] = o[:, LANES:]
        return carry

    lax.fori_loop(0, slow, fast, 0)

    for h in range(2):

        def swap(g, carry):
            at = pl.ds(pl.multiple_of(g * 16, 16), 16)
            out = digit_swap([ts[h * slow + z, at, :] for z in range(slow)])
            for i in range(slow):
                ts[h * slow + i, at, :] = out[i]
            return carry

        lax.fori_loop(0, dets // 16, swap, 0)

    for i in range(tiles // 4):
        filtered = [
            (ts[k] * w_ref[:, k * LANES : (k + 1) * LANES].astype(F32)).astype(BF16)
            for k in range(4 * i, 4 * i + 4)
        ]
        rows = lax.dot_general(
            ke_ref[...], jnp.concatenate(filtered, 0), COLS_COLS, preferred_element_type=F32
        )
        g_ref[:, 16 * i : 16 * i + 16, :] = rows.reshape(slow, 16, LANES).astype(BF16)


def all_det(det):
    me = lax.axis_index("det")
    return [lax.rem(me + d, det) for d in range(1, det)]


def det_send(src, dst, send_sem, recv_sem, to):
    return pltpu.make_async_remote_copy(
        src_ref=src,
        dst_ref=dst,
        send_sem=send_sem,
        recv_sem=recv_sem,
        device_id={"det": to},
        device_id_type=MESH,
    )


def far_first(n):
    return sorted(range(n), key=lambda d: -min(d, n - d))


def spread_kernel(
    obs, det, x_ref, e_ref, np_ref, out_ref, eout_ref,
    es, payload, gathered, wide, zs, zr, xs0, xs1, es0, es1, gs0, gs1, zs0, zs1, fs0, fs1,
):
    me = lax.axis_index("det")
    block = lax.axis_index("obs")
    n = det // 2
    chip = me // 2
    side = me // n
    peers = all_det(det)
    greet(obs, det, True, peers)

    edges = []
    for d in range(1, det):
        to = peers[d - 1]
        edges.append(
            det_send(
                e_ref.at[pl.ds(pl.multiple_of(to * 8, 8), 8)],
                es.at[pl.ds(pl.multiple_of(me * 8, 8), 8)],
                es0.at[d],
                es1.at[d],
                to,
            )
        )
        edges[-1].start()

    slot = lax.rem(me, n)

    def column(d):
        to_chip = lax.rem(chip + d, n)
        return det_send(x_ref.at[to_chip], out_ref.at[slot], xs0.at[d], xs1.at[slot], to_chip * 2 + side)

    for d in far_first(n)[:-1]:
        column(d).start()
    mine = lax.rem(me, 2) == side

    @pl.when(mine)
    def _():
        out_ref[slot] = x_ref[chip]

    @pl.when(jnp.logical_not(mine))
    def _():
        column(0).start()

    own = pl.ds(pl.multiple_of(me * 8, 8), 8)
    es[own, :] = e_ref[own, :]
    for copy in edges:
        copy.wait()
    for i in range(4):
        payload[16 * i : 16 * i + det] = es[pl.ds(i, det, stride=8), :].astype(BF16)

    def give(d):
        to = lax.rem(block + d, obs)
        return pltpu.make_async_remote_copy(
            src_ref=payload,
            dst_ref=gathered.at[block],
            send_sem=gs0.at[d],
            recv_sem=gs1.at[d],
            device_id={"obs": to},
            device_id_type=MESH,
        )

    def start(d, carry):
        give(d).start()
        return carry

    def wait(d, carry):
        give(d).wait()
        return carry

    lax.fori_loop(1, obs, start, 0)
    gathered[block] = payload[...]
    lax.fori_loop(1, obs, wait, 0)
    wide[...] = gathered[...].reshape(obs * 64, LANES).astype(F32)
    got = jnp.zeros((obs * 4, np_ref.shape[1]), F32)
    for j in range(det):
        rows = wide[pl.ds(j, obs * 4, stride=16), :].astype(BF16)
        got = got + lax.dot_general(rows, np_ref[j], (((1,), (1,)), ((), ())), preferred_element_type=F32)
    zs[...] = jnp.zeros_like(zs)
    for p in range(obs):
        zs[p, 0:4, : np_ref.shape[1]] = got[4 * p : 4 * p + 4]
    obs_exchange(obs, zs, zr, zs0, zs1)
    per = obs // det
    finals = []
    for d in range(1, det):
        to = peers[d - 1]
        finals.append(
            det_send(zr.at[pl.ds(to * per, per)], eout_ref.at[me], fs0.at[d], fs1.at[d], to)
        )
        finals[-1].start()
    eout_ref[me] = zr[pl.ds(me * per, per)]

    for d in far_first(n)[:-1]:
        column(d).wait_send()

    @pl.when(jnp.logical_not(mine))
    def _():
        column(0).wait_send()

    home = lax.rem(me, 2) * n
    for i in range(n):

        @pl.when(home + i != me)
        def _():
            det_send(out_ref.at[i], out_ref.at[i], xs0.at[0], xs1.at[i], me).wait_recv()

    for copy in finals:
        copy.wait()


def mix_kernel(det, dets, m_ref, x_ref, out_ref, given, taken, staged, ps0, ps1, ys0, ys1):
    me = lax.axis_index("det")
    n = det // 2
    chip = me // 2
    core = lax.rem(me, 2)
    partner = me + 1 - 2 * core
    half = n // 2
    greet(0, det, False, all_det(det))
    swaps, sends = [], []

    def product(to_chip):
        rows = m_ref[pl.ds(pl.multiple_of(to_chip * 2 * dets, 16), 2 * dets), :]
        return jnp.dot(rows, x_ref[...], preferred_element_type=F32)

    def finish(s, total):
        to_chip = core * half + lax.rem(chip + s, half)
        swaps[s].wait_recv()
        total = total + taken[s].astype(F32)
        for i in range(2):
            to = to_chip * 2 + i
            staged[s, i] = total[i * dets : (i + 1) * dets].astype(BF16)
            copy = det_send(staged.at[s, i], out_ref.at[chip], ys0.at[s, i], ys1.at[chip], to)

            @pl.when(to != me)
            def _():
                copy.start()

            @pl.when(to == me)
            def _():
                out_ref[chip] = staged[s, i]

            sends.append((to, copy))

    before = None
    for s in range(half):
        near = lax.rem(chip + s, half)
        given[s] = product((1 - core) * half + near).astype(BF16)
        swaps.append(det_send(given.at[s], taken.at[s], ps0.at[s], ps1.at[s], partner))
        swaps[-1].start()
        total = product(core * half + near)
        if before is not None:
            finish(s - 1, before)
        before = total
    finish(half - 1, before)
    side = me // n
    for c in range(n):

        @pl.when(c * 2 + side != me)
        def _():
            det_send(out_ref.at[c], out_ref.at[c], ys0.at[0, 0], ys1.at[c], me).wait_recv()

    for copy in swaps:
        copy.wait_send()
    for to, copy in sends:

        @pl.when(to != me)
        def _():
            copy.wait_send()


def give_kernel(
    obs, det, g_ref, along_ref, pick_ref, own_ref, sel_ref, sky_ref,
    parts, sums, terms, leave, recv, full, r0, r1, s0, s1, *sems,
):
    me = lax.axis_index("det")
    peers = all_det(det)
    greet(obs, det, True, peers)
    copies = []
    for d in sorted(range(1, det), key=lambda d: -min(d, det - d)):
        copies.append(
            pltpu.make_async_remote_copy(
                src_ref=g_ref.at[peers[d - 1]],
                dst_ref=parts.at[me],
                send_sem=r0.at[d],
                recv_sem=r1.at[d],
                device_id={"det": peers[d - 1]},
                device_id_type=MESH,
            )
        )
        copies[-1].start()
    parts[me] = g_ref[me]
    for copy in copies:
        copy.wait()
    total = parts[0].astype(F32)
    for j in range(1, det):
        total = total + parts[j].astype(F32)
    sums[...] = total
    tiles = along_ref.shape[0]
    for k in range(0, tiles, 2):
        rows = sums[4 * k : 4 * k + 8]
        high = rows.astype(BF16)
        low = (rows - high.astype(F32)).astype(BF16)
        terms[4 * k : 4 * k + 8] = pair_products(high, along_ref, k, True) + pair_products(
            low, along_ref, k, True
        )
    out = split_dot(pick_ref[...], terms[...], COLS_COLS)
    leave[...] = out.reshape(obs, CAP * MP, LANES)
    obs_exchange(obs, leave, recv, s0, s1)
    flat = recv[...].reshape(obs * CAP * MP, LANES)
    full[me] = split_dot(own_ref[...], flat, COLS_COLS).astype(BF16)
    det_gather(det, full, sems)
    held = sky_ref.shape[0]
    rows_all = sky_ref.shape[1]
    for i in range(held // 4):
        rhs = full[:, 16 * i : 16 * i + 16, :].reshape(det * 16, LANES)
        got = jnp.dot(sel_ref[...], rhs, preferred_element_type=F32)
        sky_ref[4 * i : 4 * i + 4] = got.reshape(4, rows_all, LANES)


def call(kernel, out, scratch, name, collective=None):
    if collective is None:
        params = pltpu.CompilerParams(vmem_limit_bytes=56 * 2**20)
    else:
        params = pltpu.CompilerParams(
            vmem_limit_bytes=56 * 2**20, collective_id=collective, has_side_effects=True
        )

    def run(*args):
        return pl.pallas_call(
            kernel,
            out_shape=out,
            in_specs=[VMEM] * len(args),
            out_specs=VMEM if not isinstance(out, tuple) else (VMEM,) * len(out),
            scratch_shapes=scratch,
            compiler_params=params,
            name=name,
        )(*args)

    return run


def dma(n):
    return [pltpu.SemaphoreType.DMA((n,))] * 2


def local(sky, tile_list, along, detector_kernel, sample_weight, noise_inverse):
    obs, det = lax.axis_size("obs"), lax.axis_size("det")
    me_obs, me_det = lax.axis_index("obs"), lax.axis_index("det")
    held, tiles = sky.shape[0], tile_list.shape[1]
    dets, all_dets = detector_kernel.shape[0], noise_inverse.shape[2]
    rows_all = sky.shape[1] * sky.shape[2]
    mine = rows_all // det
    fwd, inv, tw, edge, ends = tables(det)

    rows = noise_inverse[0]
    part = all_dets // 2
    core = me_det % 2
    odd = core == 1
    swapped = lax.ppermute(rows, "det", [(j, det - j) for j in range(1, det, 2)])
    offered = jnp.where(odd, rows[:, :part], rows[:, part:])
    ways = [(j, det - 1 - j if j % 2 else j + 1) for j in range(det)]
    other = lax.ppermute(offered, "det", ways)
    rows = jnp.where(odd, swapped, rows)
    both = jnp.where(odd, rows[:, part:], rows[:, :part]).astype(F32) + other.astype(F32)
    folded = lax.all_gather(both.astype(BF16), "obs", axis=0, tiled=True)
    spread_rows = jnp.pad(
        rows.reshape(-1, det, dets), ((0, 0), (0, 0), (0, LANES - dets))
    ).transpose(1, 0, 2)

    owner = tile_list // held
    earlier = jnp.arange(tiles)[None, :] < jnp.arange(tiles)[:, None]
    rank = jnp.sum(
        ((owner[:, :, None] == owner[:, None, :]) & earlier[None]).astype(jnp.int32), axis=2
    )
    slot_hit = (
        (owner == me_obs)[:, None, :] & (rank[:, None, :] == jnp.arange(CAP)[None, :, None])
    )
    inside = tile_list - me_obs * held
    wanted = jnp.max(jnp.where(slot_hit, inside[:, None, :] + 1, 0), axis=2) - 1
    wanted = jnp.broadcast_to(wanted[:, :, None], (obs, CAP, MP))
    row = jnp.arange(MP)[None, None, :]
    wanted = jnp.where(wanted >= 0, wanted * MP + row, -1).reshape(obs * CAP * MP, 1)
    own = (wanted == jnp.arange(held * MP)[None, :]).astype(BF16)
    slot = lax.dynamic_index_in_dim(owner * CAP + rank, me_obs, 0, keepdims=False)
    slot = (slot[:, None] * MP + jnp.arange(MP)[None, :]).reshape(tiles * MP, 1)
    pick = (slot == jnp.arange(obs * CAP * MP)[None, :]).astype(BF16)

    my_rows = lax.dynamic_slice_in_dim(sky.reshape(held, rows_all, LANES), me_det * mine, mine, 1)
    my_rows = jnp.pad(my_rows, ((0, 0), (0, MP - mine), (0, 0))).reshape(held * MP, LANES)
    outgoing = jnp.dot(own, my_rows, preferred_element_type=F32).reshape(obs, CAP * MP, LANES)

    wide = jnp.pad(detector_kernel.reshape(dets, det, mine), ((0, 0), (0, 0), (0, MP - mine)))
    ke = jnp.eye(4, dtype=BF16)[:, None, None, :, None] * wide[None, :, :, None, :]
    ke = ke.reshape(4 * dets, det * 16)
    sel = np.zeros((4, det, mine, det, 4, MP), np.float32)
    for q in range(4):
        for j in range(det):
            for m in range(mine):
                sel[q, j, m, j, q, m] = 1
    sel = jnp.asarray(sel.reshape(4 * rows_all, det * 16), BF16)

    block = along[0]
    n = det // 2
    scan = call(
        functools.partial(fetch_kernel, obs, det),
        jax.ShapeDtypeStruct((det, tiles * MP, LANES), BF16),
        [
            pltpu.VMEM((obs, CAP * MP, LANES), F32),
            pltpu.VMEM((tiles * MP, LANES), BF16),
            *dma(obs),
            *dma(n),
            *dma(n),
        ],
        "fetch",
        0,
    )(outgoing, pick, block)
    spectra, edges = call(
        functools.partial(forward_kernel, det),
        (
            jax.ShapeDtypeStruct((n, dets, 2 * FAST), BF16),
            jax.ShapeDtypeStruct((8 * det, LANES), F32),
        ),
        [
            pltpu.VMEM((tiles, dets, LANES), F32),
            pltpu.VMEM((det, dets, FAST), BF16),
            pltpu.VMEM((det, dets, FAST), F32),
            pltpu.VMEM((8 * det, LANES), F32),
        ],
        "forward",
    )(ke, scan, sample_weight, fwd, tw, edge, ends)
    per = obs // det
    banded, edges = call(
        functools.partial(spread_kernel, obs, det),
        (
            jax.ShapeDtypeStruct((n, dets, 2 * FAST), BF16),
            jax.ShapeDtypeStruct((det, per, 8, LANES), F32),
        ),
        [
            pltpu.VMEM((8 * det, LANES), F32),
            pltpu.VMEM((64, LANES), BF16),
            pltpu.VMEM((obs, 64, LANES), BF16),
            pltpu.VMEM((obs * 64, LANES), F32),
            pltpu.VMEM((obs, 8, LANES), F32),
            pltpu.VMEM((obs, 8, LANES), F32),
            *dma(n),
            *dma(det),
            *dma(obs),
            *dma(obs),
            *dma(det),
        ],
        "spread",
        1,
    )(spectra, edges, spread_rows)
    half = n // 2
    mixed = call(
        functools.partial(mix_kernel, det, dets),
        jax.ShapeDtypeStruct((n, dets, 2 * FAST), BF16),
        [
            pltpu.VMEM((half, 2 * dets, 2 * FAST), BF16),
            pltpu.VMEM((half, 2 * dets, 2 * FAST), BF16),
            pltpu.VMEM((half, 2, dets, 2 * FAST), BF16),
            *dma(half),
            pltpu.SemaphoreType.DMA((half, 2)),
            pltpu.SemaphoreType.DMA((n,)),
        ],
        "mix",
        2,
    )(folded, banded.reshape(n * dets, 2 * FAST))
    given = call(
        functools.partial(inverse_kernel, det),
        jax.ShapeDtypeStruct((det, tiles * MP, LANES), BF16),
        [
            pltpu.VMEM((det, dets, FAST), BF16),
            pltpu.VMEM((tiles, dets, LANES), F32),
            pltpu.VMEM((2, 8 * det, LANES), F32),
        ],
        "inverse",
    )(mixed, edges, sample_weight, ke, inv, tw, edge, ends)
    normal = call(
        functools.partial(give_kernel, obs, det),
        jax.ShapeDtypeStruct((held, rows_all, LANES), F32),
        [
            pltpu.VMEM((det, tiles * MP, LANES), BF16),
            pltpu.VMEM((tiles * MP, LANES), F32),
            pltpu.VMEM((tiles * MP, LANES), F32),
            pltpu.VMEM((obs, CAP * MP, LANES), F32),
            pltpu.VMEM((obs, CAP * MP, LANES), F32),
            pltpu.VMEM((det, held * MP, LANES), BF16),
            *dma(det),
            *dma(obs),
            *dma(n),
            *dma(n),
        ],
        "give",
        3,
    )(given, block, pick, own, sel)
    return normal.reshape(sky.shape)


def solution(mesh):
    in_specs = (
        P("obs", None, None, None),
        P(),
        P("obs", None, None, None),
        P("det", None),
        P("det", "obs"),
        P("det", "obs", None),
    )
    out_specs = P("obs", None, None, None)
    return jax.shard_map(local, mesh=mesh, in_specs=in_specs, out_specs=out_specs, check_vma=False)
```

```python
import functools
import math

import jax
import jax.numpy as jnp
import numpy as np
from jax import lax
from jax.experimental import pallas as pl
from jax.experimental.pallas import tpu as pltpu
from jax.sharding import PartitionSpec as P

CAP = 2
MP = 4
FAST = 256
LANES = 128
MESH = pl.DeviceIdType.MESH
F32 = jnp.float32
BF16 = jnp.bfloat16
VMEM = pl.BlockSpec(memory_space=pltpu.VMEM)


def band_of(slot, det):
    return slot if slot % 2 == 0 else det - slot


def tables(slow):
    lane = np.arange(FAST)
    half, rest = lane // LANES, lane % LANES
    j, i = rest // slow, rest % slow
    w = half * LANES + i * (LANES // slow) + j
    r = np.arange(LANES)
    angle = 2 * np.pi / FAST * (w[:, None] * r[None, :] % FAST)
    c, s = np.cos(angle) / math.sqrt(FAST), np.sin(angle) / math.sqrt(FAST)
    forward = np.concatenate([c, -s], 1)
    keep = (r > 0)[:, None]
    inverse = np.concatenate([c.T * keep, -s.T * keep], 0)
    twist = 2 * np.pi / (slow * FAST) * (np.arange(slow)[:, None] * r[None, :])
    tw = np.stack([np.cos(twist), np.sin(twist)], 1) / math.sqrt(slow)
    edge = np.zeros((slow, 8, slow, 8))
    for slot in range(slow):
        for v in range(2):
            turn = 2 * np.pi / slow * (band_of(slot, slow) + v / 2) * np.arange(slow)
            edge[slot, 2 * v, :, v] = np.cos(turn) / math.sqrt(slow)
            edge[slot, 2 * v + 1, :, v] = -np.sin(turn) / math.sqrt(slow)
    ends = np.zeros((8, FAST))
    ends[0] = 1 / math.sqrt(FAST)
    ends[1] = (1 - 2 * (w % 2)) / math.sqrt(FAST)
    return (
        jnp.asarray(forward, BF16),
        jnp.asarray(inverse, BF16),
        jnp.asarray(tw, F32),
        jnp.asarray(edge.reshape(8 * slow, 8 * slow), BF16),
        jnp.asarray(ends, BF16),
    )


def small_dft(re, im, sign):
    n = len(re)
    if n == 1:
        return re, im
    er, ei = small_dft(re[0::2], im[0::2], sign)
    odr, odi = small_dft(re[1::2], im[1::2], sign)
    outr, outi = [None] * n, [None] * n
    for k in range(n // 2):
        if k == 0:
            tr, ti = odr[0], odi[0]
        elif 4 * k == n:
            tr, ti = (-odi[k], odr[k]) if sign > 0 else (odi[k], -odr[k])
        else:
            c = math.cos(2 * math.pi * k / n)
            s = sign * math.sin(2 * math.pi * k / n)
            if 8 * k == n:
                tr, ti = (
                    c * (odr[k] - sign * odi[k]),
                    c * (odi[k] + sign * odr[k]),
                )
            else:
                tr, ti = c * odr[k] - s * odi[k], c * odi[k] + s * odr[k]
        outr[k], outi[k] = er[k] + tr, ei[k] + ti
        outr[k + n // 2], outi[k + n // 2] = er[k] - tr, ei[k] - ti
    return outr, outi


def digit_swap(tiles):
    n = len(tiles)
    tiles = list(tiles)
    lane = lax.broadcasted_iota(jnp.int32, tiles[0].shape, 1)
    step = 1
    while step < n:
        odd = (lane // step) % 2 == 1
        for i in range(n):
            if i & step:
                continue
            a, b = tiles[i], tiles[i | step]
            tiles[i] = jnp.where(odd, pltpu.roll(b, step, 1), a)
            tiles[i | step] = jnp.where(odd, b, pltpu.roll(a, LANES - step, 1))
        step *= 2
    return tiles


def greet(obs, det, with_obs, det_peers):
    barrier = pltpu.get_barrier_semaphore()
    count = 0
    if with_obs:
        me = lax.axis_index("obs")

        def signal(d, carry):
            pl.semaphore_signal(
                barrier, inc=1, device_id={"obs": lax.rem(me + d, obs)}, device_id_type=MESH
            )
            return carry

        lax.fori_loop(1, obs, signal, 0)
        count += obs - 1
    for peer in det_peers:
        pl.semaphore_signal(barrier, inc=1, device_id={"det": peer}, device_id_type=MESH)
    count += len(det_peers)
    pl.semaphore_wait(barrier, count)


def same_core(det):
    me = lax.axis_index("det")
    others = [lax.rem(me + 2 * d, det) for d in range(1, det // 2)]
    partner = me + 1 - 2 * lax.rem(me, 2)
    return others, partner


def obs_copies(obs, src, dst, send_sem, recv_sem, same=False):
    me = lax.axis_index("obs")

    def copy(d):
        to = lax.rem(me + d, obs)
        return pltpu.make_async_remote_copy(
            src_ref=src if same else src.at[to],
            dst_ref=dst.at[me],
            send_sem=send_sem.at[d],
            recv_sem=recv_sem.at[d],
            device_id={"obs": to},
            device_id_type=MESH,
        )

    def start():
        def step(d, carry):
            copy(d).start()
            return carry

        lax.fori_loop(1, obs, step, 0)
        dst[me] = src[...] if same else src[me]

    def wait():
        def step(d, carry):
            copy(d).wait()
            return carry

        lax.fori_loop(1, obs, step, 0)

    return start, wait


def det_send(src, dst, send_sem, recv_sem, to):
    return pltpu.make_async_remote_copy(
        src_ref=src,
        dst_ref=dst,
        send_sem=send_sem,
        recv_sem=recv_sem,
        device_id={"det": to},
        device_id_type=MESH,
    )


def far_first(n):
    return sorted(range(n), key=lambda d: -min(d, n - d))


def det_gather(det, full, sems, sent=lambda: None):
    send_sem, recv_sem, pass_send, pass_recv = sems
    me = lax.axis_index("det")
    others, partner = same_core(det)

    def copy(slot, to, a, b):
        return pltpu.make_async_remote_copy(
            src_ref=full.at[slot],
            dst_ref=full.at[slot],
            send_sem=a,
            recv_sem=b,
            device_id={"det": to},
            device_id_type=MESH,
        )

    n = det // 2
    order = sorted(range(1, n), key=lambda d: -min(d, n - d))
    outs = []
    for d in order:
        outs.append(copy(me, others[d - 1], send_sem.at[d], recv_sem.at[d]))
        outs[-1].start()
    outs.append(copy(me, partner, pass_send.at[0], pass_recv.at[0]))
    outs[-1].start()
    sent()
    for d in reversed(order):
        source = lax.rem(me + det - 2 * d, det)
        copy(source, me, send_sem.at[d], recv_sem.at[d]).wait_recv()
        outs.append(copy(source, partner, pass_send.at[d], pass_recv.at[d]))
        outs[-1].start()
    for d in range(n):
        source = lax.rem(partner + det - 2 * d, det)
        copy(source, partner, pass_send.at[d], pass_recv.at[d]).wait_recv()
    for out in outs:
        out.wait_send()


def pair_products(rows, along, k, transposed):
    dims = (((1,), (1 if transposed else 0,)), ((), ()))
    first = lax.dot_general(rows, along[k], dims, preferred_element_type=F32)
    second = lax.dot_general(rows, along[k + 1], dims, preferred_element_type=F32)
    index = lax.broadcasted_iota(jnp.int32, first.shape, 0)
    return jnp.where(index < MP, first, second)


def split_dot(exact, x, dims):
    high = x.astype(BF16)
    low = (x - high.astype(F32)).astype(BF16)
    dot = functools.partial(lax.dot_general, dimension_numbers=dims, preferred_element_type=F32)
    return dot(exact, high) + dot(exact, low)


ROWS_COLS = (((1,), (0,)), ((), ()))
COLS_COLS = (((0,), (0,)), ((), ()))


def place(slot_band, b):
    slot = slot_band.index(b)
    return slot // 2, (slot % 2) * FAST


def front_kernel(
    obs, det, grid, out_ref, pick_ref, along_ref, noise_ref, ke_ref, w_ref, fwd_ref, tw_ref, edge_ref, ends_ref,
    x_out, z_out, m_out,
    recv, fetched, scan, rows, other, ts, u, half, sums, e, es, payload, gathered, wide, zs, x,
    k0, k1, n0, n1, m0, m1, r0, r1, xs0, xs1, es0, es1, gs0, gs1, zs0, zs1, *sems,
):
    me, block = lax.axis_index("det"), lax.axis_index("obs")
    across, down = grid
    bx, by = block // down, lax.rem(block, down)
    n = det // 2
    chip, core, side = me // 2, lax.rem(me, 2), me // n
    dets, tiles = w_ref.shape[0], along_ref.shape[0]
    bands = [band_of(slot, det) for slot in range(det)]
    peers = all_det(det)
    greet(obs, det, True, peers)

    sky_start, sky_wait = obs_copies(obs, out_ref, recv, k0, k1)
    sky_start()
    part = noise_ref.shape[1] // 2
    whole = det_send(noise_ref, rows, n0.at[0], n1.at[0], lax.rem(2 * det - me, det))
    left = det_send(noise_ref.at[:, :part], other, n0.at[1], n1.at[1], det - 1 - me)
    right = det_send(noise_ref.at[:, part:], other, n0.at[1], n1.at[1], lax.rem(me + 1, det))

    @pl.when(core == 1)
    def _():
        whole.start()
        left.start()
        left.wait_send()
        whole.wait()

    @pl.when(core == 0)
    def _():
        right.start()
        rows[...] = noise_ref[...]
        right.wait_send()

    left.wait_recv()
    both = jnp.where(core == 1, rows[:, part:].astype(F32), rows[:, :part].astype(F32))
    m_out[bx, by] = (both + other[...].astype(F32)).astype(BF16)

    def sideways(d):
        to = lax.rem(bx + d, across)
        return pltpu.make_async_remote_copy(
            src_ref=m_out.at[bx, by],
            dst_ref=m_out.at[bx, by],
            send_sem=m0.at[d],
            recv_sem=m1.at[d],
            device_id={"obs": to * down + by},
            device_id_type=MESH,
        )

    def ring(way, step):
        origin = lax.rem(by + down - way * (step - 1), down)
        cut = slice(None)
        if 2 * step == down:
            cut = slice(0, across // 2) if way > 0 else slice(across // 2, across)
        at = 0 if way > 0 else 1
        return pltpu.make_async_remote_copy(
            src_ref=m_out.at[cut, origin],
            dst_ref=m_out.at[cut, origin],
            send_sem=r0.at[at, step - 1],
            recv_sem=r1.at[at, step - 1],
            device_id={"obs": bx * down + lax.rem(by + down + way, down)},
            device_id_type=MESH,
        )

    def turn(step):
        for way in (1, -1):
            if step == 1:
                if way == 1:
                    for d in range(1, across):
                        sideways(d).wait_recv()
            else:
                ring(way, step - 1).wait_recv()
            if 2 * step <= down:
                ring(way, step).start()

    steps = iter(range(1, down // 2 + 2))

    def advance():
        step = next(steps, None)
        if step is not None:
            turn(step)

    for d in range(1, across):
        sideways(d).start()

    sky_wait()
    flat = recv[...].reshape(obs * CAP * MP, LANES).astype(BF16)
    fetched[...] = jnp.dot(pick_ref[...], flat, preferred_element_type=F32).astype(BF16)
    for k in range(0, tiles, 4):
        part_rows = fetched[4 * k : 4 * k + 16]
        low = pair_products(part_rows[:8], along_ref, k, False)
        high = pair_products(part_rows[8:], along_ref, k + 2, False)
        scan[me, 4 * k : 4 * k + 16] = jnp.concatenate([low, high], 0).astype(BF16)
    det_gather(det, scan, sems, advance)

    for i in range(tiles // 4):
        rhs = scan[:, 16 * i : 16 * i + 16, :].reshape(det * 16, LANES)
        got = jnp.dot(ke_ref[...], rhs, preferred_element_type=F32)
        for q in range(4):
            k = 4 * i + q
            ts[k] = got[q * dets : (q + 1) * dets] * w_ref[:, k * LANES : (k + 1) * LANES].astype(F32)

    for h in range(2):

        def swap(g, carry):
            at = pl.ds(pl.multiple_of(g * 16, 16), 16)
            out = digit_swap([ts[h * det + i, at, :] for i in range(det)])
            for z in range(det):
                u[z, at, h * LANES : (h + 1) * LANES] = out[z].astype(BF16)
            return carry

        lax.fori_loop(0, dets // 16, swap, 0)

    sums[...] = jnp.zeros_like(sums)

    def ends(z, carry):
        sums[pl.ds(pl.multiple_of(z * 8, 8), 8), :dets] = lax.dot_general(
            ends_ref[...], u[z], (((1,), (1,)), ((), ())), preferred_element_type=F32
        )
        return carry

    lax.fori_loop(0, det, ends, 0)
    e[...] = split_dot(edge_ref[...], sums[...], ROWS_COLS)
    own = pl.ds(pl.multiple_of(me * 8, 8), 8)
    edges = []
    for d in range(1, det):
        to = peers[d - 1]
        edges.append(
            det_send(e.at[pl.ds(pl.multiple_of(to * 8, 8), 8)], es.at[own], es0.at[d], es1.at[d], to)
        )
        edges[-1].start()
    es[own, :] = e[own, :]
    advance()

    def fast(z, carry):
        a = jnp.dot(u[z], fwd_ref[...], preferred_element_type=F32)
        re, im = a[:, :LANES], a[:, LANES:]
        c, s = tw_ref[z, 0:1, :], tw_ref[z, 1:2, :]
        half[z, :, :LANES] = re * c + im * s
        half[z, :, LANES:] = im * c - re * s
        return carry

    lax.fori_loop(0, det, fast, 0)

    for copy in edges:
        copy.wait()
    for i in range(4):
        payload[16 * i : 16 * i + det] = es[pl.ds(i, det, stride=8), :].astype(BF16)
    give_start, give_wait = obs_copies(obs, payload, gathered, gs0, gs1, True)
    give_start()

    def last(g, carry):
        at = pl.ds(pl.multiple_of(g * 16, 16), 16)
        re = [half[z, at, :LANES] for z in range(det)]
        im = [half[z, at, LANES:] for z in range(det)]
        re, im = small_dft(re, im, -1)
        for b in range(det):
            to, lo = place(bands, b)
            x[to, at, lo : lo + LANES] = re[b].astype(BF16)
            x[to, at, lo + LANES : lo + FAST] = im[b].astype(BF16)
        return carry

    lax.fori_loop(0, dets // 16, last, 0)

    slot = lax.rem(me, n)

    def column(d):
        to = lax.rem(chip + d, n)
        return det_send(x.at[to], x_out.at[slot], xs0.at[d], xs1.at[slot], to * 2 + side)

    for d in far_first(n)[:-1]:
        column(d).start()
    mine = core == side

    @pl.when(mine)
    def _():
        x_out[slot] = x[chip]

    @pl.when(jnp.logical_not(mine))
    def _():
        column(0).start()

    advance()

    give_wait()
    wide[...] = gathered[...].reshape(obs * 64, LANES).astype(F32)
    width = noise_ref.shape[0]
    prod = jnp.zeros((obs * 4, width), F32)
    for j in range(det):
        lhs = wide[pl.ds(j, obs * 4, stride=16), :dets].astype(BF16)
        rhs = rows[:, j * dets : (j + 1) * dets]
        prod = prod + lax.dot_general(lhs, rhs, (((1,), (1,)), ((), ())), preferred_element_type=F32)
    zs[...] = jnp.zeros_like(zs)
    for p in range(obs):
        zs[p, 0:4, :width] = prod[4 * p : 4 * p + 4]
    z_start, z_wait = obs_copies(obs, zs, z_out, zs0, zs1)
    z_start()
    advance()
    advance()
    z_wait()

    for d in far_first(n)[:-1]:
        column(d).wait_send()

    @pl.when(jnp.logical_not(mine))
    def _():
        column(0).wait_send()

    for i in range(n):

        @pl.when(core * n + i != me)
        def _():
            det_send(x_out.at[i], x_out.at[i], xs0.at[0], xs1.at[i], me).wait_recv()

    for step in steps:
        turn(step)
    for d in range(1, across):
        sideways(d).wait_send()
    for step in range(1, down // 2 + 1):
        for way in (1, -1):
            ring(way, step).wait_send()


def all_det(det):
    me = lax.axis_index("det")
    return [lax.rem(me + d, det) for d in range(1, det)]


def det_send(src, dst, send_sem, recv_sem, to):
    return pltpu.make_async_remote_copy(
        src_ref=src,
        dst_ref=dst,
        send_sem=send_sem,
        recv_sem=recv_sem,
        device_id={"det": to},
        device_id_type=MESH,
    )


def far_first(n):
    return sorted(range(n), key=lambda d: -min(d, n - d))


def back_kernel(
    obs, det, m_ref, x_ref, z_ref, w_ref, ke_ref, inv_ref, tw_ref, edge_ref, ends_ref,
    along_ref, pick_ref, own_ref, sel_ref, sky_ref,
    given, taken, staged, y_ref, e_ref, turned, ts, sums, g_ref, pre, pairs, parts, total_ref, terms, leave, recv, full,
    ps0, ps1, ys0, ys1, fs0, fs1, g0, g1, q0, q1, s0, s1, *sems,
):
    me = lax.axis_index("det")
    n = det // 2
    chip, core = me // 2, lax.rem(me, 2)
    partner = me + 1 - 2 * core
    dets, tiles = w_ref.shape[0], along_ref.shape[0]
    bands = [band_of(slot, det) for slot in range(det)]
    slow = det
    peers = all_det(det)
    greet(obs, det, True, peers)
    per = obs // det
    finals = []
    for d in range(1, det):
        to = peers[d - 1]
        finals.append(det_send(z_ref.at[pl.ds(to * per, per)], e_ref.at[me], fs0.at[d], fs1.at[d], to))
        finals[-1].start()
    e_ref[me] = z_ref[pl.ds(me * per, per)]

    half = n // 2
    swaps, sends = [], []

    def product(to_chip):
        rows = m_ref[pl.ds(pl.multiple_of(to_chip * 2 * dets, 16), 2 * dets), :]
        return jnp.dot(rows, x_ref[...], preferred_element_type=F32)

    def finish(s, total):
        to_chip = core * half + lax.rem(chip + s, half)
        swaps[s].wait_recv()
        total = total + taken[s].astype(F32)
        for i in range(2):
            to = to_chip * 2 + i
            staged[s, i] = total[i * dets : (i + 1) * dets].astype(BF16)
            copy = det_send(staged.at[s, i], y_ref.at[chip], ys0.at[s, i], ys1.at[chip], to)

            @pl.when(to != me)
            def _():
                copy.start()

            @pl.when(to == me)
            def _():
                y_ref[chip] = staged[s, i]

            sends.append((to, copy))

    before = None
    for s in range(half):
        near = lax.rem(chip + s, half)
        given[s] = product((1 - core) * half + near).astype(BF16)
        swaps.append(det_send(given.at[s], taken.at[s], ps0.at[s], ps1.at[s], partner))
        swaps[-1].start()
        total = product(core * half + near)
        if before is not None:
            finish(s - 1, before)
        before = total
    finish(half - 1, before)
    side = me // n
    for c in range(n):

        @pl.when(c * 2 + side != me)
        def _():
            det_send(y_ref.at[c], y_ref.at[c], ys0.at[0, 0], ys1.at[c], me).wait_recv()

    for copy in swaps:
        copy.wait_send()
    for to, copy in sends:

        @pl.when(to != me)
        def _():
            copy.wait_send()
    for copy in finals:
        copy.wait()

    def first(g, carry):
        at = pl.ds(pl.multiple_of(g * 16, 16), 16)
        re, im = [], []
        for b in range(slow):
            chip, lo = place(bands, b)
            re.append(y_ref[chip, at, lo : lo + LANES].astype(F32))
            im.append(y_ref[chip, at, lo + LANES : lo + FAST].astype(F32))
        re, im = small_dft(re, im, 1)
        for z in range(slow):
            c, s = tw_ref[z, 0:1, :], tw_ref[z, 1:2, :]
            turned[z, at, :LANES] = (re[z] * c - im[z] * s).astype(BF16)
            turned[z, at, LANES:] = (im[z] * c + re[z] * s).astype(BF16)
        return carry

    lax.fori_loop(0, dets // 16, first, 0)
    part = dets // 2
    for q in range(2):
        rows = e_ref[:, q].reshape(8 * slow, LANES)
        sums[q] = split_dot(edge_ref[...], rows, COLS_COLS).astype(BF16).astype(F32)

    def fast(z, carry):
        o = jnp.dot(turned[z], inv_ref[...], preferred_element_type=F32)
        at = pl.ds(pl.multiple_of(z * 8, 8), 8)
        edge = [
            lax.dot_general(
                sums[q, at, :].astype(BF16), ends_ref[...], COLS_COLS, preferred_element_type=F32
            )[:part]
            for q in range(2)
        ]
        o = o + jnp.concatenate(edge, 0)
        ts[z] = o[:, :LANES]
        ts[slow + z] = o[:, LANES:]
        return carry

    lax.fori_loop(0, slow, fast, 0)

    for h in range(2):

        def swap(g, carry):
            at = pl.ds(pl.multiple_of(g * 16, 16), 16)
            out = digit_swap([ts[h * slow + z, at, :] for z in range(slow)])
            for i in range(slow):
                ts[h * slow + i, at, :] = out[i]
            return carry

        lax.fori_loop(0, dets // 16, swap, 0)

    for i in range(tiles // 4):
        filtered = [
            (ts[k] * w_ref[:, k * LANES : (k + 1) * LANES].astype(F32)).astype(BF16)
            for k in range(4 * i, 4 * i + 4)
        ]
        rows = lax.dot_general(
            ke_ref[...], jnp.concatenate(filtered, 0), COLS_COLS, preferred_element_type=F32
        )
        g_ref[:, :, 16 * i : 16 * i + 16, :] = rows.reshape(n, 2, 16, LANES).astype(BF16)

    swap_pairs = det_send(g_ref.at[:, 1 - core], pre, g0.at[0], g1.at[0], partner)
    swap_pairs.start()
    swap_pairs.wait()
    for c in range(n):
        pairs[c] = (g_ref[c, core].astype(F32) + pre[c].astype(F32)).astype(BF16)
    copies = []
    for d in far_first(n)[:-1]:
        to = lax.rem(chip + d, n)
        copies.append(det_send(pairs.at[to], parts.at[chip], q0.at[d], q1.at[d], to * 2 + core))
        copies[-1].start()
    parts[chip] = pairs[chip]
    for copy in copies:
        copy.wait()
    total = parts[0].astype(F32)
    for c in range(1, n):
        total = total + parts[c].astype(F32)
    total_ref[...] = total
    for k in range(0, tiles, 2):
        rows = total_ref[4 * k : 4 * k + 8]
        high = rows.astype(BF16)
        low = (rows - high.astype(F32)).astype(BF16)
        terms[4 * k : 4 * k + 8] = pair_products(high, along_ref, k, True) + pair_products(
            low, along_ref, k, True
        )
    leave[...] = split_dot(pick_ref[...], terms[...], COLS_COLS).reshape(obs, CAP * MP, LANES)
    start, wait = obs_copies(obs, leave, recv, s0, s1)
    start()
    wait()
    flat = recv[...].reshape(obs * CAP * MP, LANES)
    full[me] = split_dot(own_ref[...], flat, COLS_COLS).astype(BF16)
    det_gather(det, full, sems)
    held, rows_all = sky_ref.shape[0], sky_ref.shape[1]
    for i in range(held // 4):
        rhs = full[:, 16 * i : 16 * i + 16, :].reshape(det * 16, LANES)
        got = jnp.dot(sel_ref[...], rhs, preferred_element_type=F32)
        sky_ref[4 * i : 4 * i + 4] = got.reshape(4, rows_all, LANES)


def call(kernel, out, scratch, name, collective=None):
    if collective is None:
        params = pltpu.CompilerParams(vmem_limit_bytes=56 * 2**20)
    else:
        params = pltpu.CompilerParams(
            vmem_limit_bytes=56 * 2**20, collective_id=collective, has_side_effects=True
        )

    def run(*args):
        return pl.pallas_call(
            kernel,
            out_shape=out,
            in_specs=[VMEM] * len(args),
            out_specs=VMEM if not isinstance(out, tuple) else (VMEM,) * len(out),
            scratch_shapes=scratch,
            compiler_params=params,
            name=name,
        )(*args)

    return run


def dma(n):
    return [pltpu.SemaphoreType.DMA((n,))] * 2


def local(sky, tile_list, along, detector_kernel, sample_weight, noise_inverse):
    obs, det = lax.axis_size("obs"), lax.axis_size("det")
    me_obs, me_det = lax.axis_index("obs"), lax.axis_index("det")
    held, tiles = sky.shape[0], tile_list.shape[1]
    dets, all_dets = detector_kernel.shape[0], noise_inverse.shape[2]
    rows_all = sky.shape[1] * sky.shape[2]
    mine = rows_all // det
    fwd, inv, tw, edge, ends = tables(det)

    owner = tile_list // held
    earlier = jnp.arange(tiles)[None, :] < jnp.arange(tiles)[:, None]
    rank = jnp.sum(
        ((owner[:, :, None] == owner[:, None, :]) & earlier[None]).astype(jnp.int32), axis=2
    )
    slot_hit = (
        (owner == me_obs)[:, None, :] & (rank[:, None, :] == jnp.arange(CAP)[None, :, None])
    )
    inside = tile_list - me_obs * held
    wanted = jnp.max(jnp.where(slot_hit, inside[:, None, :] + 1, 0), axis=2) - 1
    wanted = jnp.broadcast_to(wanted[:, :, None], (obs, CAP, MP))
    row = jnp.arange(MP)[None, None, :]
    wanted = jnp.where(wanted >= 0, wanted * MP + row, -1).reshape(obs * CAP * MP, 1)
    own = (wanted == jnp.arange(held * MP)[None, :]).astype(BF16)
    slot = lax.dynamic_index_in_dim(owner * CAP + rank, me_obs, 0, keepdims=False)
    slot = (slot[:, None] * MP + jnp.arange(MP)[None, :]).reshape(tiles * MP, 1)
    pick = (slot == jnp.arange(obs * CAP * MP)[None, :]).astype(BF16)

    my_rows = lax.dynamic_slice_in_dim(sky.reshape(held, rows_all, LANES), me_det * mine, mine, 1)
    my_rows = jnp.pad(my_rows, ((0, 0), (0, MP - mine), (0, 0))).reshape(held * MP, LANES)
    outgoing = jnp.dot(own, my_rows, preferred_element_type=F32).reshape(obs, CAP * MP, LANES)

    wide = jnp.pad(detector_kernel.reshape(dets, det, mine), ((0, 0), (0, 0), (0, MP - mine)))
    ke = jnp.eye(4, dtype=BF16)[:, None, None, :, None] * wide[None, :, :, None, :]
    ke = ke.reshape(4 * dets, det * 16)
    sel = np.zeros((4, det, mine, det, 4, MP), np.float32)
    for q in range(4):
        for j in range(det):
            for m in range(mine):
                sel[q, j, m, j, q, m] = 1
    sel = jnp.asarray(sel.reshape(4 * rows_all, det * 16), BF16)

    block = along[0]
    n, half, per = det // 2, det // 4, obs // det
    down = 8 if obs == 32 else obs // 2
    grid = (obs // down, down)
    mine, part = noise_inverse.shape[1], all_dets // 2
    member = jax.ShapeDtypeStruct((n, dets, 2 * FAST), BF16)
    slots = jax.ShapeDtypeStruct((obs, CAP * MP, LANES), F32)
    slot_buffer = pltpu.VMEM(slots.shape, F32)
    row_buffer = pltpu.VMEM((tiles * MP, LANES), F32)
    banded, back, folded = call(
        functools.partial(front_kernel, obs, det, grid),
        (member, slots, jax.ShapeDtypeStruct((*grid, mine, part), BF16)),
        [
            slot_buffer,
            pltpu.VMEM((tiles * MP, LANES), BF16),
            pltpu.VMEM((det, tiles * MP, LANES), BF16),
            pltpu.VMEM((mine, all_dets), BF16),
            pltpu.VMEM((mine, part), BF16),
            pltpu.VMEM((tiles, dets, LANES), F32),
            pltpu.VMEM((det, dets, FAST), BF16),
            pltpu.VMEM((det, dets, FAST), F32),
            pltpu.VMEM((8 * det, LANES), F32),
            pltpu.VMEM((8 * det, LANES), F32),
            pltpu.VMEM((8 * det, LANES), F32),
            pltpu.VMEM((64, LANES), BF16),
            pltpu.VMEM((obs, 64, LANES), BF16),
            pltpu.VMEM((obs * 64, LANES), F32),
            slot_buffer,
            pltpu.VMEM(member.shape, BF16),
            *dma(obs),
            *dma(2),
            *dma(grid[0]),
            *[pltpu.SemaphoreType.DMA((2, down // 2))] * 2,
            *dma(n),
            *dma(det),
            *dma(obs),
            *dma(obs),
            *dma(n),
            *dma(n),
        ],
        "front",
        0,
    )(outgoing, pick, block, noise_inverse[0], ke, sample_weight, fwd, tw, edge, ends)
    normal = call(
        functools.partial(back_kernel, obs, det),
        jax.ShapeDtypeStruct((held, rows_all, LANES), F32),
        [
            pltpu.VMEM((half, 2 * dets, 2 * FAST), BF16),
            pltpu.VMEM((half, 2 * dets, 2 * FAST), BF16),
            pltpu.VMEM((half, 2, dets, 2 * FAST), BF16),
            pltpu.VMEM(member.shape, BF16),
            pltpu.VMEM((det, per, CAP * MP, LANES), F32),
            pltpu.VMEM((det, dets, FAST), BF16),
            pltpu.VMEM((tiles, dets, LANES), F32),
            pltpu.VMEM((2, 8 * det, LANES), F32),
            pltpu.VMEM((n, 2, tiles * MP, LANES), BF16),
            pltpu.VMEM((n, tiles * MP, LANES), BF16),
            pltpu.VMEM((n, tiles * MP, LANES), BF16),
            pltpu.VMEM((n, tiles * MP, LANES), BF16),
            row_buffer,
            row_buffer,
            slot_buffer,
            slot_buffer,
            pltpu.VMEM((det, held * MP, LANES), BF16),
            *dma(half),
            pltpu.SemaphoreType.DMA((half, 2)),
            pltpu.SemaphoreType.DMA((n,)),
            *dma(det),
            *dma(1),
            *dma(n),
            *dma(obs),
            *dma(n),
            *dma(n),
        ],
        "back",
        1,
    )(
        folded.reshape(all_dets, part), banded.reshape(n * dets, 2 * FAST), back,
        sample_weight, ke, inv, tw, edge, ends, block, pick, own, sel,
    )
    return normal.reshape(sky.shape)


def solution(mesh):
    in_specs = (
        P("obs", None, None, None),
        P(),
        P("obs", None, None, None),
        P("det", None),
        P("det", "obs"),
        P("det", "obs", None),
    )
    out_specs = P("obs", None, None, None)
    return jax.shard_map(local, mesh=mesh, in_specs=in_specs, out_specs=out_specs, check_vma=False)
```

```python
import functools
import math

import jax
import jax.numpy as jnp
import numpy as np
from jax import lax
from jax.experimental import pallas as pl
from jax.experimental.pallas import tpu as pltpu
from jax.sharding import PartitionSpec as P

CAP = 2
MP = 4
FAST = 256
LANES = 128
MESH = pl.DeviceIdType.MESH
F32 = jnp.float32
BF16 = jnp.bfloat16
VMEM = pl.BlockSpec(memory_space=pltpu.VMEM)


def band_of(slot, det):
    return slot if slot % 2 == 0 else det - slot


def tables(slow):
    lane = np.arange(FAST)
    half, rest = lane // LANES, lane % LANES
    j, i = rest // slow, rest % slow
    w = half * LANES + i * (LANES // slow) + j
    r = np.arange(LANES)
    angle = 2 * np.pi / FAST * (w[:, None] * r[None, :] % FAST)
    c, s = np.cos(angle) / math.sqrt(FAST), np.sin(angle) / math.sqrt(FAST)
    forward = np.concatenate([c, -s], 1)
    keep = (r > 0)[:, None]
    inverse = np.concatenate([c.T * keep, -s.T * keep], 0)
    twist = 2 * np.pi / (slow * FAST) * (np.arange(slow)[:, None] * r[None, :])
    tw = np.stack([np.cos(twist), np.sin(twist)], 1) / math.sqrt(slow)
    edge = np.zeros((slow, 8, slow, 8))
    for slot in range(slow):
        for v in range(2):
            turn = 2 * np.pi / slow * (band_of(slot, slow) + v / 2) * np.arange(slow)
            edge[slot, 2 * v, :, v] = np.cos(turn) / math.sqrt(slow)
            edge[slot, 2 * v + 1, :, v] = -np.sin(turn) / math.sqrt(slow)
    ends = np.zeros((8, FAST))
    ends[0] = 1 / math.sqrt(FAST)
    ends[1] = (1 - 2 * (w % 2)) / math.sqrt(FAST)
    return (
        jnp.asarray(forward, BF16),
        jnp.asarray(inverse, BF16),
        jnp.asarray(tw, F32),
        jnp.asarray(edge.reshape(8 * slow, 8 * slow), BF16),
        jnp.asarray(ends, BF16),
    )


def small_dft(re, im, sign):
    n = len(re)
    if n == 1:
        return re, im
    er, ei = small_dft(re[0::2], im[0::2], sign)
    odr, odi = small_dft(re[1::2], im[1::2], sign)
    outr, outi = [None] * n, [None] * n
    for k in range(n // 2):
        if k == 0:
            tr, ti = odr[0], odi[0]
        elif 4 * k == n:
            tr, ti = (-odi[k], odr[k]) if sign > 0 else (odi[k], -odr[k])
        else:
            c = math.cos(2 * math.pi * k / n)
            s = sign * math.sin(2 * math.pi * k / n)
            if 8 * k == n:
                tr, ti = (
                    c * (odr[k] - sign * odi[k]),
                    c * (odi[k] + sign * odr[k]),
                )
            else:
                tr, ti = c * odr[k] - s * odi[k], c * odi[k] + s * odr[k]
        outr[k], outi[k] = er[k] + tr, ei[k] + ti
        outr[k + n // 2], outi[k + n // 2] = er[k] - tr, ei[k] - ti
    return outr, outi


def digit_swap(tiles):
    n = len(tiles)
    tiles = list(tiles)
    lane = lax.broadcasted_iota(jnp.int32, tiles[0].shape, 1)
    step = 1
    while step < n:
        odd = (lane // step) % 2 == 1
        for i in range(n):
            if i & step:
                continue
            a, b = tiles[i], tiles[i | step]
            tiles[i] = jnp.where(odd, pltpu.roll(b, step, 1), a)
            tiles[i | step] = jnp.where(odd, b, pltpu.roll(a, LANES - step, 1))
        step *= 2
    return tiles


def greet(obs, det, with_obs, det_peers, meanwhile=None):
    barrier = pltpu.get_barrier_semaphore()
    count = 0
    if with_obs:
        me = lax.axis_index("obs")

        def signal(d, carry):
            pl.semaphore_signal(
                barrier, inc=1, device_id={"obs": lax.rem(me + d, obs)}, device_id_type=MESH
            )
            return carry

        lax.fori_loop(1, obs, signal, 0)
        count += obs - 1
    for peer in det_peers:
        pl.semaphore_signal(barrier, inc=1, device_id={"det": peer}, device_id_type=MESH)
    count += len(det_peers)
    if meanwhile is not None:
        meanwhile()
    pl.semaphore_wait(barrier, count)


def same_core(det):
    me = lax.axis_index("det")
    others = [lax.rem(me + 2 * d, det) for d in range(1, det // 2)]
    partner = me + 1 - 2 * lax.rem(me, 2)
    return others, partner


def obs_copies(obs, src, dst, send_sem, recv_sem, same=False):
    me = lax.axis_index("obs")

    def copy(d):
        to = lax.rem(me + d, obs)
        return pltpu.make_async_remote_copy(
            src_ref=src if same else src.at[to],
            dst_ref=dst.at[me],
            send_sem=send_sem.at[d],
            recv_sem=recv_sem.at[d],
            device_id={"obs": to},
            device_id_type=MESH,
        )

    def start():
        def step(d, carry):
            copy(d).start()
            return carry

        lax.fori_loop(1, obs, step, 0)
        dst[me] = src[...] if same else src[me]

    def wait():
        def step(d, carry):
            copy(d).wait()
            return carry

        lax.fori_loop(1, obs, step, 0)

    return start, wait


def det_send(src, dst, send_sem, recv_sem, to):
    return pltpu.make_async_remote_copy(
        src_ref=src,
        dst_ref=dst,
        send_sem=send_sem,
        recv_sem=recv_sem,
        device_id={"det": to},
        device_id_type=MESH,
    )


def far_first(n):
    return sorted(range(n), key=lambda d: -min(d, n - d))


def det_gather(det, full, sems, sent=lambda: None):
    send_sem, recv_sem, pass_send, pass_recv = sems
    me = lax.axis_index("det")
    others, partner = same_core(det)

    def copy(slot, to, a, b):
        return pltpu.make_async_remote_copy(
            src_ref=full.at[slot],
            dst_ref=full.at[slot],
            send_sem=a,
            recv_sem=b,
            device_id={"det": to},
            device_id_type=MESH,
        )

    n = det // 2
    order = sorted(range(1, n), key=lambda d: -min(d, n - d))
    outs = []
    for d in order:
        outs.append(copy(me, others[d - 1], send_sem.at[d], recv_sem.at[d]))
        outs[-1].start()
    outs.append(copy(me, partner, pass_send.at[0], pass_recv.at[0]))
    outs[-1].start()
    sent()
    for d in reversed(order):
        source = lax.rem(me + det - 2 * d, det)
        copy(source, me, send_sem.at[d], recv_sem.at[d]).wait_recv()
        outs.append(copy(source, partner, pass_send.at[d], pass_recv.at[d]))
        outs[-1].start()
    for d in range(n):
        source = lax.rem(partner + det - 2 * d, det)
        copy(source, partner, pass_send.at[d], pass_recv.at[d]).wait_recv()
    for out in outs:
        out.wait_send()


def pair_products(rows, along, k, transposed):
    dims = (((1,), (1 if transposed else 0,)), ((), ()))
    first = lax.dot_general(rows, along[k], dims, preferred_element_type=F32)
    second = lax.dot_general(rows, along[k + 1], dims, preferred_element_type=F32)
    index = lax.broadcasted_iota(jnp.int32, first.shape, 0)
    return jnp.where(index < MP, first, second)


def split_dot(exact, x, dims):
    high = x.astype(BF16)
    low = (x - high.astype(F32)).astype(BF16)
    dot = functools.partial(lax.dot_general, dimension_numbers=dims, preferred_element_type=F32)
    return dot(exact, high) + dot(exact, low)


ROWS_COLS = (((1,), (0,)), ((), ()))
COLS_COLS = (((0,), (0,)), ((), ()))


def place(slot_band, b):
    slot = slot_band.index(b)
    return slot // 2, (slot % 2) * FAST


def all_det(det):
    me = lax.axis_index("det")
    return [lax.rem(me + d, det) for d in range(1, det)]


def iota(shape, dim):
    return lax.broadcasted_iota(jnp.int32, shape, dim)


def selections(obs, list_ref, own, pick, mine_sel, mine, rows_all, held):
    me, block = lax.axis_index("det"), lax.axis_index("obs")
    tiles = list_ref.shape[1]
    listed = list_ref[...]
    owner = lax.div(listed, jnp.full_like(listed, held))
    place_in = iota(listed.shape, 1).astype(F32)
    hit = owner == block
    inside = (listed - block * held + 1).astype(F32)
    low = jnp.min(jnp.where(hit, place_in, F32(tiles)), 1, keepdims=True)
    high = jnp.max(jnp.where(hit, place_in, F32(-1)), 1, keepdims=True)
    first = jnp.where(hit & (place_in == low), inside, 0.0)
    second = jnp.where(hit & (place_in == high) & (high > low), inside, 0.0)
    size = obs * CAP * MP
    wanted = jnp.full((size, LANES), -1.0, F32)
    for s, found in enumerate((first, second)):
        value = jnp.broadcast_to(jnp.sum(found, 1, keepdims=True), (obs, LANES)).astype(BF16)
        row, col = iota((size, obs), 0), iota((size, obs), 1)
        spread = (col == row // (CAP * MP)) & ((row // MP) % CAP == s)
        wanted = wanted + jnp.dot(spread.astype(F32).astype(BF16), value, preferred_element_type=F32)
    wide = (size, held * MP)
    goal = wanted[:, : held * MP] * MP + (iota(wide, 0) % MP).astype(F32)
    ok = (wanted[:, : held * MP] >= 0) & (goal == iota(wide, 1).astype(F32))
    own[...] = ok.astype(F32).astype(BF16)
    wide = (held * MP, held * rows_all)
    row, col = iota(wide, 0), iota(wide, 1)
    ok = (col == (row // MP) * rows_all + me * mine + row % MP) & (row % MP < mine)
    mine_sel[...] = ok.astype(F32).astype(BF16)
    owner = owner.astype(F32)
    here = iota((obs, LANES), 0) == block
    down = lax.dot_general(
        owner.astype(BF16), here.astype(F32).astype(BF16), COLS_COLS, preferred_element_type=F32
    )
    along_row = jnp.sum(jnp.where(iota(listed.shape, 0) == block, owner, 0.0), 0, keepdims=True)
    square = (tiles, tiles)
    before = (down[:, :tiles] == along_row) & (iota(square, 1) < iota(square, 0))
    rank = jnp.sum(before.astype(F32), 1, keepdims=True)
    slot = (down * CAP + rank).astype(BF16)
    tall = (tiles * MP, tiles)
    spread = (iota(tall, 1) == iota(tall, 0) // MP).astype(F32).astype(BF16)
    slot = jnp.dot(spread, slot, preferred_element_type=F32)
    wide = (tiles * MP, size)
    goal = jnp.broadcast_to(slot[:, :1], wide) * MP + (iota(wide, 0) % MP).astype(F32)
    pick[...] = (goal == iota(wide, 1).astype(F32)).astype(F32).astype(BF16)


def normal_kernel(
    obs, det, grid, sky_in, list_ref, along_ref, noise_ref, kernel_ref, w_ref,
    expand_ref, fwd_ref, inv_ref, tw_ref, edge_ref, ends_ref, sel_ref, sky_ref,
    out_ref, own_ref, pick_ref, mine_sel, ke_ref, x_out, zz, m_out,
    recv, fetched, scan, nrows, other, ts, u, spun, sums, e, es, payload, gathered, wide, zs, x,
    given, taken, staged, y_ref, eb_ref, turned, esums, g_ref, pre, pairs, parts, total_ref, terms, leave, recv2, full,
    k0, k1, n0, n1, m0, m1, r0, r1, xs0, xs1, es0, es1, gs0, gs1, zs0, zs1,
    ps0, ps1, ys0, ys1, fs0, fs1, g0, g1, q0, q1, s0, s1, *sems,
):
    me, block = lax.axis_index("det"), lax.axis_index("obs")
    across, down = grid
    bx, by = block // down, lax.rem(block, down)
    n = det // 2
    chip, core, side = me // 2, lax.rem(me, 2), me // n
    partner = me + 1 - 2 * core
    dets, tiles = w_ref.shape[0], along_ref.shape[0]
    width = noise_ref.shape[0]
    held, rows_all = sky_ref.shape[0], sky_ref.shape[1]
    bands = [band_of(slot, det) for slot in range(det)]
    slow = det
    peers = all_det(det)

    def prepare():
        selections(obs, list_ref, own_ref, pick_ref, mine_sel, rows_all // det, rows_all, held)
        my_rows = jnp.dot(mine_sel[...], sky_in[...], preferred_element_type=F32).astype(BF16)
        got = jnp.dot(own_ref[...], my_rows, preferred_element_type=F32)
        out_ref[...] = got.reshape(obs, CAP * MP, LANES)

    greet(obs, det, True, peers, prepare)

    sky_start, sky_wait = obs_copies(obs, out_ref, recv, k0, k1)
    sky_start()
    part = noise_ref.shape[1] // 2
    whole = det_send(noise_ref, nrows, n0.at[0], n1.at[0], lax.rem(2 * det - me, det))
    left = det_send(noise_ref.at[:, :part], other, n0.at[1], n1.at[1], det - 1 - me)
    right = det_send(noise_ref.at[:, part:], other, n0.at[1], n1.at[1], lax.rem(me + 1, det))

    @pl.when(core == 1)
    def _():
        whole.start()
        left.start()
        left.wait_send()
        whole.wait()

    @pl.when(core == 0)
    def _():
        right.start()
        nrows[...] = noise_ref[...]
        right.wait_send()

    left.wait_recv()
    both = jnp.where(core == 1, nrows[:, part:].astype(F32), nrows[:, :part].astype(F32))
    m_out[bx, by] = (both + other[...].astype(F32)).astype(BF16)

    def sideways(d):
        to = lax.rem(bx + d, across)
        return pltpu.make_async_remote_copy(
            src_ref=m_out.at[bx, by],
            dst_ref=m_out.at[bx, by],
            send_sem=m0.at[d],
            recv_sem=m1.at[d],
            device_id={"obs": to * down + by},
            device_id_type=MESH,
        )

    def ring(way, step):
        origin = lax.rem(by + down - way * (step - 1), down)
        cut = slice(None)
        if 2 * step == down:
            cut = slice(0, across // 2) if way > 0 else slice(across // 2, across)
        at = 0 if way > 0 else 1
        return pltpu.make_async_remote_copy(
            src_ref=m_out.at[cut, origin],
            dst_ref=m_out.at[cut, origin],
            send_sem=r0.at[at, step - 1],
            recv_sem=r1.at[at, step - 1],
            device_id={"obs": bx * down + lax.rem(by + down + way, down)},
            device_id_type=MESH,
        )

    def turn(step):
        for way in (1, -1):
            if step == 1:
                if way == 1:
                    for d in range(1, across):
                        sideways(d).wait_recv()
            else:
                ring(way, step - 1).wait_recv()
            if 2 * step <= down:
                ring(way, step).start()

    steps = iter(range(1, down // 2 + 2))

    def advance():
        step = next(steps, None)
        if step is not None:
            turn(step)

    for d in range(1, across):
        sideways(d).start()

    for q in range(4):
        cut = expand_ref[:, q * det * 16 : (q + 1) * det * 16]
        ke_ref[q * dets : (q + 1) * dets] = jnp.dot(
            kernel_ref[...], cut, preferred_element_type=F32
        ).astype(BF16)

    sky_wait()
    flat = recv[...].reshape(obs * CAP * MP, LANES).astype(BF16)
    fetched[...] = jnp.dot(pick_ref[...], flat, preferred_element_type=F32).astype(BF16)
    for k in range(0, tiles, 4):
        part_rows = fetched[4 * k : 4 * k + 16]
        low = pair_products(part_rows[:8], along_ref, k, False)
        high = pair_products(part_rows[8:], along_ref, k + 2, False)
        scan[me, 4 * k : 4 * k + 16] = jnp.concatenate([low, high], 0).astype(BF16)
    det_gather(det, scan, sems[:4], advance)

    for i in range(tiles // 4):
        rhs = scan[:, 16 * i : 16 * i + 16, :].reshape(det * 16, LANES)
        got = jnp.dot(ke_ref[...], rhs, preferred_element_type=F32)
        for q in range(4):
            k = 4 * i + q
            ts[k] = got[q * dets : (q + 1) * dets] * w_ref[:, k * LANES : (k + 1) * LANES].astype(F32)

    for h in range(2):

        def swap(g, carry):
            at = pl.ds(pl.multiple_of(g * 16, 16), 16)
            out = digit_swap([ts[h * det + i, at, :] for i in range(det)])
            for z in range(det):
                u[z, at, h * LANES : (h + 1) * LANES] = out[z].astype(BF16)
            return carry

        lax.fori_loop(0, dets // 16, swap, 0)

    sums[...] = jnp.zeros_like(sums)

    def ends(z, carry):
        sums[pl.ds(pl.multiple_of(z * 8, 8), 8), :dets] = lax.dot_general(
            ends_ref[...], u[z], (((1,), (1,)), ((), ())), preferred_element_type=F32
        )
        return carry

    lax.fori_loop(0, det, ends, 0)
    e[...] = split_dot(edge_ref[...], sums[...], ROWS_COLS)
    own = pl.ds(pl.multiple_of(me * 8, 8), 8)
    edges = []
    for d in range(1, det):
        to = peers[d - 1]
        edges.append(
            det_send(e.at[pl.ds(pl.multiple_of(to * 8, 8), 8)], es.at[own], es0.at[d], es1.at[d], to)
        )
        edges[-1].start()
    es[own, :] = e[own, :]
    advance()

    def fast(z, carry):
        a = jnp.dot(u[z], fwd_ref[...], preferred_element_type=F32)
        re, im = a[:, :LANES], a[:, LANES:]
        c, s = tw_ref[z, 0:1, :], tw_ref[z, 1:2, :]
        spun[z, :, :LANES] = re * c + im * s
        spun[z, :, LANES:] = im * c - re * s
        return carry

    lax.fori_loop(0, det, fast, 0)

    for copy in edges:
        copy.wait()
    for i in range(4):
        payload[16 * i : 16 * i + det] = es[pl.ds(i, det, stride=8), :].astype(BF16)
    give_start, give_wait = obs_copies(obs, payload, gathered, gs0, gs1, True)
    give_start()

    def last(g, carry):
        at = pl.ds(pl.multiple_of(g * 16, 16), 16)
        re = [spun[z, at, :LANES] for z in range(det)]
        im = [spun[z, at, LANES:] for z in range(det)]
        re, im = small_dft(re, im, -1)
        for b in range(det):
            to, lo = place(bands, b)
            x[to, at, lo : lo + LANES] = re[b].astype(BF16)
            x[to, at, lo + LANES : lo + FAST] = im[b].astype(BF16)
        return carry

    lax.fori_loop(0, dets // 16, last, 0)

    slot = lax.rem(me, n)

    def column(d):
        to = lax.rem(chip + d, n)
        return det_send(x.at[to], x_out.at[slot], xs0.at[d], xs1.at[slot], to * 2 + side)

    for d in far_first(n)[:-1]:
        column(d).start()
    mine = core == side

    @pl.when(mine)
    def _():
        x_out[slot] = x[chip]

    @pl.when(jnp.logical_not(mine))
    def _():
        column(0).start()

    advance()

    advance()
    for i in range(n):

        @pl.when(core * n + i != me)
        def _():
            det_send(x_out.at[i], x_out.at[i], xs0.at[0], xs1.at[i], me).wait_recv()

    for step in steps:
        turn(step)

    hn = n // 2
    swaps, sends = [], []

    def product(to_chip):
        at = to_chip * (2 * dets // width)
        rows = m_out[at // down, pl.ds(lax.rem(at, down), 2 * dets // width)]
        rows = rows.reshape(2 * dets, m_out.shape[3])
        return jnp.dot(rows, x_out[...].reshape(n * dets, 2 * FAST), preferred_element_type=F32)

    def finish(s, total):
        to_chip = core * hn + lax.rem(chip + s, hn)
        swaps[s].wait_recv()
        total = total + taken[s].astype(F32)
        for i in range(2):
            to = to_chip * 2 + i
            staged[s, i] = total[i * dets : (i + 1) * dets].astype(BF16)
            copy = det_send(staged.at[s, i], y_ref.at[chip], ys0.at[s, i], ys1.at[chip], to)

            @pl.when(to != me)
            def _():
                copy.start()

            @pl.when(to == me)
            def _():
                y_ref[chip] = staged[s, i]

            sends.append((to, copy))

    before = None
    for s in range(hn):
        near = lax.rem(chip + s, hn)
        given[s] = product((1 - core) * hn + near).astype(BF16)
        swaps.append(det_send(given.at[s], taken.at[s], ps0.at[s], ps1.at[s], partner))
        swaps[-1].start()
        total = product(core * hn + near)
        if before is not None:
            finish(s - 1, before)
        before = total
    finish(hn - 1, before)
    give_wait()
    wide[...] = gathered[...].reshape(obs * 64, LANES).astype(F32)
    prod = jnp.zeros((obs * 4, width), F32)
    for j in range(det):
        lhs = wide[pl.ds(j, obs * 4, stride=16), :dets].astype(BF16)
        rhs = nrows[:, j * dets : (j + 1) * dets]
        prod = prod + lax.dot_general(lhs, rhs, (((1,), (1,)), ((), ())), preferred_element_type=F32)
    zs[...] = jnp.zeros_like(zs)
    for p in range(obs):
        zs[p, 0:4, :width] = prod[4 * p : 4 * p + 4]
    z_start, z_wait = obs_copies(obs, zs, zz, zs0, zs1)
    z_start()
    z_wait()
    per = obs // det
    finals = []
    for d in range(1, det):
        to = peers[d - 1]
        finals.append(det_send(zz.at[pl.ds(to * per, per)], eb_ref.at[me], fs0.at[d], fs1.at[d], to))
        finals[-1].start()
    eb_ref[me] = zz[pl.ds(me * per, per)]

    for c in range(n):

        @pl.when(c * 2 + side != me)
        def _():
            det_send(y_ref.at[c], y_ref.at[c], ys0.at[0, 0], ys1.at[c], me).wait_recv()

    for copy in finals:
        copy.wait()

    def first(g, carry):
        at = pl.ds(pl.multiple_of(g * 16, 16), 16)
        re, im = [], []
        for b in range(slow):
            chip, lo = place(bands, b)
            re.append(y_ref[chip, at, lo : lo + LANES].astype(F32))
            im.append(y_ref[chip, at, lo + LANES : lo + FAST].astype(F32))
        re, im = small_dft(re, im, 1)
        for z in range(slow):
            c, s = tw_ref[z, 0:1, :], tw_ref[z, 1:2, :]
            turned[z, at, :LANES] = (re[z] * c - im[z] * s).astype(BF16)
            turned[z, at, LANES:] = (im[z] * c + re[z] * s).astype(BF16)
        return carry

    lax.fori_loop(0, dets // 16, first, 0)
    for q in range(2):
        rows = eb_ref[:, q].reshape(8 * slow, LANES)
        esums[q] = split_dot(edge_ref[...], rows, COLS_COLS).astype(BF16).astype(F32)

    def fast(z, carry):
        o = jnp.dot(turned[z], inv_ref[...], preferred_element_type=F32)
        at = pl.ds(pl.multiple_of(z * 8, 8), 8)
        edge = [
            lax.dot_general(
                esums[q, at, :].astype(BF16), ends_ref[...], COLS_COLS, preferred_element_type=F32
            )[: dets // 2]
            for q in range(2)
        ]
        o = o + jnp.concatenate(edge, 0)
        ts[z] = o[:, :LANES]
        ts[slow + z] = o[:, LANES:]
        return carry

    lax.fori_loop(0, slow, fast, 0)

    for h in range(2):

        def swap(g, carry):
            at = pl.ds(pl.multiple_of(g * 16, 16), 16)
            out = digit_swap([ts[h * slow + z, at, :] for z in range(slow)])
            for i in range(slow):
                ts[h * slow + i, at, :] = out[i]
            return carry

        lax.fori_loop(0, dets // 16, swap, 0)

    for i in range(tiles // 4):
        filtered = [
            (ts[k] * w_ref[:, k * LANES : (k + 1) * LANES].astype(F32)).astype(BF16)
            for k in range(4 * i, 4 * i + 4)
        ]
        rows = lax.dot_general(
            ke_ref[...], jnp.concatenate(filtered, 0), COLS_COLS, preferred_element_type=F32
        )
        g_ref[:, :, 16 * i : 16 * i + 16, :] = rows.reshape(n, 2, 16, LANES).astype(BF16)

    swap_pairs = det_send(g_ref.at[:, 1 - core], pre, g0.at[0], g1.at[0], partner)
    swap_pairs.start()
    swap_pairs.wait()
    for c in range(n):
        pairs[c] = (g_ref[c, core].astype(F32) + pre[c].astype(F32)).astype(BF16)
    copies = []
    for d in far_first(n)[:-1]:
        to = lax.rem(chip + d, n)
        copies.append(det_send(pairs.at[to], parts.at[chip], q0.at[d], q1.at[d], to * 2 + core))
        copies[-1].start()
    parts[chip] = pairs[chip]
    for copy in copies:
        copy.wait()
    total = parts[0].astype(F32)
    for c in range(1, n):
        total = total + parts[c].astype(F32)
    total_ref[...] = total
    for k in range(0, tiles, 2):
        rows = total_ref[4 * k : 4 * k + 8]
        high = rows.astype(BF16)
        low = (rows - high.astype(F32)).astype(BF16)
        terms[4 * k : 4 * k + 8] = pair_products(high, along_ref, k, True) + pair_products(
            low, along_ref, k, True
        )
    leave[...] = split_dot(pick_ref[...], terms[...], COLS_COLS).reshape(obs, CAP * MP, LANES)
    start, wait = obs_copies(obs, leave, recv2, s0, s1)
    start()
    wait()
    flat = recv2[...].reshape(obs * CAP * MP, LANES)
    full[me] = split_dot(own_ref[...], flat, COLS_COLS).astype(BF16)
    det_gather(det, full, sems[4:])
    for i in range(held // 4):
        rhs = full[:, 16 * i : 16 * i + 16, :].reshape(det * 16, LANES)
        got = jnp.dot(sel_ref[...], rhs, preferred_element_type=F32)
        sky_ref[4 * i : 4 * i + 4] = got.reshape(4, rows_all, LANES)
    for copy in swaps:
        copy.wait_send()
    for to, copy in sends:

        @pl.when(to != me)
        def _():
            copy.wait_send()

    for d in far_first(n)[:-1]:
        column(d).wait_send()

    @pl.when(jnp.logical_not(mine))
    def _():
        column(0).wait_send()

    for d in range(1, across):
        sideways(d).wait_send()
    for step in range(1, down // 2 + 1):
        for way in (1, -1):
            ring(way, step).wait_send()


def call(kernel, out, scratch, name, collective=None):
    if collective is None:
        params = pltpu.CompilerParams(vmem_limit_bytes=56 * 2**20)
    else:
        params = pltpu.CompilerParams(
            vmem_limit_bytes=56 * 2**20, collective_id=collective, has_side_effects=True
        )

    def run(*args):
        return pl.pallas_call(
            kernel,
            out_shape=out,
            in_specs=[VMEM] * len(args),
            out_specs=VMEM if not isinstance(out, tuple) else (VMEM,) * len(out),
            scratch_shapes=scratch,
            compiler_params=params,
            name=name,
        )(*args)

    return run


def dma(n):
    return [pltpu.SemaphoreType.DMA((n,))] * 2


def local(sky, tile_list, along, detector_kernel, sample_weight, noise_inverse):
    obs, det = lax.axis_size("obs"), lax.axis_size("det")
    held, tiles = sky.shape[0], tile_list.shape[1]
    dets, all_dets = detector_kernel.shape[0], noise_inverse.shape[2]
    rows_all = sky.shape[1] * sky.shape[2]
    mine = rows_all // det
    fwd, inv, tw, edge, ends = tables(det)

    expand = np.zeros((rows_all, 4, det, 4, MP), np.float32)
    for q in range(4):
        for j in range(det):
            for m in range(mine):
                expand[j * mine + m, q, j, q, m] = 1
    expand = jnp.asarray(expand.reshape(rows_all, -1), BF16)
    sel = np.zeros((4, det, mine, det, 4, MP), np.float32)
    for q in range(4):
        for j in range(det):
            for m in range(mine):
                sel[q, j, m, j, q, m] = 1
    sel = jnp.asarray(sel.reshape(4 * rows_all, det * 16), BF16)

    block = along[0]
    n, half, per = det // 2, det // 4, obs // det
    down = 8 if obs == 32 else obs // 2
    grid = (obs // down, down)
    mine, part = noise_inverse.shape[1], all_dets // 2
    member = jax.ShapeDtypeStruct((n, dets, 2 * FAST), BF16)
    slots = jax.ShapeDtypeStruct((obs, CAP * MP, LANES), F32)
    slot_buffer = pltpu.VMEM(slots.shape, F32)
    row_buffer = pltpu.VMEM((tiles * MP, LANES), F32)
    pieces = pltpu.VMEM((n, tiles * MP, LANES), BF16)
    edge_rows = pltpu.VMEM((8 * det, LANES), F32)
    mixed = pltpu.VMEM((half, 2 * dets, 2 * FAST), BF16)
    normal = call(
        functools.partial(normal_kernel, obs, det, grid),
        jax.ShapeDtypeStruct((held, rows_all, LANES), F32),
        [
            slot_buffer,
            pltpu.VMEM((obs * CAP * MP, held * MP), BF16),
            pltpu.VMEM((tiles * MP, obs * CAP * MP), BF16),
            pltpu.VMEM((held * MP, held * rows_all), BF16),
            pltpu.VMEM((4 * dets, det * 16), BF16),
            pltpu.VMEM(member.shape, BF16),
            slot_buffer,
            pltpu.VMEM((*grid, mine, part), BF16),
            slot_buffer,
            pltpu.VMEM((tiles * MP, LANES), BF16),
            pltpu.VMEM((det, tiles * MP, LANES), BF16),
            pltpu.VMEM((mine, all_dets), BF16),
            pltpu.VMEM((mine, part), BF16),
            pltpu.VMEM((tiles, dets, LANES), F32),
            pltpu.VMEM((det, dets, FAST), BF16),
            pltpu.VMEM((det, dets, FAST), F32),
            edge_rows,
            edge_rows,
            edge_rows,
            pltpu.VMEM((64, LANES), BF16),
            pltpu.VMEM((obs, 64, LANES), BF16),
            pltpu.VMEM((obs * 64, LANES), F32),
            slot_buffer,
            pltpu.VMEM(member.shape, BF16),
            mixed,
            mixed,
            pltpu.VMEM((half, 2, dets, 2 * FAST), BF16),
            pltpu.VMEM(member.shape, BF16),
            pltpu.VMEM((det, per, CAP * MP, LANES), F32),
            pltpu.VMEM((det, dets, FAST), BF16),
            pltpu.VMEM((2, 8 * det, LANES), F32),
            pltpu.VMEM((n, 2, tiles * MP, LANES), BF16),
            pieces,
            pieces,
            pieces,
            row_buffer,
            row_buffer,
            slot_buffer,
            slot_buffer,
            pltpu.VMEM((det, held * MP, LANES), BF16),
            *dma(obs),
            *dma(2),
            *dma(grid[0]),
            *[pltpu.SemaphoreType.DMA((2, down // 2))] * 2,
            *dma(n),
            *dma(det),
            *dma(obs),
            *dma(obs),
            *dma(half),
            pltpu.SemaphoreType.DMA((half, 2)),
            pltpu.SemaphoreType.DMA((n,)),
            *dma(det),
            *dma(1),
            *dma(n),
            *dma(obs),
            *dma(n),
            *dma(n),
            *dma(n),
            *dma(n),
        ],
        "normal",
        0,
    )(
        sky.reshape(held * rows_all, LANES), tile_list, block, noise_inverse[0], detector_kernel, sample_weight,
        expand, fwd, inv, tw, edge, ends, sel,
    )
    return normal.reshape(sky.shape)


def solution(mesh):
    in_specs = (
        P("obs", None, None, None),
        P(),
        P("obs", None, None, None),
        P("det", None),
        P("det", "obs"),
        P("det", "obs", None),
    )
    out_specs = P("obs", None, None, None)
    return jax.shard_map(local, mesh=mesh, in_specs=in_specs, out_specs=out_specs, check_vma=False)
```

```python
import functools
import math

import jax
import jax.numpy as jnp
import numpy as np
from jax import lax
from jax.experimental import pallas as pl
from jax.experimental.pallas import tpu as pltpu
from jax.sharding import PartitionSpec as P

CAP = 2
MP = 4
FAST = 256
LANES = 128
MESH = pl.DeviceIdType.MESH
F32 = jnp.float32
BF16 = jnp.bfloat16
VMEM = pl.BlockSpec(memory_space=pltpu.VMEM)


def band_of(slot, det):
    return slot if slot % 2 == 0 else det - slot


def tables(slow):
    lane = np.arange(FAST)
    half, rest = lane // LANES, lane % LANES
    j, i = rest // slow, rest % slow
    w = half * LANES + i * (LANES // slow) + j
    r = np.arange(LANES)
    angle = 2 * np.pi / FAST * (w[:, None] * r[None, :] % FAST)
    c, s = np.cos(angle) / math.sqrt(FAST), np.sin(angle) / math.sqrt(FAST)
    forward = np.concatenate([c, -s], 1)
    keep = (r > 0)[:, None]
    inverse = np.concatenate([c.T * keep, -s.T * keep], 0)
    twist = 2 * np.pi / (slow * FAST) * (np.arange(slow)[:, None] * r[None, :])
    tw = np.stack([np.cos(twist), np.sin(twist)], 1) / math.sqrt(slow)
    edge = np.zeros((slow, 8, slow, 8))
    for slot in range(slow):
        for v in range(2):
            turn = 2 * np.pi / slow * (band_of(slot, slow) + v / 2) * np.arange(slow)
            edge[slot, 2 * v, :, v] = np.cos(turn) / math.sqrt(slow)
            edge[slot, 2 * v + 1, :, v] = -np.sin(turn) / math.sqrt(slow)
    ends = np.zeros((8, FAST))
    ends[0] = 1 / math.sqrt(FAST)
    ends[1] = (1 - 2 * (w % 2)) / math.sqrt(FAST)
    return (
        jnp.asarray(forward, BF16),
        jnp.asarray(inverse, BF16),
        jnp.asarray(tw, F32),
        jnp.asarray(edge.reshape(8 * slow, 8 * slow), BF16),
        jnp.asarray(ends, BF16),
    )


def small_dft(re, im, sign):
    n = len(re)
    if n == 1:
        return re, im
    er, ei = small_dft(re[0::2], im[0::2], sign)
    odr, odi = small_dft(re[1::2], im[1::2], sign)
    outr, outi = [None] * n, [None] * n
    for k in range(n // 2):
        if k == 0:
            tr, ti = odr[0], odi[0]
        elif 4 * k == n:
            tr, ti = (-odi[k], odr[k]) if sign > 0 else (odi[k], -odr[k])
        else:
            c = math.cos(2 * math.pi * k / n)
            s = sign * math.sin(2 * math.pi * k / n)
            if 8 * k == n:
                tr, ti = (
                    c * (odr[k] - sign * odi[k]),
                    c * (odi[k] + sign * odr[k]),
                )
            else:
                tr, ti = c * odr[k] - s * odi[k], c * odi[k] + s * odr[k]
        outr[k], outi[k] = er[k] + tr, ei[k] + ti
        outr[k + n // 2], outi[k + n // 2] = er[k] - tr, ei[k] - ti
    return outr, outi


def digit_swap(tiles):
    n = len(tiles)
    tiles = list(tiles)
    lane = lax.broadcasted_iota(jnp.int32, tiles[0].shape, 1)
    step = 1
    while step < n:
        odd = (lane // step) % 2 == 1
        for i in range(n):
            if i & step:
                continue
            a, b = tiles[i], tiles[i | step]
            tiles[i] = jnp.where(odd, pltpu.roll(b, step, 1), a)
            tiles[i | step] = jnp.where(odd, b, pltpu.roll(a, LANES - step, 1))
        step *= 2
    return tiles


def greet(obs, det, with_obs, det_peers, meanwhile=None):
    barrier = pltpu.get_barrier_semaphore()
    count = 0
    if with_obs:
        me = lax.axis_index("obs")

        def signal(d, carry):
            pl.semaphore_signal(
                barrier, inc=1, device_id={"obs": lax.rem(me + d, obs)}, device_id_type=MESH
            )
            return carry

        lax.fori_loop(1, obs, signal, 0)
        count += obs - 1
    for peer in det_peers:
        pl.semaphore_signal(barrier, inc=1, device_id={"det": peer}, device_id_type=MESH)
    count += len(det_peers)
    if meanwhile is not None:
        meanwhile()
    pl.semaphore_wait(barrier, count)


def same_core(det):
    me = lax.axis_index("det")
    others = [lax.rem(me + 2 * d, det) for d in range(1, det // 2)]
    partner = me + 1 - 2 * lax.rem(me, 2)
    return others, partner


def obs_copies(obs, src, dst, send_sem, recv_sem, same=False):
    me = lax.axis_index("obs")

    def copy(d):
        to = lax.rem(me + d, obs)
        return pltpu.make_async_remote_copy(
            src_ref=src if same else src.at[to],
            dst_ref=dst.at[me],
            send_sem=send_sem.at[d],
            recv_sem=recv_sem.at[d],
            device_id={"obs": to},
            device_id_type=MESH,
        )

    def start():
        def step(d, carry):
            copy(d).start()
            return carry

        lax.fori_loop(1, obs, step, 0)
        dst[me] = src[...] if same else src[me]

    def wait():
        def step(d, carry):
            copy(d).wait()
            return carry

        lax.fori_loop(1, obs, step, 0)

    return start, wait


def det_send(src, dst, send_sem, recv_sem, to):
    return pltpu.make_async_remote_copy(
        src_ref=src,
        dst_ref=dst,
        send_sem=send_sem,
        recv_sem=recv_sem,
        device_id={"det": to},
        device_id_type=MESH,
    )


def far_first(n):
    return sorted(range(n), key=lambda d: -min(d, n - d))


def det_gather(det, full, sems, sent=lambda: None):
    send_sem, recv_sem, pass_send, pass_recv = sems
    me = lax.axis_index("det")
    others, partner = same_core(det)

    def copy(slot, to, a, b):
        return pltpu.make_async_remote_copy(
            src_ref=full.at[slot],
            dst_ref=full.at[slot],
            send_sem=a,
            recv_sem=b,
            device_id={"det": to},
            device_id_type=MESH,
        )

    n = det // 2
    order = sorted(range(1, n), key=lambda d: -min(d, n - d))
    outs = []
    for d in order:
        outs.append(copy(me, others[d - 1], send_sem.at[d], recv_sem.at[d]))
        outs[-1].start()
    outs.append(copy(me, partner, pass_send.at[0], pass_recv.at[0]))
    outs[-1].start()
    sent()
    for d in reversed(order):
        source = lax.rem(me + det - 2 * d, det)
        copy(source, me, send_sem.at[d], recv_sem.at[d]).wait_recv()
        outs.append(copy(source, partner, pass_send.at[d], pass_recv.at[d]))
        outs[-1].start()
    for d in range(n):
        source = lax.rem(partner + det - 2 * d, det)
        copy(source, partner, pass_send.at[d], pass_recv.at[d]).wait_recv()
    for out in outs:
        out.wait_send()


def pair_products(rows, along, k, transposed):
    dims = (((1,), (1 if transposed else 0,)), ((), ()))
    first = lax.dot_general(rows, along[k], dims, preferred_element_type=F32)
    second = lax.dot_general(rows, along[k + 1], dims, preferred_element_type=F32)
    index = lax.broadcasted_iota(jnp.int32, first.shape, 0)
    return jnp.where(index < MP, first, second)


def split_dot(exact, x, dims):
    high = x.astype(BF16)
    low = (x - high.astype(F32)).astype(BF16)
    dot = functools.partial(lax.dot_general, dimension_numbers=dims, preferred_element_type=F32)
    return dot(exact, high) + dot(exact, low)


ROWS_COLS = (((1,), (0,)), ((), ()))
COLS_COLS = (((0,), (0,)), ((), ()))


def place(slot_band, b):
    slot = slot_band.index(b)
    return slot // 2, (slot % 2) * FAST


def all_det(det):
    me = lax.axis_index("det")
    return [lax.rem(me + d, det) for d in range(1, det)]


def iota(shape, dim):
    return lax.broadcasted_iota(jnp.int32, shape, dim)


def selections(obs, list_ref, own, pick, mine_sel, mine, rows_all, held):
    me, block = lax.axis_index("det"), lax.axis_index("obs")
    tiles = list_ref.shape[1]
    listed = list_ref[...]
    owner = lax.div(listed, jnp.full_like(listed, held))
    place_in = iota(listed.shape, 1).astype(F32)
    hit = owner == block
    inside = (listed - block * held + 1).astype(F32)
    low = jnp.min(jnp.where(hit, place_in, F32(tiles)), 1, keepdims=True)
    high = jnp.max(jnp.where(hit, place_in, F32(-1)), 1, keepdims=True)
    first = jnp.where(hit & (place_in == low), inside, 0.0)
    second = jnp.where(hit & (place_in == high) & (high > low), inside, 0.0)
    size = obs * CAP * MP
    wanted = jnp.full((size, LANES), -1.0, F32)
    for s, found in enumerate((first, second)):
        value = jnp.broadcast_to(jnp.sum(found, 1, keepdims=True), (obs, LANES)).astype(BF16)
        row, col = iota((size, obs), 0), iota((size, obs), 1)
        spread = (col == row // (CAP * MP)) & ((row // MP) % CAP == s)
        wanted = wanted + jnp.dot(spread.astype(F32).astype(BF16), value, preferred_element_type=F32)
    wide = (size, held * MP)
    goal = wanted[:, : held * MP] * MP + (iota(wide, 0) % MP).astype(F32)
    ok = (wanted[:, : held * MP] >= 0) & (goal == iota(wide, 1).astype(F32))
    own[...] = ok.astype(F32).astype(BF16)
    wide = (held * MP, held * rows_all)
    row, col = iota(wide, 0), iota(wide, 1)
    ok = (col == (row // MP) * rows_all + me * mine + row % MP) & (row % MP < mine)
    mine_sel[...] = ok.astype(F32).astype(BF16)
    owner = owner.astype(F32)
    here = iota((obs, LANES), 0) == block
    down = lax.dot_general(
        owner.astype(BF16), here.astype(F32).astype(BF16), COLS_COLS, preferred_element_type=F32
    )
    along_row = jnp.sum(jnp.where(iota(listed.shape, 0) == block, owner, 0.0), 0, keepdims=True)
    square = (tiles, tiles)
    before = (down[:, :tiles] == along_row) & (iota(square, 1) < iota(square, 0))
    rank = jnp.sum(before.astype(F32), 1, keepdims=True)
    slot = (down * CAP + rank).astype(BF16)
    tall = (tiles * MP, tiles)
    spread = (iota(tall, 1) == iota(tall, 0) // MP).astype(F32).astype(BF16)
    slot = jnp.dot(spread, slot, preferred_element_type=F32)
    wide = (tiles * MP, size)
    goal = jnp.broadcast_to(slot[:, :1], wide) * MP + (iota(wide, 0) % MP).astype(F32)
    pick[...] = (goal == iota(wide, 1).astype(F32)).astype(F32).astype(BF16)


def normal_kernel(
    obs, det, grid, sky_in, list_ref, along_ref, noise_ref, kernel_ref, w_ref,
    expand_ref, fwd_ref, inv_ref, tw_ref, edge_ref, ends_ref, sel_ref, sky_ref,
    out_ref, own_ref, pick_ref, mine_sel, ke_ref, x_out, zz, m_out,
    recv, fetched, scan, nrows, other, ts, u, spun, sums, e, es, payload, gathered, wide, zs, x,
    given, taken, staged, y_ref, eb_ref, turned, esums, g_ref, pre, pairs, parts, total_ref, terms, leave, recv2, full, by_x, by_y,
    k0, k1, n0, n1, m0, m1, r0, r1, xs0, xs1, es0, es1, gs0, gs1, zs0, zs1,
    ps0, ps1, ys0, ys1, vx0, vx1, wx0, vy0, vy1, wy0, fs0, fs1, g0, g1, q0, q1, s0, s1, *sems,
):
    me, block = lax.axis_index("det"), lax.axis_index("obs")
    across, down = grid
    bx, by = block // down, lax.rem(block, down)
    n = det // 2
    chip, core, side = me // 2, lax.rem(me, 2), me // n
    partner = me + 1 - 2 * core
    dets, tiles = w_ref.shape[0], along_ref.shape[0]
    width = noise_ref.shape[0]
    held, rows_all = sky_ref.shape[0], sky_ref.shape[1]
    bands = [band_of(slot, det) for slot in range(det)]
    slow = det
    peers = all_det(det)

    def prepare():
        selections(obs, list_ref, own_ref, pick_ref, mine_sel, rows_all // det, rows_all, held)
        my_rows = jnp.dot(mine_sel[...], sky_in[...], preferred_element_type=F32).astype(BF16)
        got = jnp.dot(own_ref[...], my_rows, preferred_element_type=F32)
        out_ref[...] = got.reshape(obs, CAP * MP, LANES)

    greet(obs, det, True, peers, prepare)

    sky_start, sky_wait = obs_copies(obs, out_ref, recv, k0, k1)
    sky_start()
    part = noise_ref.shape[1] // 2
    whole = det_send(noise_ref, nrows, n0.at[0], n1.at[0], lax.rem(2 * det - me, det))
    left = det_send(noise_ref.at[:, :part], other, n0.at[1], n1.at[1], det - 1 - me)
    right = det_send(noise_ref.at[:, part:], other, n0.at[1], n1.at[1], lax.rem(me + 1, det))

    @pl.when(core == 1)
    def _():
        whole.start()
        left.start()
        left.wait_send()
        whole.wait()

    @pl.when(core == 0)
    def _():
        right.start()
        nrows[...] = noise_ref[...]
        right.wait_send()

    left.wait_recv()
    both = jnp.where(core == 1, nrows[:, part:].astype(F32), nrows[:, :part].astype(F32))
    m_out[bx, by] = (both + other[...].astype(F32)).astype(BF16)

    def sideways(d):
        to = lax.rem(bx + d, across)
        return pltpu.make_async_remote_copy(
            src_ref=m_out.at[bx, by],
            dst_ref=m_out.at[bx, by],
            send_sem=m0.at[d],
            recv_sem=m1.at[d],
            device_id={"obs": to * down + by},
            device_id_type=MESH,
        )

    def ring(way, step):
        origin = lax.rem(by + down - way * (step - 1), down)
        cut = slice(None)
        if 2 * step == down:
            cut = slice(0, across // 2) if way > 0 else slice(across // 2, across)
        at = 0 if way > 0 else 1
        return pltpu.make_async_remote_copy(
            src_ref=m_out.at[cut, origin],
            dst_ref=m_out.at[cut, origin],
            send_sem=r0.at[at, step - 1],
            recv_sem=r1.at[at, step - 1],
            device_id={"obs": bx * down + lax.rem(by + down + way, down)},
            device_id_type=MESH,
        )

    def turn(step):
        for way in (1, -1):
            if step == 1:
                if way == 1:
                    for d in range(1, across):
                        sideways(d).wait_recv()
            else:
                ring(way, step - 1).wait_recv()
            if 2 * step <= down:
                ring(way, step).start()

    steps = iter(range(1, down // 2 + 2))

    def advance():
        step = next(steps, None)
        if step is not None:
            turn(step)

    for d in range(1, across):
        sideways(d).start()

    for q in range(4):
        cut = expand_ref[:, q * det * 16 : (q + 1) * det * 16]
        ke_ref[q * dets : (q + 1) * dets] = jnp.dot(
            kernel_ref[...], cut, preferred_element_type=F32
        ).astype(BF16)

    sky_wait()
    flat = recv[...].reshape(obs * CAP * MP, LANES).astype(BF16)
    fetched[...] = jnp.dot(pick_ref[...], flat, preferred_element_type=F32).astype(BF16)
    for k in range(0, tiles, 4):
        part_rows = fetched[4 * k : 4 * k + 16]
        low = pair_products(part_rows[:8], along_ref, k, False)
        high = pair_products(part_rows[8:], along_ref, k + 2, False)
        scan[me, 4 * k : 4 * k + 16] = jnp.concatenate([low, high], 0).astype(BF16)
    det_gather(det, scan, sems[:4], advance)

    chunk = dets // 2
    cuts = [slice(c * chunk, (c + 1) * chunk) for c in range(2)]
    far = n // 2
    relayed = n >= 4
    slot = lax.rem(me, n)
    back_chip = lax.rem(chip + n - 1, n)
    from_chip = lax.rem(chip + 1, n)
    from_side = from_chip // far
    final_chip = lax.rem(from_chip + far, n)
    mine = core == side
    lefts = []

    def column(d, c):
        to = lax.rem(chip + d, n)
        return det_send(
            x.at[to, cuts[c]], x_out.at[slot, cuts[c]], xs0.at[d, c], xs1.at[slot, c], to * 2 + side
        )

    def over(source):
        to = back_chip * 2 + side
        return det_send(x.at[lax.rem(chip + far, n), cuts[0]], by_x.at[source], vx0.at[0], vx1.at[source], to)

    def onward(source):
        at = lax.rem(from_chip * 2 + source, n)
        return det_send(
            by_x.at[source], x_out.at[at, cuts[0]], wx0.at[source], xs1.at[at, 0], final_chip * 2 + from_side
        )

    def timestream(c):
        for i in range(tiles // 4):
            rhs = scan[:, 16 * i : 16 * i + 16, :].reshape(det * 16, LANES)
            lhs = [ke_ref[q * dets + c * chunk : q * dets + (c + 1) * chunk] for q in range(4)]
            got = jnp.dot(jnp.concatenate(lhs, 0), rhs, preferred_element_type=F32)
            for q in range(4):
                k = 4 * i + q
                weight = w_ref[cuts[c], k * LANES : (k + 1) * LANES].astype(F32)
                ts[k, cuts[c]] = got[q * chunk : (q + 1) * chunk] * weight
        for h in range(2):

            def swap(g, carry):
                at = pl.ds(pl.multiple_of(c * chunk + g * 16, 16), 16)
                out = digit_swap([ts[h * det + i, at, :] for i in range(det)])
                for z in range(det):
                    u[z, at, h * LANES : (h + 1) * LANES] = out[z].astype(BF16)
                return carry

            lax.fori_loop(0, chunk // 16, swap, 0)

    def transform(c):
        def fast(z, carry):
            a = jnp.dot(u[z, cuts[c]], fwd_ref[...], preferred_element_type=F32)
            re, im = a[:, :LANES], a[:, LANES:]
            cs, sn = tw_ref[z, 0:1, :], tw_ref[z, 1:2, :]
            spun[z, cuts[c], :LANES] = re * cs + im * sn
            spun[z, cuts[c], LANES:] = im * cs - re * sn
            return carry

        lax.fori_loop(0, det, fast, 0)

        def last(g, carry):
            at = pl.ds(pl.multiple_of(c * chunk + g * 16, 16), 16)
            re = [spun[z, at, :LANES] for z in range(det)]
            im = [spun[z, at, LANES:] for z in range(det)]
            re, im = small_dft(re, im, -1)
            for b in range(det):
                to, lo = place(bands, b)
                x[to, at, lo : lo + LANES] = re[b].astype(BF16)
                x[to, at, lo + LANES : lo + FAST] = im[b].astype(BF16)
            return carry

        lax.fori_loop(0, chunk // 16, last, 0)

    def send_columns(c):
        for d in far_first(n)[:-1]:
            if relayed and c == 0 and d == far:
                for source in range(2):

                    @pl.when(core == source)
                    def _():
                        over(source).start()
            else:
                column(d, c).start()
                lefts.append(column(d, c))

        @pl.when(mine)
        def _():
            x_out[slot, cuts[c]] = x[chip, cuts[c]]

        @pl.when(jnp.logical_not(mine))
        def _():
            column(0, c).start()

    timestream(0)
    transform(0)
    send_columns(0)
    advance()
    timestream(1)

    sums[...] = jnp.zeros_like(sums)

    def ends(z, carry):
        sums[pl.ds(pl.multiple_of(z * 8, 8), 8), :dets] = lax.dot_general(
            ends_ref[...], u[z], (((1,), (1,)), ((), ())), preferred_element_type=F32
        )
        return carry

    transform(1)
    send_columns(1)
    advance()
    if relayed:

        @pl.when(core == from_side)
        def _():
            for source in range(2):
                det_send(by_x.at[source], by_x.at[source], vx0.at[0], vx1.at[source], me).wait_recv()
                onward(source).start()

    lax.fori_loop(0, det, ends, 0)
    e[...] = split_dot(edge_ref[...], sums[...], ROWS_COLS)
    own = pl.ds(pl.multiple_of(me * 8, 8), 8)
    edges = []
    for d in range(1, det):
        to = peers[d - 1]
        edges.append(
            det_send(e.at[pl.ds(pl.multiple_of(to * 8, 8), 8)], es.at[own], es0.at[d], es1.at[d], to)
        )
        edges[-1].start()
    es[own, :] = e[own, :]
    advance()
    for copy in edges:
        copy.wait()
    for i in range(4):
        payload[16 * i : 16 * i + det] = es[pl.ds(i, det, stride=8), :].astype(BF16)
    give_start, give_wait = obs_copies(obs, payload, gathered, gs0, gs1, True)
    give_start()
    advance()
    for i in range(n):

        @pl.when(core * n + i != me)
        def _():
            for c in range(2):
                det_send(
                    x_out.at[i, cuts[c]], x_out.at[i, cuts[c]], xs0.at[0, c], xs1.at[i, c], me
                ).wait_recv()

    for step in steps:
        turn(step)

    hn = n // 2
    swaps, sends = [], []

    def product(to_chip, c):
        blocks = [to_chip * 4 + 2 * i + c for i in range(2)]
        rows = jnp.concatenate([m_out[at // down, lax.rem(at, down)] for at in blocks], 0)
        return jnp.dot(rows, x_out[...].reshape(n * dets, 2 * FAST), preferred_element_type=F32)

    def finish(c, s, total):
        to_chip = core * hn + lax.rem(chip + s, hn)
        swaps[c * hn + s].wait_recv()
        total = total + taken[c, s].astype(F32)
        for i in range(2):
            to = to_chip * 2 + i
            staged[c, s, i] = total[i * chunk : (i + 1) * chunk].astype(BF16)
            copy = det_send(
                staged.at[c, s, i], y_ref.at[chip, cuts[c]], ys0.at[c, s, i], ys1.at[chip, c], to
            )
            direct = to != me
            if relayed and c == 0 and s == 0:
                direct = direct & mine
                around = det_send(
                    staged.at[c, s, i], by_y, vy0.at[i], vy1.at[0], back_chip * 2 + i
                )

                @pl.when(jnp.logical_not(mine))
                def _():
                    around.start()

                sends.append((jnp.logical_not(mine), around))

            @pl.when(direct)
            def _():
                copy.start()

            @pl.when(to == me)
            def _():
                y_ref[chip, cuts[c]] = staged[c, s, i]

            sends.append((direct, copy))

    before = None
    for c in range(2):
        for s in range(hn):
            near = lax.rem(chip + s, hn)
            given[c, s] = product((1 - core) * hn + near, c).astype(BF16)
            swaps.append(
                det_send(given.at[c, s], taken.at[c, s], ps0.at[c, s], ps1.at[c, s], partner)
            )
            swaps[-1].start()
            total = product(core * hn + near, c)
            if before is not None:
                finish(*before)
            before = (c, s, total)
    finish(*before)
    y_onward = det_send(
        by_y, y_ref.at[from_chip, cuts[0]], wy0.at[0], ys1.at[from_chip, 0], final_chip * 2 + core
    )
    if relayed:
        det_send(by_y, by_y, vy0.at[0], vy1.at[0], me).wait_recv()
        y_onward.start()

    give_wait()
    wide[...] = gathered[...].reshape(obs * 64, LANES).astype(F32)
    prod = jnp.zeros((obs * 4, width), F32)
    for j in range(det):
        lhs = wide[pl.ds(j, obs * 4, stride=16), :dets].astype(BF16)
        rhs = nrows[:, j * dets : (j + 1) * dets]
        prod = prod + lax.dot_general(lhs, rhs, (((1,), (1,)), ((), ())), preferred_element_type=F32)
    zs[...] = jnp.zeros_like(zs)
    for p in range(obs):
        zs[p, 0:4, :width] = prod[4 * p : 4 * p + 4]
    z_start, z_wait = obs_copies(obs, zs, zz, zs0, zs1)
    z_start()
    z_wait()
    per = obs // det
    finals = []
    for d in range(1, det):
        to = peers[d - 1]
        finals.append(det_send(zz.at[pl.ds(to * per, per)], eb_ref.at[me], fs0.at[d], fs1.at[d], to))
        finals[-1].start()
    eb_ref[me] = zz[pl.ds(me * per, per)]

    for copy in finals:
        copy.wait()
    for q in range(2):
        rows = eb_ref[:, q].reshape(8 * slow, LANES)
        esums[q] = split_dot(edge_ref[...], rows, COLS_COLS).astype(BF16).astype(F32)

    def inverse(c):
        for i in range(n):

            @pl.when(i * 2 + side != me)
            def _():
                det_send(
                    y_ref.at[i, cuts[c]], y_ref.at[i, cuts[c]], ys0.at[0, 0, 0], ys1.at[i, c], me
                ).wait_recv()

        def first(g, carry):
            at = pl.ds(pl.multiple_of(c * chunk + g * 16, 16), 16)
            re, im = [], []
            for b in range(slow):
                to, lo = place(bands, b)
                re.append(y_ref[to, at, lo : lo + LANES].astype(F32))
                im.append(y_ref[to, at, lo + LANES : lo + FAST].astype(F32))
            re, im = small_dft(re, im, 1)
            for z in range(slow):
                cs, sn = tw_ref[z, 0:1, :], tw_ref[z, 1:2, :]
                turned[z, at, :LANES] = (re[z] * cs - im[z] * sn).astype(BF16)
                turned[z, at, LANES:] = (im[z] * cs + re[z] * sn).astype(BF16)
            return carry

        lax.fori_loop(0, chunk // 16, first, 0)

        def fast(z, carry):
            at = pl.ds(pl.multiple_of(z * 8, 8), 8)
            o = jnp.dot(turned[z, cuts[c]], inv_ref[...], preferred_element_type=F32)
            o = o + lax.dot_general(
                esums[c, at, :].astype(BF16), ends_ref[...], COLS_COLS, preferred_element_type=F32
            )[:chunk]
            ts[z, cuts[c]] = o[:, :LANES]
            ts[slow + z, cuts[c]] = o[:, LANES:]
            return carry

        lax.fori_loop(0, slow, fast, 0)
        for h in range(2):

            def swap(g, carry):
                at = pl.ds(pl.multiple_of(c * chunk + g * 16, 16), 16)
                out = digit_swap([ts[h * slow + z, at, :] for z in range(slow)])
                for i in range(slow):
                    ts[h * slow + i, at, :] = out[i]
                return carry

            lax.fori_loop(0, chunk // 16, swap, 0)

    inverse(0)
    inverse(1)
    for i in range(tiles // 4):
        filtered = [
            (ts[k] * w_ref[:, k * LANES : (k + 1) * LANES].astype(F32)).astype(BF16)
            for k in range(4 * i, 4 * i + 4)
        ]
        rows = lax.dot_general(
            ke_ref[...], jnp.concatenate(filtered, 0), COLS_COLS, preferred_element_type=F32
        )
        g_ref[:, :, 16 * i : 16 * i + 16, :] = rows.reshape(n, 2, 16, LANES).astype(BF16)

    swap_pairs = det_send(g_ref.at[:, 1 - core], pre, g0.at[0], g1.at[0], partner)
    swap_pairs.start()
    swap_pairs.wait()
    for c in range(n):
        pairs[c] = (g_ref[c, core].astype(F32) + pre[c].astype(F32)).astype(BF16)
    copies = []
    for d in far_first(n)[:-1]:
        to = lax.rem(chip + d, n)
        copies.append(det_send(pairs.at[to], parts.at[chip], q0.at[d], q1.at[d], to * 2 + core))
        copies[-1].start()
    parts[chip] = pairs[chip]
    for copy in copies:
        copy.wait()
    total = parts[0].astype(F32)
    for c in range(1, n):
        total = total + parts[c].astype(F32)
    total_ref[...] = total
    for k in range(0, tiles, 2):
        rows = total_ref[4 * k : 4 * k + 8]
        high = rows.astype(BF16)
        low = (rows - high.astype(F32)).astype(BF16)
        terms[4 * k : 4 * k + 8] = pair_products(high, along_ref, k, True) + pair_products(
            low, along_ref, k, True
        )
    leave[...] = split_dot(pick_ref[...], terms[...], COLS_COLS).reshape(obs, CAP * MP, LANES)
    start, wait = obs_copies(obs, leave, recv2, s0, s1)
    start()
    wait()
    flat = recv2[...].reshape(obs * CAP * MP, LANES)
    full[me] = split_dot(own_ref[...], flat, COLS_COLS).astype(BF16)
    det_gather(det, full, sems[4:])
    for i in range(held // 4):
        rhs = full[:, 16 * i : 16 * i + 16, :].reshape(det * 16, LANES)
        got = jnp.dot(sel_ref[...], rhs, preferred_element_type=F32)
        sky_ref[4 * i : 4 * i + 4] = got.reshape(4, rows_all, LANES)
    for copy in swaps:
        copy.wait_send()
    for started, copy in sends:

        @pl.when(started)
        def _():
            copy.wait_send()

    for copy in lefts:
        copy.wait_send()

    @pl.when(jnp.logical_not(mine))
    def _():
        for c in range(2):
            column(0, c).wait_send()

    if relayed:
        over(0).wait_send()
        y_onward.wait_send()

        @pl.when(core == from_side)
        def _():
            for source in range(2):
                onward(source).wait_send()

    for d in range(1, across):
        sideways(d).wait_send()
    for step in range(1, down // 2 + 1):
        for way in (1, -1):
            ring(way, step).wait_send()


def call(kernel, out, scratch, name, collective=None):
    if collective is None:
        params = pltpu.CompilerParams(vmem_limit_bytes=56 * 2**20)
    else:
        params = pltpu.CompilerParams(
            vmem_limit_bytes=56 * 2**20, collective_id=collective, has_side_effects=True
        )

    def run(*args):
        return pl.pallas_call(
            kernel,
            out_shape=out,
            in_specs=[VMEM] * len(args),
            out_specs=VMEM if not isinstance(out, tuple) else (VMEM,) * len(out),
            scratch_shapes=scratch,
            compiler_params=params,
            name=name,
        )(*args)

    return run


def dma(n):
    return [pltpu.SemaphoreType.DMA((n,))] * 2


def local(sky, tile_list, along, detector_kernel, sample_weight, noise_inverse):
    obs, det = lax.axis_size("obs"), lax.axis_size("det")
    held, tiles = sky.shape[0], tile_list.shape[1]
    dets, all_dets = detector_kernel.shape[0], noise_inverse.shape[2]
    rows_all = sky.shape[1] * sky.shape[2]
    mine = rows_all // det
    fwd, inv, tw, edge, ends = tables(det)

    expand = np.zeros((rows_all, 4, det, 4, MP), np.float32)
    for q in range(4):
        for j in range(det):
            for m in range(mine):
                expand[j * mine + m, q, j, q, m] = 1
    expand = jnp.asarray(expand.reshape(rows_all, -1), BF16)
    sel = np.zeros((4, det, mine, det, 4, MP), np.float32)
    for q in range(4):
        for j in range(det):
            for m in range(mine):
                sel[q, j, m, j, q, m] = 1
    sel = jnp.asarray(sel.reshape(4 * rows_all, det * 16), BF16)

    block = along[0]
    n, half, per = det // 2, det // 4, obs // det
    down = 8 if obs == 32 else obs // 2
    grid = (obs // down, down)
    mine, part = noise_inverse.shape[1], all_dets // 2
    member = jax.ShapeDtypeStruct((n, dets, 2 * FAST), BF16)
    slots = jax.ShapeDtypeStruct((obs, CAP * MP, LANES), F32)
    slot_buffer = pltpu.VMEM(slots.shape, F32)
    row_buffer = pltpu.VMEM((tiles * MP, LANES), F32)
    pieces = pltpu.VMEM((n, tiles * MP, LANES), BF16)
    edge_rows = pltpu.VMEM((8 * det, LANES), F32)
    mixed = pltpu.VMEM((2, half, dets, 2 * FAST), BF16)
    normal = call(
        functools.partial(normal_kernel, obs, det, grid),
        jax.ShapeDtypeStruct((held, rows_all, LANES), F32),
        [
            slot_buffer,
            pltpu.VMEM((obs * CAP * MP, held * MP), BF16),
            pltpu.VMEM((tiles * MP, obs * CAP * MP), BF16),
            pltpu.VMEM((held * MP, held * rows_all), BF16),
            pltpu.VMEM((4 * dets, det * 16), BF16),
            pltpu.VMEM(member.shape, BF16),
            slot_buffer,
            pltpu.VMEM((*grid, mine, part), BF16),
            slot_buffer,
            pltpu.VMEM((tiles * MP, LANES), BF16),
            pltpu.VMEM((det, tiles * MP, LANES), BF16),
            pltpu.VMEM((mine, all_dets), BF16),
            pltpu.VMEM((mine, part), BF16),
            pltpu.VMEM((tiles, dets, LANES), F32),
            pltpu.VMEM((det, dets, FAST), BF16),
            pltpu.VMEM((det, dets, FAST), F32),
            edge_rows,
            edge_rows,
            edge_rows,
            pltpu.VMEM((64, LANES), BF16),
            pltpu.VMEM((obs, 64, LANES), BF16),
            pltpu.VMEM((obs * 64, LANES), F32),
            slot_buffer,
            pltpu.VMEM(member.shape, BF16),
            mixed,
            mixed,
            pltpu.VMEM((2, half, 2, dets // 2, 2 * FAST), BF16),
            pltpu.VMEM(member.shape, BF16),
            pltpu.VMEM((det, per, CAP * MP, LANES), F32),
            pltpu.VMEM((det, dets, FAST), BF16),
            pltpu.VMEM((2, 8 * det, LANES), F32),
            pltpu.VMEM((n, 2, tiles * MP, LANES), BF16),
            pieces,
            pieces,
            pieces,
            row_buffer,
            row_buffer,
            slot_buffer,
            slot_buffer,
            pltpu.VMEM((det, held * MP, LANES), BF16),
            pltpu.VMEM((2, dets // 2, 2 * FAST), BF16),
            pltpu.VMEM((dets // 2, 2 * FAST), BF16),
            *dma(obs),
            *dma(2),
            *dma(grid[0]),
            *[pltpu.SemaphoreType.DMA((2, down // 2))] * 2,
            *[pltpu.SemaphoreType.DMA((n, 2))] * 2,
            *dma(det),
            *dma(obs),
            *dma(obs),
            *[pltpu.SemaphoreType.DMA((2, half))] * 2,
            pltpu.SemaphoreType.DMA((2, half, 2)),
            pltpu.SemaphoreType.DMA((n, 2)),
            *dma(2),
            *dma(2),
            *dma(1),
            *dma(det),
            *dma(1),
            *dma(n),
            *dma(obs),
            *dma(n),
            *dma(n),
            *dma(n),
            *dma(n),
        ],
        "normal",
        0,
    )(
        sky.reshape(held * rows_all, LANES), tile_list, block, noise_inverse[0], detector_kernel, sample_weight,
        expand, fwd, inv, tw, edge, ends, sel,
    )
    return normal.reshape(sky.shape)


def solution(mesh):
    in_specs = (
        P("obs", None, None, None),
        P(),
        P("obs", None, None, None),
        P("det", None),
        P("det", "obs"),
        P("det", "obs", None),
    )
    out_specs = P("obs", None, None, None)
    return jax.shard_map(local, mesh=mesh, in_specs=in_specs, out_specs=out_specs, check_vma=False)
```

```python
import functools
import math

import jax
import jax.numpy as jnp
import numpy as np
from jax import lax
from jax.experimental import pallas as pl
from jax.experimental.pallas import tpu as pltpu
from jax.sharding import PartitionSpec as P

CAP = 2
MP = 4
FAST = 256
LANES = 128
MESH = pl.DeviceIdType.MESH
F32 = jnp.float32
BF16 = jnp.bfloat16
VMEM = pl.BlockSpec(memory_space=pltpu.VMEM)


def band_of(slot, det):
    return slot if slot % 2 == 0 else det - slot


def tables(slow):
    lane = np.arange(FAST)
    half, rest = lane // LANES, lane % LANES
    j, i = rest // slow, rest % slow
    w = half * LANES + i * (LANES // slow) + j
    r = np.arange(LANES)
    angle = 2 * np.pi / FAST * (w[:, None] * r[None, :] % FAST)
    c, s = np.cos(angle) / math.sqrt(FAST), np.sin(angle) / math.sqrt(FAST)
    forward = np.concatenate([c, -s], 1)
    keep = (r > 0)[:, None]
    inverse = np.concatenate([c.T * keep, -s.T * keep], 0)
    twist = 2 * np.pi / (slow * FAST) * (np.arange(slow)[:, None] * r[None, :])
    tw = np.stack([np.cos(twist), np.sin(twist)], 1) / math.sqrt(slow)
    edge = np.zeros((slow, 8, slow, 8))
    for slot in range(slow):
        for v in range(2):
            turn = 2 * np.pi / slow * (band_of(slot, slow) + v / 2) * np.arange(slow)
            edge[slot, 2 * v, :, v] = np.cos(turn) / math.sqrt(slow)
            edge[slot, 2 * v + 1, :, v] = -np.sin(turn) / math.sqrt(slow)
    ends = np.zeros((8, FAST))
    ends[0] = 1 / math.sqrt(FAST)
    ends[1] = (1 - 2 * (w % 2)) / math.sqrt(FAST)
    return (
        jnp.asarray(forward, BF16),
        jnp.asarray(inverse, BF16),
        jnp.asarray(tw, F32),
        jnp.asarray(edge.reshape(8 * slow, 8 * slow), BF16),
        jnp.asarray(ends, BF16),
    )


def small_dft(re, im, sign):
    n = len(re)
    if n == 1:
        return re, im
    er, ei = small_dft(re[0::2], im[0::2], sign)
    odr, odi = small_dft(re[1::2], im[1::2], sign)
    outr, outi = [None] * n, [None] * n
    for k in range(n // 2):
        if k == 0:
            tr, ti = odr[0], odi[0]
        elif 4 * k == n:
            tr, ti = (-odi[k], odr[k]) if sign > 0 else (odi[k], -odr[k])
        else:
            c = math.cos(2 * math.pi * k / n)
            s = sign * math.sin(2 * math.pi * k / n)
            if 8 * k == n:
                tr, ti = (
                    c * (odr[k] - sign * odi[k]),
                    c * (odi[k] + sign * odr[k]),
                )
            else:
                tr, ti = c * odr[k] - s * odi[k], c * odi[k] + s * odr[k]
        outr[k], outi[k] = er[k] + tr, ei[k] + ti
        outr[k + n // 2], outi[k + n // 2] = er[k] - tr, ei[k] - ti
    return outr, outi


def digit_swap(tiles):
    n = len(tiles)
    tiles = list(tiles)
    lane = lax.broadcasted_iota(jnp.int32, tiles[0].shape, 1)
    step = 1
    while step < n:
        odd = (lane // step) % 2 == 1
        for i in range(n):
            if i & step:
                continue
            a, b = tiles[i], tiles[i | step]
            tiles[i] = jnp.where(odd, pltpu.roll(b, step, 1), a)
            tiles[i | step] = jnp.where(odd, b, pltpu.roll(a, LANES - step, 1))
        step *= 2
    return tiles


def greet(obs, det, with_obs, det_peers, meanwhile=None):
    barrier = pltpu.get_barrier_semaphore()
    count = 0
    if with_obs:
        me = lax.axis_index("obs")

        def signal(d, carry):
            pl.semaphore_signal(
                barrier, inc=1, device_id={"obs": lax.rem(me + d, obs)}, device_id_type=MESH
            )
            return carry

        lax.fori_loop(1, obs, signal, 0)
        count += obs - 1
    for peer in det_peers:
        pl.semaphore_signal(barrier, inc=1, device_id={"det": peer}, device_id_type=MESH)
    count += len(det_peers)
    if meanwhile is not None:
        meanwhile()
    pl.semaphore_wait(barrier, count)


def same_core(det):
    me = lax.axis_index("det")
    others = [lax.rem(me + 2 * d, det) for d in range(1, det // 2)]
    partner = me + 1 - 2 * lax.rem(me, 2)
    return others, partner


def obs_copies(obs, src, dst, send_sem, recv_sem, same=False):
    me = lax.axis_index("obs")

    def copy(d):
        to = lax.rem(me + d, obs)
        return pltpu.make_async_remote_copy(
            src_ref=src if same else src.at[to],
            dst_ref=dst.at[me],
            send_sem=send_sem.at[d],
            recv_sem=recv_sem.at[d],
            device_id={"obs": to},
            device_id_type=MESH,
        )

    def start():
        def step(d, carry):
            copy(d).start()
            return carry

        lax.fori_loop(1, obs, step, 0)
        dst[me] = src[...] if same else src[me]

    def wait():
        def step(d, carry):
            copy(d).wait()
            return carry

        lax.fori_loop(1, obs, step, 0)

    return start, wait


def det_send(src, dst, send_sem, recv_sem, to):
    return pltpu.make_async_remote_copy(
        src_ref=src,
        dst_ref=dst,
        send_sem=send_sem,
        recv_sem=recv_sem,
        device_id={"det": to},
        device_id_type=MESH,
    )


def far_first(n):
    return sorted(range(n), key=lambda d: -min(d, n - d))


def det_gather(det, full, sems, sent=lambda: None):
    send_sem, recv_sem, pass_send, pass_recv = sems
    me = lax.axis_index("det")
    others, partner = same_core(det)

    def copy(slot, to, a, b):
        return pltpu.make_async_remote_copy(
            src_ref=full.at[slot],
            dst_ref=full.at[slot],
            send_sem=a,
            recv_sem=b,
            device_id={"det": to},
            device_id_type=MESH,
        )

    n = det // 2
    far = n // 2
    handed = n >= 4
    order = [d for d in far_first(n)[:-1] if d != far or not handed]
    outs = []
    for d in order:
        outs.append(copy(me, others[d - 1], send_sem.at[d], recv_sem.at[d]))
        outs[-1].start()
    outs.append(copy(me, partner, pass_send.at[0], pass_recv.at[0]))
    outs[-1].start()
    sent()
    for d in order[::-1] + ([far] if handed else []):
        source = lax.rem(me + det - 2 * d, det)
        copy(source, me, send_sem.at[d], recv_sem.at[d]).wait_recv()
        if handed and d == n - far + 1:
            outs.append(copy(source, others[n - 2], send_sem.at[far], recv_sem.at[far]))
            outs[-1].start()
        outs.append(copy(source, partner, pass_send.at[d], pass_recv.at[d]))
        outs[-1].start()
    for d in range(n):
        source = lax.rem(partner + det - 2 * d, det)
        copy(source, partner, pass_send.at[d], pass_recv.at[d]).wait_recv()
    for out in outs:
        out.wait_send()


def pair_products(rows, along, k, transposed):
    dims = (((1,), (1 if transposed else 0,)), ((), ()))
    first = lax.dot_general(rows, along[k], dims, preferred_element_type=F32)
    second = lax.dot_general(rows, along[k + 1], dims, preferred_element_type=F32)
    index = lax.broadcasted_iota(jnp.int32, first.shape, 0)
    return jnp.where(index < MP, first, second)


def split_dot(exact, x, dims):
    high = x.astype(BF16)
    low = (x - high.astype(F32)).astype(BF16)
    dot = functools.partial(lax.dot_general, dimension_numbers=dims, preferred_element_type=F32)
    return dot(exact, high) + dot(exact, low)


ROWS_COLS = (((1,), (0,)), ((), ()))
COLS_COLS = (((0,), (0,)), ((), ()))


def place(slot_band, b):
    slot = slot_band.index(b)
    return slot // 2, (slot % 2) * FAST


def all_det(det):
    me = lax.axis_index("det")
    return [lax.rem(me + d, det) for d in range(1, det)]


def iota(shape, dim):
    return lax.broadcasted_iota(jnp.int32, shape, dim)


def selections(obs, list_ref, own, pick, mine_sel, mine, rows_all, held):
    me, block = lax.axis_index("det"), lax.axis_index("obs")
    tiles = list_ref.shape[1]
    listed = list_ref[...]
    owner = lax.div(listed, jnp.full_like(listed, held))
    place_in = iota(listed.shape, 1).astype(F32)
    hit = owner == block
    inside = (listed - block * held + 1).astype(F32)
    low = jnp.min(jnp.where(hit, place_in, F32(tiles)), 1, keepdims=True)
    high = jnp.max(jnp.where(hit, place_in, F32(-1)), 1, keepdims=True)
    first = jnp.where(hit & (place_in == low), inside, 0.0)
    second = jnp.where(hit & (place_in == high) & (high > low), inside, 0.0)
    size = obs * CAP * MP
    wanted = jnp.full((size, LANES), -1.0, F32)
    for s, found in enumerate((first, second)):
        value = jnp.broadcast_to(jnp.sum(found, 1, keepdims=True), (obs, LANES)).astype(BF16)
        row, col = iota((size, obs), 0), iota((size, obs), 1)
        spread = (col == row // (CAP * MP)) & ((row // MP) % CAP == s)
        wanted = wanted + jnp.dot(spread.astype(F32).astype(BF16), value, preferred_element_type=F32)
    wide = (size, held * MP)
    goal = wanted[:, : held * MP] * MP + (iota(wide, 0) % MP).astype(F32)
    ok = (wanted[:, : held * MP] >= 0) & (goal == iota(wide, 1).astype(F32))
    own[...] = ok.astype(F32).astype(BF16)
    wide = (held * MP, held * rows_all)
    row, col = iota(wide, 0), iota(wide, 1)
    ok = (col == (row // MP) * rows_all + me * mine + row % MP) & (row % MP < mine)
    mine_sel[...] = ok.astype(F32).astype(BF16)
    owner = owner.astype(F32)
    here = iota((obs, LANES), 0) == block
    down = lax.dot_general(
        owner.astype(BF16), here.astype(F32).astype(BF16), COLS_COLS, preferred_element_type=F32
    )
    along_row = jnp.sum(jnp.where(iota(listed.shape, 0) == block, owner, 0.0), 0, keepdims=True)
    square = (tiles, tiles)
    before = (down[:, :tiles] == along_row) & (iota(square, 1) < iota(square, 0))
    rank = jnp.sum(before.astype(F32), 1, keepdims=True)
    slot = (down * CAP + rank).astype(BF16)
    tall = (tiles * MP, tiles)
    spread = (iota(tall, 1) == iota(tall, 0) // MP).astype(F32).astype(BF16)
    slot = jnp.dot(spread, slot, preferred_element_type=F32)
    wide = (tiles * MP, size)
    goal = jnp.broadcast_to(slot[:, :1], wide) * MP + (iota(wide, 0) % MP).astype(F32)
    pick[...] = (goal == iota(wide, 1).astype(F32)).astype(F32).astype(BF16)


def normal_kernel(
    obs, det, grid, sky_in, list_ref, along_ref, noise_ref, kernel_ref, w_ref,
    expand_ref, fwd_ref, inv_ref, tw_ref, edge_ref, ends_ref, sel_ref, sky_ref,
    out_ref, own_ref, pick_ref, mine_sel, ke_ref, x_out, zz, m_out,
    recv, fetched, scan, nrows, other, ts, u, spun, sums, e, es, payload, gathered, wide, zs, x,
    given, taken, staged, y_ref, eb_ref, turned, esums, g_ref, pre, pairs, parts, total_ref, terms, leave, recv2, full, by_x, by_y,
    k0, k1, n0, n1, m0, m1, r0, r1, xs0, xs1, es0, es1, gs0, gs1, zs0, zs1,
    ps0, ps1, ys0, ys1, vx0, vx1, wx0, vy0, vy1, wy0, fs0, fs1, g0, g1, q0, q1, s0, s1, *sems,
):
    me, block = lax.axis_index("det"), lax.axis_index("obs")
    across, down = grid
    bx, by = block // down, lax.rem(block, down)
    n = det // 2
    chip, core, side = me // 2, lax.rem(me, 2), me // n
    partner = me + 1 - 2 * core
    dets, tiles = w_ref.shape[0], along_ref.shape[0]
    width = noise_ref.shape[0]
    held, rows_all = sky_ref.shape[0], sky_ref.shape[1]
    bands = [band_of(slot, det) for slot in range(det)]
    slow = det
    peers = all_det(det)

    def prepare():
        selections(obs, list_ref, own_ref, pick_ref, mine_sel, rows_all // det, rows_all, held)
        my_rows = jnp.dot(mine_sel[...], sky_in[...], preferred_element_type=F32).astype(BF16)
        got = jnp.dot(own_ref[...], my_rows, preferred_element_type=F32)
        out_ref[...] = got.reshape(obs, CAP * MP, LANES)

    greet(obs, det, True, peers, prepare)

    sky_start, sky_wait = obs_copies(obs, out_ref, recv, k0, k1)
    sky_start()
    part = noise_ref.shape[1] // 2
    whole = det_send(noise_ref, nrows, n0.at[0], n1.at[0], lax.rem(2 * det - me, det))
    left = det_send(noise_ref.at[:, :part], other, n0.at[1], n1.at[1], det - 1 - me)
    right = det_send(noise_ref.at[:, part:], other, n0.at[1], n1.at[1], lax.rem(me + 1, det))

    @pl.when(core == 1)
    def _():
        whole.start()
        left.start()
        left.wait_send()
        whole.wait()

    @pl.when(core == 0)
    def _():
        right.start()
        nrows[...] = noise_ref[...]
        right.wait_send()

    left.wait_recv()
    both = jnp.where(core == 1, nrows[:, part:].astype(F32), nrows[:, :part].astype(F32))
    m_out[bx, by] = (both + other[...].astype(F32)).astype(BF16)

    def sideways(d):
        to = lax.rem(bx + d, across)
        return pltpu.make_async_remote_copy(
            src_ref=m_out.at[bx, by],
            dst_ref=m_out.at[bx, by],
            send_sem=m0.at[d],
            recv_sem=m1.at[d],
            device_id={"obs": to * down + by},
            device_id_type=MESH,
        )

    def ring(way, step):
        origin = lax.rem(by + down - way * (step - 1), down)
        cut = slice(None)
        if 2 * step == down:
            cut = slice(0, across // 2) if way > 0 else slice(across // 2, across)
        at = 0 if way > 0 else 1
        return pltpu.make_async_remote_copy(
            src_ref=m_out.at[cut, origin],
            dst_ref=m_out.at[cut, origin],
            send_sem=r0.at[at, step - 1],
            recv_sem=r1.at[at, step - 1],
            device_id={"obs": bx * down + lax.rem(by + down + way, down)},
            device_id_type=MESH,
        )

    def turn(step):
        for way in (1, -1):
            if step == 1:
                if way == 1:
                    for d in range(1, across):
                        sideways(d).wait_recv()
            else:
                ring(way, step - 1).wait_recv()
            if 2 * step <= down:
                ring(way, step).start()

    steps = iter(range(1, down // 2 + 2))

    def advance():
        step = next(steps, None)
        if step is not None:
            turn(step)

    for d in range(1, across):
        sideways(d).start()

    for q in range(4):
        cut = expand_ref[:, q * det * 16 : (q + 1) * det * 16]
        ke_ref[q * dets : (q + 1) * dets] = lax.dot_general(
            kernel_ref[...], cut, COLS_COLS, preferred_element_type=F32
        ).astype(BF16)

    sky_wait()
    flat = recv[...].reshape(obs * CAP * MP, LANES).astype(BF16)
    fetched[...] = jnp.dot(pick_ref[...], flat, preferred_element_type=F32).astype(BF16)
    for k in range(0, tiles, 4):
        part_rows = fetched[4 * k : 4 * k + 16]
        low = pair_products(part_rows[:8], along_ref, k, False)
        high = pair_products(part_rows[8:], along_ref, k + 2, False)
        scan[me, 4 * k : 4 * k + 16] = jnp.concatenate([low, high], 0).astype(BF16)
    det_gather(det, scan, sems[:4], advance)

    chunk = dets // 2
    cuts = [slice(c * chunk, (c + 1) * chunk) for c in range(2)]
    far = n // 2
    relayed = n >= 4
    slot = lax.rem(me, n)
    back_chip = lax.rem(chip + n - 1, n)
    from_chip = lax.rem(chip + 1, n)
    from_side = from_chip // far
    final_chip = lax.rem(from_chip + far, n)
    mine = core == side
    lefts = []

    def column(d, c):
        to = lax.rem(chip + d, n)
        return det_send(
            x.at[to, cuts[c]], x_out.at[slot, cuts[c]], xs0.at[d, c], xs1.at[slot, c], to * 2 + side
        )

    def over(source):
        to = back_chip * 2 + side
        return det_send(x.at[lax.rem(chip + far, n), cuts[0]], by_x.at[source], vx0.at[0], vx1.at[source], to)

    def onward(source):
        at = lax.rem(from_chip * 2 + source, n)
        return det_send(
            by_x.at[source], x_out.at[at, cuts[0]], wx0.at[source], xs1.at[at, 0], final_chip * 2 + from_side
        )

    def timestream(c):
        for i in range(tiles // 4):
            rhs = scan[:, 16 * i : 16 * i + 16, :].reshape(det * 16, LANES)
            lhs = [ke_ref[q * dets + c * chunk : q * dets + (c + 1) * chunk] for q in range(4)]
            got = jnp.dot(jnp.concatenate(lhs, 0), rhs, preferred_element_type=F32)
            for q in range(4):
                k = 4 * i + q
                weight = w_ref[cuts[c], k * LANES : (k + 1) * LANES].astype(F32)
                ts[k, cuts[c]] = got[q * chunk : (q + 1) * chunk] * weight
        for h in range(2):

            def swap(g, carry):
                at = pl.ds(pl.multiple_of(c * chunk + g * 16, 16), 16)
                out = digit_swap([ts[h * det + i, at, :] for i in range(det)])
                for z in range(det):
                    u[z, at, h * LANES : (h + 1) * LANES] = out[z].astype(BF16)
                return carry

            lax.fori_loop(0, chunk // 16, swap, 0)

    def transform(c):
        def fast(z, carry):
            a = jnp.dot(u[z, cuts[c]], fwd_ref[...], preferred_element_type=F32)
            re, im = a[:, :LANES], a[:, LANES:]
            cs, sn = tw_ref[z, 0:1, :], tw_ref[z, 1:2, :]
            spun[z, cuts[c], :LANES] = re * cs + im * sn
            spun[z, cuts[c], LANES:] = im * cs - re * sn
            return carry

        lax.fori_loop(0, det, fast, 0)

        def last(g, carry):
            at = pl.ds(pl.multiple_of(c * chunk + g * 16, 16), 16)
            re = [spun[z, at, :LANES] for z in range(det)]
            im = [spun[z, at, LANES:] for z in range(det)]
            re, im = small_dft(re, im, -1)
            for b in range(det):
                to, lo = place(bands, b)
                x[to, at, lo : lo + LANES] = re[b].astype(BF16)
                x[to, at, lo + LANES : lo + FAST] = im[b].astype(BF16)
            return carry

        lax.fori_loop(0, chunk // 16, last, 0)

    def send_columns(c):
        for d in far_first(n)[:-1]:
            if relayed and c == 0 and d == far:
                for source in range(2):

                    @pl.when(core == source)
                    def _():
                        over(source).start()
            else:
                column(d, c).start()
                lefts.append(column(d, c))

        @pl.when(mine)
        def _():
            x_out[slot, cuts[c]] = x[chip, cuts[c]]

        @pl.when(jnp.logical_not(mine))
        def _():
            column(0, c).start()

    advance()
    timestream(0)
    transform(0)
    send_columns(0)
    timestream(1)
    advance()

    sums[...] = jnp.zeros_like(sums)

    def ends(z, carry):
        sums[pl.ds(pl.multiple_of(z * 8, 8), 8), :dets] = lax.dot_general(
            ends_ref[...], u[z], (((1,), (1,)), ((), ())), preferred_element_type=F32
        )
        return carry

    transform(1)
    send_columns(1)
    if relayed:

        @pl.when(core == from_side)
        def _():
            for source in range(2):
                det_send(by_x.at[source], by_x.at[source], vx0.at[0], vx1.at[source], me).wait_recv()
                onward(source).start()

    lax.fori_loop(0, det, ends, 0)
    e[...] = split_dot(edge_ref[...], sums[...], ROWS_COLS)
    own = pl.ds(pl.multiple_of(me * 8, 8), 8)
    edges = []
    for d in range(1, det):
        to = peers[d - 1]
        edges.append(
            det_send(e.at[pl.ds(pl.multiple_of(to * 8, 8), 8)], es.at[own], es0.at[d], es1.at[d], to)
        )
        edges[-1].start()
    es[own, :] = e[own, :]
    advance()
    for copy in edges:
        copy.wait()
    for i in range(4):
        payload[16 * i : 16 * i + det] = es[pl.ds(i, det, stride=8), :].astype(BF16)
    give_start, give_wait = obs_copies(obs, payload, gathered, gs0, gs1, True)
    for step in steps:
        turn(step)
    give_start()
    for i in range(n):

        @pl.when(core * n + i != me)
        def _():
            for c in range(2):
                det_send(
                    x_out.at[i, cuts[c]], x_out.at[i, cuts[c]], xs0.at[0, c], xs1.at[i, c], me
                ).wait_recv()

    hn = n // 2
    swaps, sends = [], []

    def product(to_chip, c):
        blocks = [to_chip * 4 + 2 * i + c for i in range(2)]
        rows = jnp.concatenate([m_out[at // down, lax.rem(at, down)] for at in blocks], 0)
        return jnp.dot(rows, x_out[...].reshape(n * dets, 2 * FAST), preferred_element_type=F32)

    def finish(c, s, total):
        to_chip = core * hn + lax.rem(chip + s, hn)
        swaps[c * hn + s].wait_recv()
        total = total + taken[c, s].astype(F32)
        for i in range(2):
            to = to_chip * 2 + i
            staged[c, s, i] = total[i * chunk : (i + 1) * chunk].astype(BF16)
            copy = det_send(
                staged.at[c, s, i], y_ref.at[chip, cuts[c]], ys0.at[c, s, i], ys1.at[chip, c], to
            )
            direct = to != me
            if relayed and c == 0 and s == 0:
                direct = direct & mine
                around = det_send(
                    staged.at[c, s, i], by_y, vy0.at[i], vy1.at[0], back_chip * 2 + i
                )

                @pl.when(jnp.logical_not(mine))
                def _():
                    around.start()

                sends.append((jnp.logical_not(mine), around))

            @pl.when(direct)
            def _():
                copy.start()

            @pl.when(to == me)
            def _():
                y_ref[chip, cuts[c]] = staged[c, s, i]

            sends.append((direct, copy))

    before = None
    for c in range(2):
        for s in range(hn):
            near = lax.rem(chip + s, hn)
            given[c, s] = product((1 - core) * hn + near, c).astype(BF16)
            swaps.append(
                det_send(given.at[c, s], taken.at[c, s], ps0.at[c, s], ps1.at[c, s], partner)
            )
            swaps[-1].start()
            total = product(core * hn + near, c)
            if before is not None:
                finish(*before)
            before = (c, s, total)
    finish(*before)
    y_onward = det_send(
        by_y, y_ref.at[from_chip, cuts[0]], wy0.at[0], ys1.at[from_chip, 0], final_chip * 2 + core
    )
    if relayed:
        det_send(by_y, by_y, vy0.at[0], vy1.at[0], me).wait_recv()
        y_onward.start()

    give_wait()
    wide[...] = gathered[...].reshape(obs * 64, LANES).astype(F32)
    prod = jnp.zeros((obs * 4, width), F32)
    for j in range(det):
        lhs = wide[pl.ds(j, obs * 4, stride=16), :dets].astype(BF16)
        rhs = nrows[:, j * dets : (j + 1) * dets]
        prod = prod + lax.dot_general(lhs, rhs, (((1,), (1,)), ((), ())), preferred_element_type=F32)
    zs[...] = jnp.zeros_like(zs)
    for p in range(obs):
        zs[p, 0:4, :width] = prod[4 * p : 4 * p + 4]
    z_start, z_wait = obs_copies(obs, zs, zz, zs0, zs1)
    z_start()
    z_wait()
    per = obs // det
    finals = []
    for d in range(1, det):
        to = peers[d - 1]
        finals.append(det_send(zz.at[pl.ds(to * per, per)], eb_ref.at[me], fs0.at[d], fs1.at[d], to))
        finals[-1].start()
    eb_ref[me] = zz[pl.ds(me * per, per)]

    for copy in finals:
        copy.wait()
    for q in range(2):
        rows = eb_ref[:, q].reshape(8 * slow, LANES)
        esums[q] = split_dot(edge_ref[...], rows, COLS_COLS).astype(BF16).astype(F32)

    def inverse(c):
        for i in range(n):

            @pl.when(i * 2 + side != me)
            def _():
                det_send(
                    y_ref.at[i, cuts[c]], y_ref.at[i, cuts[c]], ys0.at[0, 0, 0], ys1.at[i, c], me
                ).wait_recv()

        def first(g, carry):
            at = pl.ds(pl.multiple_of(c * chunk + g * 16, 16), 16)
            re, im = [], []
            for b in range(slow):
                to, lo = place(bands, b)
                re.append(y_ref[to, at, lo : lo + LANES].astype(F32))
                im.append(y_ref[to, at, lo + LANES : lo + FAST].astype(F32))
            re, im = small_dft(re, im, 1)
            for z in range(slow):
                cs, sn = tw_ref[z, 0:1, :], tw_ref[z, 1:2, :]
                turned[z, at, :LANES] = (re[z] * cs - im[z] * sn).astype(BF16)
                turned[z, at, LANES:] = (im[z] * cs + re[z] * sn).astype(BF16)
            return carry

        lax.fori_loop(0, chunk // 16, first, 0)

        def fast(z, carry):
            at = pl.ds(pl.multiple_of(z * 8, 8), 8)
            o = jnp.dot(turned[z, cuts[c]], inv_ref[...], preferred_element_type=F32)
            o = o + lax.dot_general(
                esums[c, at, :].astype(BF16), ends_ref[...], COLS_COLS, preferred_element_type=F32
            )[:chunk]
            ts[z, cuts[c]] = o[:, :LANES]
            ts[slow + z, cuts[c]] = o[:, LANES:]
            return carry

        lax.fori_loop(0, slow, fast, 0)
        for h in range(2):

            def swap(g, carry):
                at = pl.ds(pl.multiple_of(c * chunk + g * 16, 16), 16)
                out = digit_swap([ts[h * slow + z, at, :] for z in range(slow)])
                for i in range(slow):
                    ts[h * slow + i, at, :] = out[i]
                return carry

            lax.fori_loop(0, chunk // 16, swap, 0)

    inverse(0)
    inverse(1)
    for i in range(tiles // 4):
        filtered = [
            (ts[k] * w_ref[:, k * LANES : (k + 1) * LANES].astype(F32)).astype(BF16)
            for k in range(4 * i, 4 * i + 4)
        ]
        rows = lax.dot_general(
            ke_ref[...], jnp.concatenate(filtered, 0), COLS_COLS, preferred_element_type=F32
        )
        g_ref[:, :, 16 * i : 16 * i + 16, :] = rows.reshape(n, 2, 16, LANES).astype(BF16)

    swap_pairs = det_send(g_ref.at[:, 1 - core], pre, g0.at[0], g1.at[0], partner)
    swap_pairs.start()
    swap_pairs.wait()
    for c in range(n):
        pairs[c] = (g_ref[c, core].astype(F32) + pre[c].astype(F32)).astype(BF16)
    copies = []
    for d in far_first(n)[:-1]:
        to = lax.rem(chip + d, n)
        copies.append(det_send(pairs.at[to], parts.at[chip], q0.at[d], q1.at[d], to * 2 + core))
        copies[-1].start()
    parts[chip] = pairs[chip]
    for copy in copies:
        copy.wait()
    total = parts[0].astype(F32)
    for c in range(1, n):
        total = total + parts[c].astype(F32)
    total_ref[...] = total
    for k in range(0, tiles, 2):
        rows = total_ref[4 * k : 4 * k + 8]
        high = rows.astype(BF16)
        low = (rows - high.astype(F32)).astype(BF16)
        terms[4 * k : 4 * k + 8] = pair_products(high, along_ref, k, True) + pair_products(
            low, along_ref, k, True
        )
    leave[...] = split_dot(pick_ref[...], terms[...], COLS_COLS).reshape(obs, CAP * MP, LANES)
    start, wait = obs_copies(obs, leave, recv2, s0, s1)
    start()
    wait()
    flat = recv2[...].reshape(obs * CAP * MP, LANES)
    full[me] = split_dot(own_ref[...], flat, COLS_COLS).astype(BF16)
    det_gather(det, full, sems[4:])
    for i in range(held // 4):
        rhs = full[:, 16 * i : 16 * i + 16, :].reshape(det * 16, LANES)
        got = jnp.dot(sel_ref[...], rhs, preferred_element_type=F32)
        sky_ref[4 * i : 4 * i + 4] = got.reshape(4, rows_all, LANES)
    for copy in swaps:
        copy.wait_send()
    for started, copy in sends:

        @pl.when(started)
        def _():
            copy.wait_send()

    for copy in lefts:
        copy.wait_send()

    @pl.when(jnp.logical_not(mine))
    def _():
        for c in range(2):
            column(0, c).wait_send()

    if relayed:
        over(0).wait_send()
        y_onward.wait_send()

        @pl.when(core == from_side)
        def _():
            for source in range(2):
                onward(source).wait_send()

    for d in range(1, across):
        sideways(d).wait_send()
    for step in range(1, down // 2 + 1):
        for way in (1, -1):
            ring(way, step).wait_send()


def call(kernel, out, scratch, name, collective=None):
    if collective is None:
        params = pltpu.CompilerParams(vmem_limit_bytes=56 * 2**20)
    else:
        params = pltpu.CompilerParams(
            vmem_limit_bytes=56 * 2**20, collective_id=collective, has_side_effects=True
        )

    def run(*args):
        return pl.pallas_call(
            kernel,
            out_shape=out,
            in_specs=[VMEM] * len(args),
            out_specs=VMEM if not isinstance(out, tuple) else (VMEM,) * len(out),
            scratch_shapes=scratch,
            compiler_params=params,
            name=name,
        )(*args)

    return run


def dma(n):
    return [pltpu.SemaphoreType.DMA((n,))] * 2


def local(sky, tile_list, along, detector_kernel, sample_weight, noise_inverse):
    obs, det = lax.axis_size("obs"), lax.axis_size("det")
    held, tiles = sky.shape[0], tile_list.shape[1]
    dets, all_dets = detector_kernel.shape[0], noise_inverse.shape[2]
    rows_all = sky.shape[1] * sky.shape[2]
    mine = rows_all // det
    fwd, inv, tw, edge, ends = tables(det)

    expand = np.zeros((rows_all, 4, det, 4, MP), np.float32)
    for q in range(4):
        for j in range(det):
            for m in range(mine):
                expand[j * mine + m, q, j, q, m] = 1
    expand = jnp.asarray(expand.reshape(rows_all, -1), BF16)
    sel = np.zeros((4, det, mine, det, 4, MP), np.float32)
    for q in range(4):
        for j in range(det):
            for m in range(mine):
                sel[q, j, m, j, q, m] = 1
    sel = jnp.asarray(sel.reshape(4 * rows_all, det * 16), BF16)

    block = along[0]
    n, half, per = det // 2, det // 4, obs // det
    down = 8 if obs == 32 else obs // 2
    grid = (obs // down, down)
    mine, part = noise_inverse.shape[1], all_dets // 2
    member = jax.ShapeDtypeStruct((n, dets, 2 * FAST), BF16)
    slots = jax.ShapeDtypeStruct((obs, CAP * MP, LANES), F32)
    slot_buffer = pltpu.VMEM(slots.shape, F32)
    row_buffer = pltpu.VMEM((tiles * MP, LANES), F32)
    pieces = pltpu.VMEM((n, tiles * MP, LANES), BF16)
    edge_rows = pltpu.VMEM((8 * det, LANES), F32)
    mixed = pltpu.VMEM((2, half, dets, 2 * FAST), BF16)
    normal = call(
        functools.partial(normal_kernel, obs, det, grid),
        jax.ShapeDtypeStruct((held, rows_all, LANES), F32),
        [
            slot_buffer,
            pltpu.VMEM((obs * CAP * MP, held * MP), BF16),
            pltpu.VMEM((tiles * MP, obs * CAP * MP), BF16),
            pltpu.VMEM((held * MP, held * rows_all), BF16),
            pltpu.VMEM((4 * dets, det * 16), BF16),
            pltpu.VMEM(member.shape, BF16),
            slot_buffer,
            pltpu.VMEM((*grid, mine, part), BF16),
            slot_buffer,
            pltpu.VMEM((tiles * MP, LANES), BF16),
            pltpu.VMEM((det, tiles * MP, LANES), BF16),
            pltpu.VMEM((mine, all_dets), BF16),
            pltpu.VMEM((mine, part), BF16),
            pltpu.VMEM((tiles, dets, LANES), F32),
            pltpu.VMEM((det, dets, FAST), BF16),
            pltpu.VMEM((det, dets, FAST), F32),
            edge_rows,
            edge_rows,
            edge_rows,
            pltpu.VMEM((64, LANES), BF16),
            pltpu.VMEM((obs, 64, LANES), BF16),
            pltpu.VMEM((obs * 64, LANES), F32),
            slot_buffer,
            pltpu.VMEM(member.shape, BF16),
            mixed,
            mixed,
            pltpu.VMEM((2, half, 2, dets // 2, 2 * FAST), BF16),
            pltpu.VMEM(member.shape, BF16),
            pltpu.VMEM((det, per, CAP * MP, LANES), F32),
            pltpu.VMEM((det, dets, FAST), BF16),
            pltpu.VMEM((2, 8 * det, LANES), F32),
            pltpu.VMEM((n, 2, tiles * MP, LANES), BF16),
            pieces,
            pieces,
            pieces,
            row_buffer,
            row_buffer,
            slot_buffer,
            slot_buffer,
            pltpu.VMEM((det, held * MP, LANES), BF16),
            pltpu.VMEM((2, dets // 2, 2 * FAST), BF16),
            pltpu.VMEM((dets // 2, 2 * FAST), BF16),
            *dma(obs),
            *dma(2),
            *dma(grid[0]),
            *[pltpu.SemaphoreType.DMA((2, down // 2))] * 2,
            *[pltpu.SemaphoreType.DMA((n, 2))] * 2,
            *dma(det),
            *dma(obs),
            *dma(obs),
            *[pltpu.SemaphoreType.DMA((2, half))] * 2,
            pltpu.SemaphoreType.DMA((2, half, 2)),
            pltpu.SemaphoreType.DMA((n, 2)),
            *dma(2),
            *dma(2),
            *dma(1),
            *dma(det),
            *dma(1),
            *dma(n),
            *dma(obs),
            *dma(n),
            *dma(n),
            *dma(n),
            *dma(n),
        ],
        "normal",
        0,
    )(
        sky.reshape(held * rows_all, LANES), tile_list, block, noise_inverse[0], detector_kernel.T, sample_weight,
        expand, fwd, inv, tw, edge, ends, sel,
    )
    return normal.reshape(sky.shape)


def solution(mesh):
    in_specs = (
        P("obs", None, None, None),
        P(),
        P("obs", None, None, None),
        P("det", None),
        P("det", "obs"),
        P("det", "obs", None),
    )
    out_specs = P("obs", None, None, None)
    return jax.shard_map(local, mesh=mesh, in_specs=in_specs, out_specs=out_specs, check_vma=False)
```

```python
import functools
import math

import jax
import jax.numpy as jnp
import numpy as np
from jax import lax
from jax.experimental import pallas as pl
from jax.experimental.pallas import tpu as pltpu
from jax.sharding import PartitionSpec as P

CAP = 2
MP = 4
FAST = 256
LANES = 128
MESH = pl.DeviceIdType.MESH
F32 = jnp.float32
BF16 = jnp.bfloat16
VMEM = pl.BlockSpec(memory_space=pltpu.VMEM)


def band_of(slot, det):
    return slot if slot % 2 == 0 else det - slot


def tables(slow):
    lane = np.arange(FAST)
    half, rest = lane // LANES, lane % LANES
    j, i = rest // slow, rest % slow
    w = half * LANES + i * (LANES // slow) + j
    r = np.arange(LANES)
    angle = 2 * np.pi / FAST * (w[:, None] * r[None, :] % FAST)
    c, s = np.cos(angle) / math.sqrt(FAST), np.sin(angle) / math.sqrt(FAST)
    forward = np.concatenate([c, -s], 1)
    keep = (r > 0)[:, None]
    inverse = np.concatenate([c.T * keep, -s.T * keep], 0)
    twist = 2 * np.pi / (slow * FAST) * (np.arange(slow)[:, None] * r[None, :])
    tw = np.stack([np.cos(twist), np.sin(twist)], 1) / math.sqrt(slow)
    edge = np.zeros((slow, 8, slow, 8))
    for slot in range(slow):
        for v in range(2):
            turn = 2 * np.pi / slow * (band_of(slot, slow) + v / 2) * np.arange(slow)
            edge[slot, 2 * v, :, v] = np.cos(turn) / math.sqrt(slow)
            edge[slot, 2 * v + 1, :, v] = -np.sin(turn) / math.sqrt(slow)
    ends = np.zeros((8, FAST))
    ends[0] = 1 / math.sqrt(FAST)
    ends[1] = (1 - 2 * (w % 2)) / math.sqrt(FAST)
    return (
        jnp.asarray(forward, BF16),
        jnp.asarray(inverse, BF16),
        jnp.asarray(tw, F32),
        jnp.asarray(edge.reshape(8 * slow, 8 * slow), BF16),
        jnp.asarray(ends, BF16),
    )


def small_dft(re, im, sign):
    n = len(re)
    if n == 1:
        return re, im
    er, ei = small_dft(re[0::2], im[0::2], sign)
    odr, odi = small_dft(re[1::2], im[1::2], sign)
    outr, outi = [None] * n, [None] * n
    for k in range(n // 2):
        if k == 0:
            tr, ti = odr[0], odi[0]
        elif 4 * k == n:
            tr, ti = (-odi[k], odr[k]) if sign > 0 else (odi[k], -odr[k])
        else:
            c = math.cos(2 * math.pi * k / n)
            s = sign * math.sin(2 * math.pi * k / n)
            if 8 * k == n:
                tr, ti = (
                    c * (odr[k] - sign * odi[k]),
                    c * (odi[k] + sign * odr[k]),
                )
            else:
                tr, ti = c * odr[k] - s * odi[k], c * odi[k] + s * odr[k]
        outr[k], outi[k] = er[k] + tr, ei[k] + ti
        outr[k + n // 2], outi[k + n // 2] = er[k] - tr, ei[k] - ti
    return outr, outi


def digit_swap(tiles):
    n = len(tiles)
    tiles = list(tiles)
    lane = lax.broadcasted_iota(jnp.int32, tiles[0].shape, 1)
    step = 1
    while step < n:
        odd = (lane // step) % 2 == 1
        for i in range(n):
            if i & step:
                continue
            a, b = tiles[i], tiles[i | step]
            tiles[i] = jnp.where(odd, pltpu.roll(b, step, 1), a)
            tiles[i | step] = jnp.where(odd, b, pltpu.roll(a, LANES - step, 1))
        step *= 2
    return tiles


def greet(obs, det, with_obs, det_peers, meanwhile=None):
    barrier = pltpu.get_barrier_semaphore()
    count = 0
    if with_obs:
        me = lax.axis_index("obs")

        def signal(d, carry):
            pl.semaphore_signal(
                barrier, inc=1, device_id={"obs": lax.rem(me + d, obs)}, device_id_type=MESH
            )
            return carry

        lax.fori_loop(1, obs, signal, 0)
        count += obs - 1
    for peer in det_peers:
        pl.semaphore_signal(barrier, inc=1, device_id={"det": peer}, device_id_type=MESH)
    count += len(det_peers)
    if meanwhile is not None:
        meanwhile()
    pl.semaphore_wait(barrier, count)


def same_core(det):
    me = lax.axis_index("det")
    others = [lax.rem(me + 2 * d, det) for d in range(1, det // 2)]
    partner = me + 1 - 2 * lax.rem(me, 2)
    return others, partner


def obs_copies(obs, src, dst, send_sem, recv_sem, same=False):
    me = lax.axis_index("obs")

    def copy(d):
        to = lax.rem(me + d, obs)
        return pltpu.make_async_remote_copy(
            src_ref=src if same else src.at[to],
            dst_ref=dst.at[me],
            send_sem=send_sem.at[d],
            recv_sem=recv_sem.at[d],
            device_id={"obs": to},
            device_id_type=MESH,
        )

    def start():
        def step(d, carry):
            copy(d).start()
            return carry

        lax.fori_loop(1, obs, step, 0)
        dst[me] = src[...] if same else src[me]

    def wait():
        def step(d, carry):
            copy(d).wait()
            return carry

        lax.fori_loop(1, obs, step, 0)

    return start, wait


def det_send(src, dst, send_sem, recv_sem, to):
    return pltpu.make_async_remote_copy(
        src_ref=src,
        dst_ref=dst,
        send_sem=send_sem,
        recv_sem=recv_sem,
        device_id={"det": to},
        device_id_type=MESH,
    )


def far_first(n):
    return sorted(range(n), key=lambda d: -min(d, n - d))


def det_gather(det, full, sems, sent=lambda: None):
    send_sem, recv_sem, pass_send, pass_recv = sems
    me = lax.axis_index("det")
    others, partner = same_core(det)

    def copy(slot, to, a, b):
        return pltpu.make_async_remote_copy(
            src_ref=full.at[slot],
            dst_ref=full.at[slot],
            send_sem=a,
            recv_sem=b,
            device_id={"det": to},
            device_id_type=MESH,
        )

    n = det // 2
    far = n // 2
    handed = n >= 4
    order = [d for d in far_first(n)[:-1] if d != far or not handed]
    outs = []
    for d in order:
        outs.append(copy(me, others[d - 1], send_sem.at[d], recv_sem.at[d]))
        outs[-1].start()
    outs.append(copy(me, partner, pass_send.at[0], pass_recv.at[0]))
    outs[-1].start()
    sent()
    for d in order[::-1] + ([far] if handed else []):
        source = lax.rem(me + det - 2 * d, det)
        copy(source, me, send_sem.at[d], recv_sem.at[d]).wait_recv()
        if handed and d == n - far + 1:
            outs.append(copy(source, others[n - 2], send_sem.at[far], recv_sem.at[far]))
            outs[-1].start()
        outs.append(copy(source, partner, pass_send.at[d], pass_recv.at[d]))
        outs[-1].start()
    for d in range(n):
        source = lax.rem(partner + det - 2 * d, det)
        copy(source, partner, pass_send.at[d], pass_recv.at[d]).wait_recv()
    for out in outs:
        out.wait_send()


def pair_products(rows, along, k, transposed):
    dims = (((1,), (1 if transposed else 0,)), ((), ()))
    first = lax.dot_general(rows, along[k], dims, preferred_element_type=F32)
    second = lax.dot_general(rows, along[k + 1], dims, preferred_element_type=F32)
    index = lax.broadcasted_iota(jnp.int32, first.shape, 0)
    return jnp.where(index < MP, first, second)


def split_dot(exact, x, dims):
    high = x.astype(BF16)
    low = (x - high.astype(F32)).astype(BF16)
    dot = functools.partial(lax.dot_general, dimension_numbers=dims, preferred_element_type=F32)
    return dot(exact, high) + dot(exact, low)


ROWS_COLS = (((1,), (0,)), ((), ()))
COLS_COLS = (((0,), (0,)), ((), ()))


def place(slot_band, b):
    slot = slot_band.index(b)
    return slot // 2, (slot % 2) * FAST


def all_det(det):
    me = lax.axis_index("det")
    return [lax.rem(me + d, det) for d in range(1, det)]


def iota(shape, dim):
    return lax.broadcasted_iota(jnp.int32, shape, dim)


def selections(obs, list_ref, own, pick, mine_sel, mine, rows_all, held):
    me, block = lax.axis_index("det"), lax.axis_index("obs")
    tiles = list_ref.shape[1]
    listed = list_ref[...]
    owner = lax.div(listed, jnp.full_like(listed, held))
    place_in = iota(listed.shape, 1).astype(F32)
    hit = owner == block
    inside = (listed - block * held + 1).astype(F32)
    low = jnp.min(jnp.where(hit, place_in, F32(tiles)), 1, keepdims=True)
    high = jnp.max(jnp.where(hit, place_in, F32(-1)), 1, keepdims=True)
    first = jnp.where(hit & (place_in == low), inside, 0.0)
    second = jnp.where(hit & (place_in == high) & (high > low), inside, 0.0)
    size = obs * CAP * MP
    wanted = jnp.full((size, LANES), -1.0, F32)
    for s, found in enumerate((first, second)):
        value = jnp.broadcast_to(jnp.sum(found, 1, keepdims=True), (obs, LANES)).astype(BF16)
        row, col = iota((size, obs), 0), iota((size, obs), 1)
        spread = (col == row // (CAP * MP)) & ((row // MP) % CAP == s)
        wanted = wanted + jnp.dot(spread.astype(F32).astype(BF16), value, preferred_element_type=F32)
    wide = (size, held * MP)
    goal = wanted[:, : held * MP] * MP + (iota(wide, 0) % MP).astype(F32)
    ok = (wanted[:, : held * MP] >= 0) & (goal == iota(wide, 1).astype(F32))
    own[...] = ok.astype(F32).astype(BF16)
    wide = (held * MP, held * rows_all)
    row, col = iota(wide, 0), iota(wide, 1)
    ok = (col == (row // MP) * rows_all + me * mine + row % MP) & (row % MP < mine)
    mine_sel[...] = ok.astype(F32).astype(BF16)
    owner = owner.astype(F32)
    here = iota((obs, LANES), 0) == block
    down = lax.dot_general(
        owner.astype(BF16), here.astype(F32).astype(BF16), COLS_COLS, preferred_element_type=F32
    )
    along_row = jnp.sum(jnp.where(iota(listed.shape, 0) == block, owner, 0.0), 0, keepdims=True)
    square = (tiles, tiles)
    before = (down[:, :tiles] == along_row) & (iota(square, 1) < iota(square, 0))
    rank = jnp.sum(before.astype(F32), 1, keepdims=True)
    slot = (down * CAP + rank).astype(BF16)
    tall = (tiles * MP, tiles)
    spread = (iota(tall, 1) == iota(tall, 0) // MP).astype(F32).astype(BF16)
    slot = jnp.dot(spread, slot, preferred_element_type=F32)
    wide = (tiles * MP, size)
    goal = jnp.broadcast_to(slot[:, :1], wide) * MP + (iota(wide, 0) % MP).astype(F32)
    pick[...] = (goal == iota(wide, 1).astype(F32)).astype(F32).astype(BF16)


def normal_kernel(
    obs, det, grid, sky_in, list_ref, along_ref, noise_ref, kernel_ref, w_ref,
    expand_ref, fwd_ref, inv_ref, tw_ref, edge_ref, ends_ref, sel_ref, sky_ref,
    out_ref, own_ref, pick_ref, mine_sel, ke_ref, x_out, zz, m_out,
    recv, fetched, scan, nrows, other, ts, u, spun, sums, e, es, payload, gathered, wide, zs, x,
    given, taken, staged, y_ref, eb_ref, turned, esums, g_ref, pre, pairs, parts, total_ref, terms, leave, recv2, full, by_x, by_y,
    k0, k1, n0, n1, m0, m1, r0, r1, xs0, xs1, es0, es1, gs0, gs1, zs0, zs1,
    ps0, ps1, ys0, ys1, vx0, vx1, wx0, vy0, vy1, wy0, fs0, fs1, g0, g1, q0, q1, s0, s1, *sems,
):
    me, block = lax.axis_index("det"), lax.axis_index("obs")
    across, down = grid
    bx, by = block // down, lax.rem(block, down)
    n = det // 2
    chip, core, side = me // 2, lax.rem(me, 2), me // n
    partner = me + 1 - 2 * core
    dets, tiles = w_ref.shape[0], along_ref.shape[0]
    width = noise_ref.shape[0]
    held, rows_all = sky_ref.shape[0], sky_ref.shape[1]
    bands = [band_of(slot, det) for slot in range(det)]
    slow = det
    peers = all_det(det)

    def prepare():
        selections(obs, list_ref, own_ref, pick_ref, mine_sel, rows_all // det, rows_all, held)
        my_rows = jnp.dot(mine_sel[...], sky_in[...], preferred_element_type=F32).astype(BF16)
        got = jnp.dot(own_ref[...], my_rows, preferred_element_type=F32)
        out_ref[...] = got.reshape(obs, CAP * MP, LANES)

    greet(obs, det, True, peers, prepare)

    sky_start, sky_wait = obs_copies(obs, out_ref, recv, k0, k1)
    sky_start()
    part = noise_ref.shape[1] // 2
    whole = det_send(noise_ref, nrows, n0.at[0], n1.at[0], lax.rem(2 * det - me, det))
    left = det_send(noise_ref.at[:, :part], other, n0.at[1], n1.at[1], det - 1 - me)
    right = det_send(noise_ref.at[:, part:], other, n0.at[1], n1.at[1], lax.rem(me + 1, det))

    @pl.when(core == 1)
    def _():
        whole.start()
        left.start()
        left.wait_send()
        whole.wait()

    @pl.when(core == 0)
    def _():
        right.start()
        nrows[...] = noise_ref[...]
        right.wait_send()

    left.wait_recv()
    both = jnp.where(core == 1, nrows[:, part:].astype(F32), nrows[:, :part].astype(F32))
    m_out[bx, by] = (both + other[...].astype(F32)).astype(BF16)

    def sideways(d):
        to = lax.rem(bx + d, across)
        return pltpu.make_async_remote_copy(
            src_ref=m_out.at[bx, by],
            dst_ref=m_out.at[bx, by],
            send_sem=m0.at[d],
            recv_sem=m1.at[d],
            device_id={"obs": to * down + by},
            device_id_type=MESH,
        )

    def ring(way, step):
        origin = lax.rem(by + down - way * (step - 1), down)
        cut = slice(None)
        if 2 * step == down:
            cut = slice(0, across // 2) if way > 0 else slice(across // 2, across)
        at = 0 if way > 0 else 1
        return pltpu.make_async_remote_copy(
            src_ref=m_out.at[cut, origin],
            dst_ref=m_out.at[cut, origin],
            send_sem=r0.at[at, step - 1],
            recv_sem=r1.at[at, step - 1],
            device_id={"obs": bx * down + lax.rem(by + down + way, down)},
            device_id_type=MESH,
        )

    def turn(step):
        for way in (1, -1):
            if step == 1:
                if way == 1:
                    for d in range(1, across):
                        sideways(d).wait_recv()
            else:
                ring(way, step - 1).wait_recv()
            if 2 * step <= down:
                ring(way, step).start()

    steps = iter(range(1, down // 2 + 2))

    def advance():
        step = next(steps, None)
        if step is not None:
            turn(step)

    for d in range(1, across):
        sideways(d).start()

    for q in range(4):
        cut = expand_ref[:, q * det * 16 : (q + 1) * det * 16]
        ke_ref[q * dets : (q + 1) * dets] = lax.dot_general(
            kernel_ref[...], cut, COLS_COLS, preferred_element_type=F32
        ).astype(BF16)

    sky_wait()
    flat = recv[...].reshape(obs * CAP * MP, LANES).astype(BF16)
    fetched[...] = jnp.dot(pick_ref[...], flat, preferred_element_type=F32).astype(BF16)
    for k in range(0, tiles, 4):
        part_rows = fetched[4 * k : 4 * k + 16]
        low = pair_products(part_rows[:8], along_ref, k, False)
        high = pair_products(part_rows[8:], along_ref, k + 2, False)
        scan[me, 4 * k : 4 * k + 16] = jnp.concatenate([low, high], 0).astype(BF16)
    det_gather(det, scan, sems[:4], advance)

    chunk = dets // 2
    cuts = [slice(c * chunk, (c + 1) * chunk) for c in range(2)]
    far = n // 2
    relayed = n >= 4
    slot = lax.rem(me, n)
    back_chip = lax.rem(chip + n - 1, n)
    from_chip = lax.rem(chip + 1, n)
    from_side = from_chip // far
    final_chip = lax.rem(from_chip + far, n)
    mine = core == side
    lefts = []

    def column(d, c):
        to = lax.rem(chip + d, n)
        return det_send(
            x.at[to, cuts[c]], x_out.at[slot, cuts[c]], xs0.at[d, c], xs1.at[slot, c], to * 2 + side
        )

    def over(source):
        to = back_chip * 2 + side
        return det_send(x.at[lax.rem(chip + far, n), cuts[0]], by_x.at[source], vx0.at[0], vx1.at[source], to)

    def onward(source):
        at = lax.rem(from_chip * 2 + source, n)
        return det_send(
            by_x.at[source], x_out.at[at, cuts[0]], wx0.at[source], xs1.at[at, 0], final_chip * 2 + from_side
        )

    def timestream(c):
        for i in range(tiles // 4):
            rhs = scan[:, 16 * i : 16 * i + 16, :].reshape(det * 16, LANES)
            lhs = [ke_ref[q * dets + c * chunk : q * dets + (c + 1) * chunk] for q in range(4)]
            got = jnp.dot(jnp.concatenate(lhs, 0), rhs, preferred_element_type=F32)
            for q in range(4):
                k = 4 * i + q
                weight = w_ref[cuts[c], k * LANES : (k + 1) * LANES].astype(F32)
                ts[k, cuts[c]] = got[q * chunk : (q + 1) * chunk] * weight
        for h in range(2):

            def swap(g, carry):
                at = pl.ds(pl.multiple_of(c * chunk + g * 16, 16), 16)
                out = digit_swap([ts[h * det + i, at, :] for i in range(det)])
                for z in range(det):
                    u[z, at, h * LANES : (h + 1) * LANES] = out[z].astype(BF16)
                return carry

            lax.fori_loop(0, chunk // 16, swap, 0)

    def transform(c):
        def fast(z, carry):
            a = jnp.dot(u[z, cuts[c]], fwd_ref[...], preferred_element_type=F32)
            re, im = a[:, :LANES], a[:, LANES:]
            cs, sn = tw_ref[z, 0:1, :], tw_ref[z, 1:2, :]
            spun[z, cuts[c], :LANES] = re * cs + im * sn
            spun[z, cuts[c], LANES:] = im * cs - re * sn
            return carry

        lax.fori_loop(0, det, fast, 0)

        def last(g, carry):
            at = pl.ds(pl.multiple_of(c * chunk + g * 16, 16), 16)
            re = [spun[z, at, :LANES] for z in range(det)]
            im = [spun[z, at, LANES:] for z in range(det)]
            re, im = small_dft(re, im, -1)
            for b in range(det):
                to, lo = place(bands, b)
                x[to, at, lo : lo + LANES] = re[b].astype(BF16)
                x[to, at, lo + LANES : lo + FAST] = im[b].astype(BF16)
            return carry

        lax.fori_loop(0, chunk // 16, last, 0)

    def send_columns(c):
        for d in far_first(n)[:-1]:
            if relayed and c == 0 and d == far:
                for source in range(2):

                    @pl.when(core == source)
                    def _():
                        over(source).start()
            else:
                column(d, c).start()
                lefts.append(column(d, c))

        @pl.when(mine)
        def _():
            x_out[slot, cuts[c]] = x[chip, cuts[c]]

        @pl.when(jnp.logical_not(mine))
        def _():
            column(0, c).start()

    advance()
    timestream(0)
    transform(0)
    send_columns(0)
    timestream(1)
    advance()

    sums[...] = jnp.zeros_like(sums)

    def ends(z, carry):
        sums[pl.ds(pl.multiple_of(z * 8, 8), 8), :dets] = lax.dot_general(
            ends_ref[...], u[z], (((1,), (1,)), ((), ())), preferred_element_type=F32
        )
        return carry

    transform(1)
    send_columns(1)
    if relayed:

        @pl.when(core == from_side)
        def _():
            for source in range(2):
                det_send(by_x.at[source], by_x.at[source], vx0.at[0], vx1.at[source], me).wait_recv()
                onward(source).start()

    lax.fori_loop(0, det, ends, 0)
    e[...] = split_dot(edge_ref[...], sums[...], ROWS_COLS)
    own = pl.ds(pl.multiple_of(me * 8, 8), 8)
    edges = []
    for d in range(1, det):
        to = peers[d - 1]
        edges.append(
            det_send(e.at[pl.ds(pl.multiple_of(to * 8, 8), 8)], es.at[own], es0.at[d], es1.at[d], to)
        )
        edges[-1].start()
    es[own, :] = e[own, :]
    advance()
    for copy in edges:
        copy.wait()
    for i in range(4):
        payload[16 * i : 16 * i + det] = es[pl.ds(i, det, stride=8), :].astype(BF16)
    give_start, give_wait = obs_copies(obs, payload, gathered, gs0, gs1, True)
    for step in steps:
        turn(step)
    give_start()
    for i in range(n):

        @pl.when(core * n + i != me)
        def _():
            for c in range(2):
                det_send(
                    x_out.at[i, cuts[c]], x_out.at[i, cuts[c]], xs0.at[0, c], xs1.at[i, c], me
                ).wait_recv()

    hn = n // 2
    swaps, sends = [], []

    def product(to_chips, c):
        blocks = [to_chip * 4 + 2 * i + c for to_chip in to_chips for i in range(2)]
        rows = jnp.concatenate([m_out[at // down, lax.rem(at, down)] for at in blocks], 0)
        return jnp.dot(rows, x_out[...].reshape(n * dets, 2 * FAST), preferred_element_type=F32)

    def finish(c, s, total):
        to_chip = core * hn + lax.rem(chip + s, hn)
        swaps[c * hn + s].wait_recv()
        total = total + taken[c, s].astype(F32)
        for i in range(2):
            to = to_chip * 2 + i
            staged[c, s, i] = total[i * chunk : (i + 1) * chunk].astype(BF16)
            copy = det_send(
                staged.at[c, s, i], y_ref.at[chip, cuts[c]], ys0.at[c, s, i], ys1.at[chip, c], to
            )
            direct = to != me
            if relayed and c == 0 and s == 0:
                direct = direct & mine
                around = det_send(
                    staged.at[c, s, i], by_y, vy0.at[i], vy1.at[0], back_chip * 2 + i
                )

                @pl.when(jnp.logical_not(mine))
                def _():
                    around.start()

                sends.append((jnp.logical_not(mine), around))

            @pl.when(direct)
            def _():
                copy.start()

            @pl.when(to == me)
            def _():
                y_ref[chip, cuts[c]] = staged[c, s, i]

            sends.append((direct, copy))

    before = None
    for c in range(2):
        for s in range(hn):
            near = lax.rem(chip + s, hn)
            got = product(((1 - core) * hn + near, core * hn + near), c)
            given[c, s] = got[:dets].astype(BF16)
            swaps.append(
                det_send(given.at[c, s], taken.at[c, s], ps0.at[c, s], ps1.at[c, s], partner)
            )
            swaps[-1].start()
            total = got[dets:]
            if before is not None:
                finish(*before)
            before = (c, s, total)
    finish(*before)
    y_onward = det_send(
        by_y, y_ref.at[from_chip, cuts[0]], wy0.at[0], ys1.at[from_chip, 0], final_chip * 2 + core
    )
    if relayed:
        det_send(by_y, by_y, vy0.at[0], vy1.at[0], me).wait_recv()
        y_onward.start()

    give_wait()
    wide[...] = gathered[...].reshape(obs * 64, LANES).astype(F32)
    prod = jnp.zeros((obs * 4, width), F32)
    for j in range(det):
        lhs = wide[pl.ds(j, obs * 4, stride=16), :dets].astype(BF16)
        rhs = nrows[:, j * dets : (j + 1) * dets]
        prod = prod + lax.dot_general(lhs, rhs, (((1,), (1,)), ((), ())), preferred_element_type=F32)
    zs[...] = jnp.zeros_like(zs)
    for p in range(obs):
        zs[p, 0:4, :width] = prod[4 * p : 4 * p + 4]
    z_start, z_wait = obs_copies(obs, zs, zz, zs0, zs1)
    z_start()
    z_wait()
    per = obs // det
    finals = []
    for d in range(1, det):
        to = peers[d - 1]
        finals.append(det_send(zz.at[pl.ds(to * per, per)], eb_ref.at[me], fs0.at[d], fs1.at[d], to))
        finals[-1].start()
    eb_ref[me] = zz[pl.ds(me * per, per)]

    for copy in finals:
        copy.wait()
    for q in range(2):
        rows = eb_ref[:, q].reshape(8 * slow, LANES)
        esums[q] = split_dot(edge_ref[...], rows, COLS_COLS).astype(BF16).astype(F32)

    def inverse(c):
        for i in range(n):

            @pl.when(i * 2 + side != me)
            def _():
                det_send(
                    y_ref.at[i, cuts[c]], y_ref.at[i, cuts[c]], ys0.at[0, 0, 0], ys1.at[i, c], me
                ).wait_recv()

        def first(g, carry):
            at = pl.ds(pl.multiple_of(c * chunk + g * 16, 16), 16)
            re, im = [], []
            for b in range(slow):
                to, lo = place(bands, b)
                re.append(y_ref[to, at, lo : lo + LANES].astype(F32))
                im.append(y_ref[to, at, lo + LANES : lo + FAST].astype(F32))
            re, im = small_dft(re, im, 1)
            for z in range(slow):
                cs, sn = tw_ref[z, 0:1, :], tw_ref[z, 1:2, :]
                turned[z, at, :LANES] = (re[z] * cs - im[z] * sn).astype(BF16)
                turned[z, at, LANES:] = (im[z] * cs + re[z] * sn).astype(BF16)
            return carry

        lax.fori_loop(0, chunk // 16, first, 0)

        def fast(z, carry):
            at = pl.ds(pl.multiple_of(z * 8, 8), 8)
            o = jnp.dot(turned[z, cuts[c]], inv_ref[...], preferred_element_type=F32)
            o = o + lax.dot_general(
                esums[c, at, :].astype(BF16), ends_ref[...], COLS_COLS, preferred_element_type=F32
            )[:chunk]
            ts[z, cuts[c]] = o[:, :LANES]
            ts[slow + z, cuts[c]] = o[:, LANES:]
            return carry

        lax.fori_loop(0, slow, fast, 0)
        for h in range(2):

            def swap(g, carry):
                at = pl.ds(pl.multiple_of(c * chunk + g * 16, 16), 16)
                out = digit_swap([ts[h * slow + z, at, :] for z in range(slow)])
                for i in range(slow):
                    ts[h * slow + i, at, :] = out[i]
                return carry

            lax.fori_loop(0, chunk // 16, swap, 0)

    inverse(0)
    inverse(1)
    for i in range(tiles // 4):
        filtered = [
            (ts[k] * w_ref[:, k * LANES : (k + 1) * LANES].astype(F32)).astype(BF16)
            for k in range(4 * i, 4 * i + 4)
        ]
        rows = lax.dot_general(
            ke_ref[...], jnp.concatenate(filtered, 0), COLS_COLS, preferred_element_type=F32
        )
        g_ref[:, :, 16 * i : 16 * i + 16, :] = rows.reshape(n, 2, 16, LANES).astype(BF16)

    swap_pairs = det_send(g_ref.at[:, 1 - core], pre, g0.at[0], g1.at[0], partner)
    swap_pairs.start()
    swap_pairs.wait()
    for c in range(n):
        pairs[c] = (g_ref[c, core].astype(F32) + pre[c].astype(F32)).astype(BF16)
    copies = []
    for d in far_first(n)[:-1]:
        to = lax.rem(chip + d, n)
        copies.append(det_send(pairs.at[to], parts.at[chip], q0.at[d], q1.at[d], to * 2 + core))
        copies[-1].start()
    parts[chip] = pairs[chip]
    for copy in copies:
        copy.wait()
    total = parts[0].astype(F32)
    for c in range(1, n):
        total = total + parts[c].astype(F32)
    total_ref[...] = total
    for k in range(0, tiles, 2):
        rows = total_ref[4 * k : 4 * k + 8]
        high = rows.astype(BF16)
        low = (rows - high.astype(F32)).astype(BF16)
        terms[4 * k : 4 * k + 8] = pair_products(high, along_ref, k, True) + pair_products(
            low, along_ref, k, True
        )
    leave[...] = split_dot(pick_ref[...], terms[...], COLS_COLS).reshape(obs, CAP * MP, LANES)
    start, wait = obs_copies(obs, leave, recv2, s0, s1)
    start()
    wait()
    flat = recv2[...].reshape(obs * CAP * MP, LANES)
    full[me] = split_dot(own_ref[...], flat, COLS_COLS).astype(BF16)
    det_gather(det, full, sems[4:])
    for i in range(held // 4):
        rhs = full[:, 16 * i : 16 * i + 16, :].reshape(det * 16, LANES)
        got = jnp.dot(sel_ref[...], rhs, preferred_element_type=F32)
        sky_ref[4 * i : 4 * i + 4] = got.reshape(4, rows_all, LANES)
    for copy in swaps:
        copy.wait_send()
    for started, copy in sends:

        @pl.when(started)
        def _():
            copy.wait_send()

    for copy in lefts:
        copy.wait_send()

    @pl.when(jnp.logical_not(mine))
    def _():
        for c in range(2):
            column(0, c).wait_send()

    if relayed:
        over(0).wait_send()
        y_onward.wait_send()

        @pl.when(core == from_side)
        def _():
            for source in range(2):
                onward(source).wait_send()

    for d in range(1, across):
        sideways(d).wait_send()
    for step in range(1, down // 2 + 1):
        for way in (1, -1):
            ring(way, step).wait_send()


def call(kernel, out, scratch, name, collective=None):
    if collective is None:
        params = pltpu.CompilerParams(vmem_limit_bytes=56 * 2**20)
    else:
        params = pltpu.CompilerParams(
            vmem_limit_bytes=56 * 2**20, collective_id=collective, has_side_effects=True
        )

    def run(*args):
        return pl.pallas_call(
            kernel,
            out_shape=out,
            in_specs=[VMEM] * len(args),
            out_specs=VMEM if not isinstance(out, tuple) else (VMEM,) * len(out),
            scratch_shapes=scratch,
            compiler_params=params,
            name=name,
        )(*args)

    return run


def dma(n):
    return [pltpu.SemaphoreType.DMA((n,))] * 2


def local(sky, tile_list, along, detector_kernel, sample_weight, noise_inverse):
    obs, det = lax.axis_size("obs"), lax.axis_size("det")
    held, tiles = sky.shape[0], tile_list.shape[1]
    dets, all_dets = detector_kernel.shape[0], noise_inverse.shape[2]
    rows_all = sky.shape[1] * sky.shape[2]
    mine = rows_all // det
    fwd, inv, tw, edge, ends = tables(det)

    expand = np.zeros((rows_all, 4, det, 4, MP), np.float32)
    for q in range(4):
        for j in range(det):
            for m in range(mine):
                expand[j * mine + m, q, j, q, m] = 1
    expand = jnp.asarray(expand.reshape(rows_all, -1), BF16)
    sel = np.zeros((4, det, mine, det, 4, MP), np.float32)
    for q in range(4):
        for j in range(det):
            for m in range(mine):
                sel[q, j, m, j, q, m] = 1
    sel = jnp.asarray(sel.reshape(4 * rows_all, det * 16), BF16)

    block = along[0]
    n, half, per = det // 2, det // 4, obs // det
    down = 8 if obs == 32 else obs // 2
    grid = (obs // down, down)
    mine, part = noise_inverse.shape[1], all_dets // 2
    member = jax.ShapeDtypeStruct((n, dets, 2 * FAST), BF16)
    slots = jax.ShapeDtypeStruct((obs, CAP * MP, LANES), F32)
    slot_buffer = pltpu.VMEM(slots.shape, F32)
    row_buffer = pltpu.VMEM((tiles * MP, LANES), F32)
    pieces = pltpu.VMEM((n, tiles * MP, LANES), BF16)
    edge_rows = pltpu.VMEM((8 * det, LANES), F32)
    mixed = pltpu.VMEM((2, half, dets, 2 * FAST), BF16)
    normal = call(
        functools.partial(normal_kernel, obs, det, grid),
        jax.ShapeDtypeStruct((held, rows_all, LANES), F32),
        [
            slot_buffer,
            pltpu.VMEM((obs * CAP * MP, held * MP), BF16),
            pltpu.VMEM((tiles * MP, obs * CAP * MP), BF16),
            pltpu.VMEM((held * MP, held * rows_all), BF16),
            pltpu.VMEM((4 * dets, det * 16), BF16),
            pltpu.VMEM(member.shape, BF16),
            slot_buffer,
            pltpu.VMEM((*grid, mine, part), BF16),
            slot_buffer,
            pltpu.VMEM((tiles * MP, LANES), BF16),
            pltpu.VMEM((det, tiles * MP, LANES), BF16),
            pltpu.VMEM((mine, all_dets), BF16),
            pltpu.VMEM((mine, part), BF16),
            pltpu.VMEM((tiles, dets, LANES), F32),
            pltpu.VMEM((det, dets, FAST), BF16),
            pltpu.VMEM((det, dets, FAST), F32),
            edge_rows,
            edge_rows,
            edge_rows,
            pltpu.VMEM((64, LANES), BF16),
            pltpu.VMEM((obs, 64, LANES), BF16),
            pltpu.VMEM((obs * 64, LANES), F32),
            slot_buffer,
            pltpu.VMEM(member.shape, BF16),
            mixed,
            mixed,
            pltpu.VMEM((2, half, 2, dets // 2, 2 * FAST), BF16),
            pltpu.VMEM(member.shape, BF16),
            pltpu.VMEM((det, per, CAP * MP, LANES), F32),
            pltpu.VMEM((det, dets, FAST), BF16),
            pltpu.VMEM((2, 8 * det, LANES), F32),
            pltpu.VMEM((n, 2, tiles * MP, LANES), BF16),
            pieces,
            pieces,
            pieces,
            row_buffer,
            row_buffer,
            slot_buffer,
            slot_buffer,
            pltpu.VMEM((det, held * MP, LANES), BF16),
            pltpu.VMEM((2, dets // 2, 2 * FAST), BF16),
            pltpu.VMEM((dets // 2, 2 * FAST), BF16),
            *dma(obs),
            *dma(2),
            *dma(grid[0]),
            *[pltpu.SemaphoreType.DMA((2, down // 2))] * 2,
            *[pltpu.SemaphoreType.DMA((n, 2))] * 2,
            *dma(det),
            *dma(obs),
            *dma(obs),
            *[pltpu.SemaphoreType.DMA((2, half))] * 2,
            pltpu.SemaphoreType.DMA((2, half, 2)),
            pltpu.SemaphoreType.DMA((n, 2)),
            *dma(2),
            *dma(2),
            *dma(1),
            *dma(det),
            *dma(1),
            *dma(n),
            *dma(obs),
            *dma(n),
            *dma(n),
            *dma(n),
            *dma(n),
        ],
        "normal",
        0,
    )(
        sky.reshape(held * rows_all, LANES), tile_list, block, noise_inverse[0], detector_kernel.T, sample_weight,
        expand, fwd, inv, tw, edge, ends, sel,
    )
    return normal.reshape(sky.shape)


def solution(mesh):
    in_specs = (
        P("obs", None, None, None),
        P(),
        P("obs", None, None, None),
        P("det", None),
        P("det", "obs"),
        P("det", "obs", None),
    )
    out_specs = P("obs", None, None, None)
    return jax.shard_map(local, mesh=mesh, in_specs=in_specs, out_specs=out_specs, check_vma=False)
```
